32 devices in a mesh: groups: 2 (over y), blocks: 16 (over z, x, core).
Axes of the slice: x: 2, y: 2, z: 4, core: 2. Of those that a mesh axis runs over, the one named last changes fastest.
Arguments:
- snapshot: bfloat16 [2, 128, 32, 512], P('groups', 'blocks'), parts along dimension 0, may hold values from -6 to 6
- cotangent: bfloat16 [2, 128, 32, 512], P('groups', 'blocks'), parts along dimension 0, may hold values from -6 to 6
- first_weight: bfloat16 [32, 864], replicated, may hold values from -0.21875 to 0.21875
- second_weight: bfloat16 [32, 864], replicated, may hold values from -0.21875 to 0.21875
- face_codes: int32 [32, 2], P(('groups', 'blocks')), parts along dimension 0, may hold values from 0 to 3, as said below
Outputs:
- input_grad: float32 [2, 128, 32, 512], P('groups', 'blocks'), parts along dimension 0
- first_update: float32 [64, 864], P('groups'), parts along dimension 0
- second_update: float32 [64, 864], P('groups'), parts along dimension 0
The draws below stay inside these ranges and needn't reach their ends.
There are 2 independent parts, one for each index of `groups`. The reference program is written for one: setup_inputs(seed, part) draws one part's arguments, and reference() takes and returns one part's arrays. A program takes and returns all parts, laid end to end along the dimension named above; an argument that names none is the same for every part. Nothing has to cross between parts.
Inputs may be any that keep to these rules, and one draw needn't show every extreme that they name: face_codes[b, 1] equals face_codes[(b + 1) mod 16, 0]: both blocks of an interface carry the same code.
All inputs are finite; a program needn't handle non-finite values.
Results may differ from the reference program's by a relative error of at most 0.003.
Values may be sent and summed in bfloat16 or wider, within the bound.
No kernel may reach another device: no remote copies, remote signals or barrier semaphores. Data moves between devices by JAX's collectives and lax.ppermute only.
A program may use at most 64 MiB of HBM per device.

```python
import jax
import jax.numpy as jnp
from jax import lax

CH = 32
TAPS = 27
R_CELLS = 32
Z_CELLS = 16
A_CELLS = 8
BATCH = 1
A_TOTAL = 128
RZ = 512
N_BLOCKS = 16


def draw_face_codes(key, part):
    codes = jax.random.randint(key, (N_BLOCKS,), 0, 4, dtype=jnp.int32)
    return jnp.stack([jnp.roll(codes, 1), codes], axis=1)


def block_levels(stream_key, shape, cuts, least, top_value):
    def one(position, blocks):
        steps = jax.random.uniform(jax.random.fold_in(jax.random.fold_in(stream_key, 6), position), (blocks,), jnp.float32, least / len(cuts), top_value / len(cuts))
        return jnp.repeat(jnp.exp(steps), shape[position] // blocks).reshape((-1,) + (1,) * (len(shape) - position - 1))

    level = one(*cuts[0])
    for cut in cuts[1:]:
        level = level * one(*cut)
    return level


def noise(stream_key, shape, scale, reach, shards=(), kind=jnp.bfloat16):
    gain = block_levels(stream_key, shape, shards, -0.22, 0.18) if shards else 1.0
    values = jax.random.normal(stream_key, shape, jnp.float32) * scale * gain
    return jnp.minimum(jnp.maximum(values, -reach), reach).astype(kind)


def setup_inputs(seed: int = 0, part: int = 0) -> dict:
    streams_of = jax.random.split(jax.random.key(seed), 6)
    part_keys = jax.random.split(jax.random.fold_in(streams_of[5], part), 6)
    return {
        "snapshot": noise(part_keys[0], (BATCH, A_TOTAL, CH, RZ), 1.0, 6.0, ((1, 16),)),
        "cotangent": noise(part_keys[1], (BATCH, A_TOTAL, CH, RZ), 1.0, 6.0, ((1, 16),)),
        "first_weight": noise(streams_of[2], (CH, TAPS * CH), (TAPS * CH) ** -0.5, 0.21875),
        "second_weight": noise(streams_of[3], (CH, TAPS * CH), (TAPS * CH) ** -0.5, 0.21875),
        "face_codes": draw_face_codes(jax.random.fold_in(jax.random.fold_in(streams_of[5], part), 71), part),
    }


def flip_planes(planes, codes):
    first_bit = (codes % 2 == 1)[None, :, None, None, None]
    planes = jnp.where(first_bit, planes[:, :, :, ::-1, :], planes)
    second_bit = (codes // 2 == 1)[None, :, None, None, None]
    return jnp.where(second_bit, planes[:, :, :, :, ::-1], planes)

def pad_domain(field, face_codes):
    lower = flip_planes(jnp.roll(field[:, :, -1], 1, axis=1), face_codes[:, 0])
    upper = flip_planes(jnp.roll(field[:, :, 0], -1, axis=1), face_codes[:, 1])
    full = jnp.concatenate([lower[:, :, None], field, upper[:, :, None]], axis=2)
    return jnp.pad(full, ((0, 0), (0, 0), (0, 0), (0, 0), (1, 1), (1, 1)))

def convolve(field, weight, face_codes):
    padded = pad_domain(field, face_codes)
    count = field.shape[2]
    channels = field.shape[3]
    radial = field.shape[4]
    vertical = field.shape[5]
    total = jnp.zeros(field.shape[:3] + (weight.shape[0], radial, vertical), jnp.float32)
    for step_a in range(3):
        for step_r in range(3):
            for step_z in range(3):
                tap_index = 9 * step_a + 3 * step_r + step_z
                piece = padded[:, :, step_a:step_a + count, :, step_r:step_r + radial, step_z:step_z + vertical]
                kernel = weight[:, tap_index * channels:(tap_index + 1) * channels]
                total = total + jnp.einsum('oc,bnacrz->bnaorz', kernel, piece)
    return total

def weight_gradient(field, cotan, face_codes):
    padded = pad_domain(field, face_codes)
    count = field.shape[2]
    radial = field.shape[4]
    vertical = field.shape[5]
    pieces = []
    for step_a in range(3):
        for step_r in range(3):
            for step_z in range(3):
                piece = padded[:, :, step_a:step_a + count, :, step_r:step_r + radial, step_z:step_z + vertical]
                pieces.append(jnp.einsum('bnaorz,bnacrz->oc', cotan, piece))
    return jnp.concatenate(pieces, axis=1)

def normalize(grad):
    return grad / jnp.sqrt(jnp.mean(grad * grad) + 1e-06)

def reference(snapshot, cotangent, first_weight, second_weight, face_codes):
    batch_count = snapshot.shape[0]
    shape_six = (batch_count, N_BLOCKS, A_CELLS, CH, R_CELLS, Z_CELLS)
    field = snapshot.astype(jnp.float32).reshape(shape_six)
    cotan = cotangent.astype(jnp.float32).reshape(shape_six)
    weight_one = first_weight.astype(jnp.float32)
    weight_two = second_weight.astype(jnp.float32)
    pre = convolve(field, weight_one, face_codes)
    hidden = lax.optimization_barrier(jax.nn.silu(pre).astype(jnp.bfloat16)).astype(jnp.float32)
    second_grad = weight_gradient(hidden, cotan, face_codes)
    _, back_two = jax.vjp(lambda value: convolve(value, weight_two, face_codes), hidden)
    hidden_grad, = back_two(cotan)
    sigmoid_part = jax.nn.sigmoid(pre)
    pre_grad = hidden_grad * sigmoid_part * (1.0 + pre * (1.0 - sigmoid_part))
    pre_grad = lax.optimization_barrier(pre_grad.astype(jnp.bfloat16)).astype(jnp.float32)
    first_grad = weight_gradient(field, pre_grad, face_codes)
    _, back_one = jax.vjp(lambda value: convolve(value, weight_one, face_codes), field)
    field_grad, = back_one(pre_grad)
    input_grad = (cotan + field_grad).reshape(batch_count, N_BLOCKS * A_CELLS, CH, R_CELLS * Z_CELLS)
    return (input_grad, normalize(first_grad), normalize(second_grad))
```

```python
import jax
import jax.numpy as jnp
from jax import lax
from jax.experimental import pallas as pl
from jax.experimental.pallas import tpu as pltpu
from jax.sharding import PartitionSpec as P

R_CELLS = 32
AXIS = "blocks"
F32 = jnp.float32
BF16 = jnp.bfloat16
VMEM_LIMIT = 40 * 1024 * 1024


def tap_masks(cells, vertical):
    lane = lax.broadcasted_iota(jnp.int32, (1, cells), 1)
    z = lane % vertical
    r = lane // vertical
    radial = cells // vertical
    masks = []
    for step_r in range(3):
        for step_z in range(3):
            ok = None
            if step_r == 0:
                ok = r >= 1
            if step_r == 2:
                ok = r < radial - 1
            if step_z == 0:
                ok = (z >= 1) if ok is None else ok & (z >= 1)
            if step_z == 2:
                ok = (z < vertical - 1) if ok is None else ok & (z < vertical - 1)
            masks.append(ok)
    return masks


def im2col(plane, store, masks, vertical):
    cells = plane.shape[1]
    wide = plane.astype(F32)
    for tap in range(9):
        offset = (tap // 3 - 1) * vertical + (tap % 3 - 1)
        if offset == 0:
            store(tap, plane)
            continue
        moved = pltpu.roll(wide, (-offset) % cells, 1)
        moved = jnp.where(masks[tap], moved, 0.0)
        store(tap, moved.astype(BF16))


def flipped_tap(tap, code):
    a, r, z = tap // 9, (tap // 3) % 3, tap % 3
    if code % 2 == 1:
        r = 2 - r
    if code // 2 == 1:
        z = 2 - z
    return 9 * a + 3 * r + z


(FW1_LO, FW1_HI, A2, A2_0, A2_7, A2_M, A2_P, A1, A1_0, A1_7) = range(10)


def prepare_kernel(codes_ref, w1_ref, w2_ref, out_ref):
    channels = w1_ref.shape[0]
    k_lo = codes_ref[0, 0]
    k_hi = codes_ref[0, 1]

    def block(tap):
        return slice(tap * channels, (tap + 1) * channels)

    for weight_ref, row in ((w1_ref, A1), (w2_ref, A2)):
        turned = weight_ref[...].astype(F32).T
        for tap in range(27):
            out_ref[row, :, block(tap)] = turned[block(26 - tap), :].astype(BF16)

    out_ref[A2_0, :, :] = out_ref[A2]
    out_ref[A2_7, :, :] = out_ref[A2]
    out_ref[A2_M, :, :] = out_ref[A2]
    out_ref[A2_P, :, :] = out_ref[A2]
    out_ref[A1_0, :, :] = out_ref[A1]
    out_ref[A1_7, :, :] = out_ref[A1]

    for code in range(4):

        @pl.when(k_lo == code)
        def _(code=code):
            for tap in range(27):
                source = flipped_tap(tap, code)
                out_ref[FW1_LO, :, block(tap)] = w1_ref[:, block(source)]
                if tap < 18:
                    out_ref[A2_M, :, block(tap)] = out_ref[A2, :, block(source)]
                if tap < 9:
                    out_ref[A2_0, :, block(tap)] = out_ref[A2, :, block(source)]
                    out_ref[A1_0, :, block(tap)] = out_ref[A1, :, block(source)]

        @pl.when(k_hi == code)
        def _(code=code):
            for tap in range(27):
                source = flipped_tap(tap, code)
                out_ref[FW1_HI, :, block(tap)] = w1_ref[:, block(source)]
                if tap >= 9:
                    out_ref[A2_P, :, block(tap)] = out_ref[A2, :, block(source)]
                if tap >= 18:
                    out_ref[A2_7, :, block(tap)] = out_ref[A2, :, block(source)]
                    out_ref[A1_7, :, block(tap)] = out_ref[A1, :, block(source)]


def dot(a, b):
    return jnp.dot(a, b, preferred_element_type=F32)


def dot_nt(a, b):
    return lax.dot_general(a, b, (((1,), (1,)), ((), ())), preferred_element_type=F32)


def flip_matrix(code, cells, vertical):
    row = lax.broadcasted_iota(jnp.int32, (cells, cells), 0)
    col = lax.broadcasted_iota(jnp.int32, (cells, cells), 1)
    bits = jnp.where(code % 2 == 1, cells - vertical, 0) + jnp.where(code // 2 == 1, vertical - 1, 0)
    return jnp.where(row == (col ^ bits), 1.0, 0.0).astype(BF16)


def make_main_kernel(count, channels, cells, vertical):
    span = 9 * channels

    def kernel(codes_ref, x_ref, g_ref, pair_ref, cross_ref, w1_ref, wp_ref,
               keep_ref, send_ref, pg_ref, xs_ref, cs_ref, h_ref, pr_ref):
        odd = lax.axis_index(AXIS) % 2
        masks = tap_masks(cells, vertical)

        def fill(ref, position, plane):
            def store(tap, value):
                start = position * span + tap * channels
                ref[start:start + channels, :] = value

            im2col(plane, store, masks, vertical)

        is_odd = odd == 1
        for side in range(2):
            lower = side == 0
            a_val = pair_ref[...].reshape(4 * channels, cells)
            b_val = cross_ref[...].reshape(4 * channels, cells)
            planes = jnp.where(is_odd, a_val, b_val) if lower else jnp.where(is_odd, b_val, a_val)
            turn = flip_matrix(codes_ref[0, side], cells, vertical)
            planes = dot(planes, turn).astype(BF16)
            base = 0 if lower else count + 2
            for index in range(2):
                fill(xs_ref, base + index, planes[index * channels:(index + 1) * channels])
                fill(cs_ref, base + index, planes[(index + 2) * channels:(index + 3) * channels])
        for a in range(count):
            fill(xs_ref, a + 2, x_ref[a])
            fill(cs_ref, a + 2, g_ref[a])

        zero = jnp.zeros((channels, cells), BF16)
        for a in range(-1, count + 1):
            low = (a + 1) * span
            window = slice(low, low + 3 * span)
            w_fwd = wp_ref[FW1_LO] if a == -1 else wp_ref[FW1_HI] if a == count else w1_ref[...]
            row = {-1: A2_M, 0: A2_0, count - 1: A2_7, count: A2_P}.get(a, A2)
            pre = dot(w_fwd, xs_ref[window, :])
            grad = dot(wp_ref[row], cs_ref[window, :])
            sig = jax.nn.sigmoid(pre)
            hidden = (pre * sig).astype(BF16)
            h_ref[(a + 1) * channels:(a + 2) * channels, :] = hidden
            pg = (grad * sig * (1.0 + pre * (1.0 - sig))).astype(BF16)
            pg_ref[a + 1, :, :] = pg
            place = count + 1 - a
            pr_ref[place * channels:(place + 1) * channels, :] = zero if a in (-1, count) else pg
        pr_ref[0:channels, :] = zero
        pr_ref[(count + 3) * channels:(count + 4) * channels, :] = zero

        grad_two = None
        for a in range(count):
            left = h_ref[a * channels:(a + 3) * channels, :]
            right = cs_ref[(a + 2) * span:(a + 3) * span, :]
            term = dot_nt(left, right)
            grad_two = term if grad_two is None else grad_two + term
        grad_one = None
        for a in range(-1, count + 1):
            start = (count - a) * channels
            left = pr_ref[start:start + 3 * channels, :]
            right = xs_ref[(a + 2) * span:(a + 3) * span, :]
            term = dot_nt(left, right)
            grad_one = term if grad_one is None else grad_one + term

        def put(ref, one):
            if one:
                for step in range(3):
                    ref[:, step * span:(step + 1) * span] = grad_one[step * channels:(step + 1) * channels]
            else:
                turned = grad_two.T
                for step in range(3):
                    for tap in range(9):
                        at = (9 * step + tap) * channels
                        ref[:, at:at + channels] = turned[
                            (8 - tap) * channels:(9 - tap) * channels, step * channels:(step + 1) * channels]

        @pl.when(odd == 0)
        def _():
            put(keep_ref, True)
            put(send_ref, False)

        @pl.when(odd == 1)
        def _():
            put(keep_ref, False)
            put(send_ref, True)

    return kernel


def make_input_kernel(count, channels, cells, vertical):
    span = 9 * channels

    def kernel(pg_ref, g_ref, wp_ref, out_ref, ps_ref):
        masks = tap_masks(cells, vertical)
        for a in range(count + 2):
            def store(tap, value, a=a):
                start = a * span + tap * channels
                ps_ref[start:start + channels, :] = value

            im2col(pg_ref[a], store, masks, vertical)
        for a in range(count):
            row = A1_0 if a == 0 else A1_7 if a == count - 1 else A1
            out_ref[a, :, :] = g_ref[a].astype(F32) + dot(wp_ref[row], ps_ref[a * span:(a + 3) * span, :])

    return kernel


def normalize_kernel(v_ref, o_ref):
    v = v_ref[...]
    o_ref[...] = v / jnp.sqrt(jnp.mean(v * v) + 1e-06)


VM = pl.BlockSpec(memory_space=pltpu.VMEM)
SM = pl.BlockSpec(memory_space=pltpu.SMEM)
PARAMS = pltpu.CompilerParams(vmem_limit_bytes=VMEM_LIMIT)


def body(snapshot, cotangent, first_weight, second_weight, face_codes):
    count, channels, cells = snapshot.shape[1:]
    vertical = cells // R_CELLS
    size = lax.axis_size(AXIS)
    x, g = snapshot[0], cotangent[0]
    odd = lax.axis_index(AXIS) % 2 == 1
    low = jnp.concatenate([x[:2], g[:2]], axis=0)
    high = jnp.concatenate([x[count - 2:], g[count - 2:]], axis=0)

    def cross_of(b):
        return (b + 1) % size if b % 2 == 1 else (b - 1) % size

    cross = lax.ppermute(jnp.where(odd, high, low), AXIS, [(b, cross_of(b)) for b in range(size)])
    pair = lax.ppermute(jnp.where(odd, low, high), AXIS, [(b, b ^ 1) for b in range(size)])

    weights = pl.pallas_call(
        prepare_kernel,
        out_shape=jax.ShapeDtypeStruct((10, channels, 27 * channels), BF16),
        in_specs=[SM, VM, VM], out_specs=VM, compiler_params=PARAMS, name="prepare",
    )(face_codes, first_weight, second_weight)

    grads = jax.ShapeDtypeStruct((channels, 27 * channels), F32)
    keep, send, pre_grad = pl.pallas_call(
        make_main_kernel(count, channels, cells, vertical),
        out_shape=(grads, grads, jax.ShapeDtypeStruct((count + 2, channels, cells), BF16)),
        in_specs=[SM, VM, VM, VM, VM, VM, VM], out_specs=(VM, VM, VM),
        scratch_shapes=[
            pltpu.VMEM(((count + 4) * 9 * channels, cells), BF16),
            pltpu.VMEM(((count + 4) * 9 * channels, cells), BF16),
            pltpu.VMEM(((count + 2) * channels, cells), BF16),
            pltpu.VMEM(((count + 4) * channels, cells), BF16),
        ],
        compiler_params=PARAMS, name="main",
    )(face_codes, x, g, pair, cross, first_weight, weights)

    def swap(value, bit):
        return lax.ppermute(value, AXIS, [(b, b ^ bit) for b in range(size)])

    total = keep + swap(send, 1)
    bit = 2
    while bit < size:
        total = total + swap(total, bit)
        bit *= 2

    input_grad = pl.pallas_call(
        make_input_kernel(count, channels, cells, vertical),
        out_shape=jax.ShapeDtypeStruct((count, channels, cells), F32),
        in_specs=[VM, VM, VM], out_specs=VM,
        scratch_shapes=[pltpu.VMEM(((count + 2) * 9 * channels, cells), BF16)],
        compiler_params=PARAMS, name="input_grad",
    )(pre_grad, g, weights)

    mine = pl.pallas_call(
        normalize_kernel, out_shape=grads, in_specs=[VM], out_specs=VM, compiler_params=PARAMS, name="normalize",
    )(total)
    other = swap(mine, 1)
    return (input_grad[None], jnp.where(odd, other, mine), jnp.where(odd, mine, other))


def solution(mesh):
    return jax.shard_map(
        body,
        mesh=mesh,
        in_specs=(
            P("groups", "blocks", None, None),
            P("groups", "blocks", None, None),
            P(),
            P(),
            P(("groups", "blocks"), None),
        ),
        out_specs=(P("groups", "blocks", None, None), P("groups", None), P("groups", None)),
        check_vma=False,
    )
```

```python
import jax
import jax.numpy as jnp
from jax import lax
from jax.experimental import pallas as pl
from jax.experimental.pallas import tpu as pltpu
from jax.sharding import PartitionSpec as P

R_CELLS = 32
AXIS = "blocks"
F32 = jnp.float32
BF16 = jnp.bfloat16
VMEM_LIMIT = 24 * 1024 * 1024


def tap_masks(cells, vertical):
    lane = lax.broadcasted_iota(jnp.int32, (1, cells), 1)
    z = lane % vertical
    r = lane // vertical
    radial = cells // vertical
    masks = []
    for step_r in range(3):
        for step_z in range(3):
            ok = None
            if step_r == 0:
                ok = r >= 1
            if step_r == 2:
                ok = r < radial - 1
            if step_z == 0:
                ok = (z >= 1) if ok is None else ok & (z >= 1)
            if step_z == 2:
                ok = (z < vertical - 1) if ok is None else ok & (z < vertical - 1)
            masks.append(ok)
    return masks


def im2col(plane, store, masks, vertical):
    cells = plane.shape[1]
    wide = plane.astype(F32)
    for tap in range(9):
        offset = (tap // 3 - 1) * vertical + (tap % 3 - 1)
        if offset == 0:
            store(tap, plane)
            continue
        moved = pltpu.roll(wide, (-offset) % cells, 1)
        moved = jnp.where(masks[tap], moved, 0.0)
        store(tap, moved.astype(BF16))


def dot(a, b):
    return jnp.dot(a, b, preferred_element_type=F32)


def dot_nt(a, b):
    return lax.dot_general(a, b, (((1,), (1,)), ((), ())), preferred_element_type=F32)


def flip_matrix(code, cells, vertical):
    row = lax.broadcasted_iota(jnp.int32, (cells, cells), 0)
    col = lax.broadcasted_iota(jnp.int32, (1, cells), 1)
    bits = jnp.where(code % 2 == 1, cells - vertical, 0) + jnp.where(code // 2 == 1, vertical - 1, 0)
    return jnp.where(row == (col ^ bits), 1.0, 0.0).astype(BF16)


def tap_flip_matrix(code, channels):
    size = 9 * channels
    row = lax.broadcasted_iota(jnp.int32, (size, size), 0)
    col = lax.broadcasted_iota(jnp.int32, (1, size), 1)
    tap = col // channels
    r, z = tap // 3, tap % 3
    r = jnp.where(code % 2 == 1, 2 - r, r)
    z = jnp.where(code // 2 == 1, 2 - z, z)
    return jnp.where(row == (3 * r + z) * channels + col % channels, 1.0, 0.0).astype(BF16)


def activation(pre, grad):
    sig = jax.nn.sigmoid(pre)
    hidden = (pre * sig).astype(BF16)
    return hidden, (grad * sig * (1.0 + pre * (1.0 - sig))).astype(BF16)


def filler(ref, channels, masks, vertical):
    def fill(position, plane):
        def store(tap, value):
            start = (9 * position + tap) * channels
            ref[start:start + channels, :] = value

        im2col(plane, store, masks, vertical)

    return fill


def make_pack_kernel(count, channels, cells):
    def kernel(codes_ref, x_ref, g_ref, w1_ref, w2_ref,
               cross_ref, pair_ref, codes_out, x_out, g_out, w1_out, w2_out, scalars, sems):
        copies = [
            pltpu.make_async_copy(source, target, sems.at[index])
            for index, (source, target) in enumerate(
                ((x_ref, x_out), (g_ref, g_out), (w1_ref, w1_out), (w2_ref, w2_out), (codes_ref, scalars)))
        ]
        for copy in copies:
            copy.start()
        is_odd = lax.axis_index(AXIS) % 2 == 1
        for index, field in enumerate((x_out, g_out)):
            copies[index].wait()
            low, high = field[0:2], field[count - 2:count]
            cross_ref[2 * index:2 * index + 2, :, :] = jnp.where(is_odd, high, low)
            pair_ref[2 * index:2 * index + 2, :, :] = jnp.where(is_odd, low, high)
        for copy in copies[2:]:
            copy.wait()
        for side in range(2):
            codes_out[side, :, :] = jnp.full((8, 128), scalars[0, side], jnp.int32)

    return kernel


def make_interior_kernel(count, channels, cells, vertical):
    span = 9 * channels
    wide = 3 * channels
    last = count - 1

    def kernel(codes_ref, x_ref, g_ref, w1_ref, w2_ref,
               ws_ref, lo_ref, hi_ref, turn_ref, pe_ref, ge_ref, xs_ref, cs_ref, pg_ref, g1_ref, g2_ref,
               h_ref, pr_ref):
        masks = tap_masks(cells, vertical)
        for step in range(3):
            ws_ref[step * channels:(step + 1) * channels, :] = w1_ref[:, step * span:(step + 1) * span]
        for weight_ref, base in ((w2_ref, wide), (w1_ref, 2 * wide)):
            turned = weight_ref[...].astype(F32).T
            for step in range(3):
                for tap in range(9):
                    at = (9 * (2 - step) + 8 - tap) * channels
                    ws_ref[base + step * channels:base + (step + 1) * channels, tap * channels:(tap + 1) * channels] = (
                        turned[at:at + channels, :].astype(BF16))
        lo_ref[...] = dot(ws_ref[...], tap_flip_matrix(codes_ref[0, 0:1, 0:1], channels)).astype(BF16)
        hi_ref[...] = dot(ws_ref[...], tap_flip_matrix(codes_ref[1, 0:1, 0:1], channels)).astype(BF16)
        for side in range(2):
            turn_ref[side, :, :] = flip_matrix(codes_ref[side, 0:1, 0:1], cells, vertical)

        fill_x = filler(xs_ref, channels, masks, vertical)
        fill_g = filler(cs_ref, channels, masks, vertical)
        for a in range(count):
            fill_x(a, x_ref[a])
            fill_g(a, g_ref[a])

        h_ref[...] = jnp.zeros_like(h_ref)
        pr_ref[...] = jnp.zeros_like(pr_ref)
        pre, grad = {}, {}

        def add(table, key, value):
            table[key] = value if key not in table else table[key] + value

        for a in range(count):
            columns = slice(a * span, (a + 1) * span)
            y = dot(ws_ref[0:wide, :], xs_ref[columns, :])
            v = dot(ws_ref[wide:2 * wide, :], cs_ref[columns, :])
            for step in range(3):
                target = a + 1 - step
                rows = slice(step * channels, (step + 1) * channels)
                add(grad, target, v[rows])
                if 0 <= target <= last:
                    add(pre, target, y[rows])
            if a == 0:
                pre[-1] = dot(lo_ref[2 * channels:wide, :], xs_ref[columns, :])
            if a == last:
                pre[count] = dot(hi_ref[0:channels, :], xs_ref[columns, :])
            done = a - 1
            if 1 <= done <= last - 1:
                hidden, pg = activation(pre.pop(done), grad.pop(done))
                h_ref[(done + 1) * channels:(done + 2) * channels, :] = hidden
                pg_ref[done - 1, :, :] = pg
                place = count + 1 - done
                pr_ref[place * channels:(place + 1) * channels, :] = pg
            if a == 1:
                for index, plane in ((0, -1), (1, 0)):
                    pe_ref[index, :, :] = pre.pop(plane)
                    ge_ref[index, :, :] = grad.pop(plane)
        for index, plane in ((2, last), (3, count)):
            pe_ref[index, :, :] = pre.pop(plane)
            ge_ref[index, :, :] = grad.pop(plane)

        grad_one, grad_two = None, None
        for a in range(count):
            term = dot_nt(cs_ref[a * span:(a + 1) * span, :], h_ref[a * channels:(a + 3) * channels, :])
            grad_two = term if grad_two is None else grad_two + term
            start = (count - a) * channels
            term = dot_nt(xs_ref[a * span:(a + 1) * span, :], pr_ref[start:start + wide, :])
            grad_one = term if grad_one is None else grad_one + term
        g2_ref[...] = grad_two
        turned = grad_one.T
        for step in range(3):
            g1_ref[:, step * span:(step + 1) * span] = turned[step * channels:(step + 1) * channels]

    return kernel


def make_edge_kernel(count, channels, cells, vertical):
    span = 9 * channels
    wide = 3 * channels
    last = count - 1

    def kernel(pair_ref, cross_ref, ws_ref, lo_ref, hi_ref, turn_ref, pe_ref, ge_ref, xs_ref, cs_ref, g1_ref, g2_ref,
               keep_ref, send_ref, pg_ref, xh_ref, ch_ref):
        odd = lax.axis_index(AXIS) % 2
        is_odd = odd == 1
        masks = tap_masks(cells, vertical)
        fill_x = filler(xh_ref, channels, masks, vertical)
        fill_c = filler(ch_ref, channels, masks, vertical)
        pair = pair_ref[...].reshape(4 * channels, cells)
        cross = cross_ref[...].reshape(4 * channels, cells)
        for side in range(2):
            planes = jnp.where(is_odd, pair, cross) if side == 0 else jnp.where(is_odd, cross, pair)
            planes = dot(planes, turn_ref[side]).astype(BF16)
            for index in range(2):
                fill_x(2 * side + index, planes[index * channels:(index + 1) * channels])
                fill_c(2 * side + index, planes[(index + 2) * channels:(index + 3) * channels])

        def halo(ref, index):
            return ref[index * span:(index + 1) * span, :]

        def rows(ref, part, first, end):
            return ref[part * wide + first * channels:part * wide + end * channels, :]

        near = dot(jnp.concatenate([rows(ws_ref, 0, 0, 1), rows(lo_ref, 0, 1, 2)], axis=0), halo(xh_ref, 1))
        pre_m = pe_ref[0] + near[channels:] + dot(rows(lo_ref, 0, 0, 1), halo(xh_ref, 0))
        pre_0 = pe_ref[1] + near[:channels]
        near = dot(rows(lo_ref, 1, 0, 2), halo(ch_ref, 1))
        grad_m = ge_ref[0] + near[channels:] + dot(rows(lo_ref, 1, 0, 1), halo(ch_ref, 0))
        grad_0 = ge_ref[1] + near[:channels]
        near = dot(jnp.concatenate([rows(hi_ref, 0, 1, 2), rows(ws_ref, 0, 2, 3)], axis=0), halo(xh_ref, 2))
        pre_p = pe_ref[3] + near[:channels] + dot(rows(hi_ref, 0, 2, 3), halo(xh_ref, 3))
        pre_7 = pe_ref[2] + near[channels:]
        near = dot(rows(hi_ref, 1, 1, 3), halo(ch_ref, 2))
        grad_p = ge_ref[3] + near[:channels] + dot(rows(hi_ref, 1, 2, 3), halo(ch_ref, 3))
        grad_7 = ge_ref[2] + near[channels:]

        hid_m, pg_m = activation(pre_m, grad_m)
        hid_0, pg_0 = activation(pre_0, grad_0)
        hid_7, pg_7 = activation(pre_7, grad_7)
        hid_p, pg_p = activation(pre_p, grad_p)
        for index, pg in enumerate((pg_m, pg_0, pg_7, pg_p)):
            pg_ref[index, :, :] = pg

        zero = jnp.zeros((channels, cells), BF16)
        grad_two = g2_ref[...]
        for a, stack in ((0, (hid_m, hid_0, zero)), (1, (hid_0, zero, zero)),
                         (last - 1, (zero, zero, hid_7)), (last, (zero, hid_7, hid_p))):
            grad_two = grad_two + dot_nt(cs_ref[a * span:(a + 1) * span, :], jnp.concatenate(stack, axis=0))
        low_end = dot_nt(pg_0, halo(xh_ref, 1))
        low_own = dot_nt(pg_0, xs_ref[0:2 * span, :])
        high_own = dot_nt(pg_7, xs_ref[(last - 1) * span:(last + 1) * span, :])
        high_end = dot_nt(pg_7, halo(xh_ref, 2))

        def put(ref, one):
            if one:
                ref[:, 0:span] = g1_ref[:, 0:span] + low_end + high_own[:, 0:span]
                ref[:, span:2 * span] = g1_ref[:, span:2 * span] + low_own[:, 0:span] + high_own[:, span:]
                ref[:, 2 * span:] = g1_ref[:, 2 * span:] + low_own[:, span:] + high_end
            else:
                for step in range(3):
                    for tap in range(9):
                        at = (9 * step + tap) * channels
                        ref[:, at:at + channels] = grad_two[
                            (8 - tap) * channels:(9 - tap) * channels, step * channels:(step + 1) * channels]

        @pl.when(odd == 0)
        def _():
            put(keep_ref, True)
            put(send_ref, False)

        @pl.when(odd == 1)
        def _():
            put(keep_ref, False)
            put(send_ref, True)

    return kernel


def make_input_kernel(count, channels, cells, vertical):
    span = 9 * channels
    wide = 3 * channels

    def kernel(pi_ref, pe_ref, g_ref, ws_ref, lo_ref, hi_ref, out_ref, ps_ref):
        fill = filler(ps_ref, channels, tap_masks(cells, vertical), vertical)
        total = {}
        for a in range(-1, count + 1):
            plane = pe_ref[a + 1] if a <= 0 else pe_ref[a - count + 3] if a >= count - 1 else pi_ref[a - 1]
            fill(a + 1, plane)
            columns = ps_ref[(a + 1) * span:(a + 2) * span, :]
            if a == -1:
                total[0] = dot(lo_ref[2 * wide:2 * wide + channels, :], columns)
            elif a == count:
                total[count - 1] = total[count - 1] + dot(hi_ref[3 * wide - channels:3 * wide, :], columns)
            else:
                y = dot(ws_ref[2 * wide:3 * wide, :], columns)
                for step in range(3):
                    target = a + 1 - step
                    if 0 <= target < count:
                        part = y[step * channels:(step + 1) * channels]
                        total[target] = part if target not in total else total[target] + part
            if a >= 1:
                out_ref[a - 1, :, :] = g_ref[a - 1].astype(F32) + total.pop(a - 1)

    return kernel


def normalize_kernel(mine_ref, other_ref, one_ref, two_ref):
    odd = lax.axis_index(AXIS) % 2

    def scaled(ref):
        v = ref[...]
        return v / jnp.sqrt(jnp.mean(v * v) + 1e-06)

    @pl.when(odd == 0)
    def _():
        one_ref[...] = scaled(mine_ref)
        two_ref[...] = scaled(other_ref)

    @pl.when(odd == 1)
    def _():
        one_ref[...] = scaled(other_ref)
        two_ref[...] = scaled(mine_ref)


VM = pl.BlockSpec(memory_space=pltpu.VMEM)
SM = pl.BlockSpec(memory_space=pltpu.SMEM)
HB = pl.BlockSpec(memory_space=pltpu.HBM)
PARAMS = pltpu.CompilerParams(vmem_limit_bytes=VMEM_LIMIT)


def body(snapshot, cotangent, first_weight, second_weight, face_codes):
    count, channels, cells = snapshot.shape[1:]
    vertical = cells // R_CELLS
    size = lax.axis_size(AXIS)
    x, g = snapshot[0], cotangent[0]
    def call(kernel, outs, operands, name, scratch=(), specs=None):
        return pl.pallas_call(
            kernel, out_shape=outs, in_specs=specs or [VM] * len(operands),
            out_specs=jax.tree.map(lambda _: VM, outs),
            scratch_shapes=list(scratch), compiler_params=PARAMS, name=name,
        )(*operands)

    span = 9 * channels
    shape = jax.ShapeDtypeStruct
    sizes = (count, channels, cells, vertical)
    stack = shape((span, span), BF16)
    edges = shape((4, channels, cells), F32)
    columns = shape((count * span, cells), BF16)
    grads = shape((channels, 27 * channels), F32)
    half = shape((4, channels, cells), BF16)
    cross, pair, codes, x, g, first_weight, second_weight = call(
        make_pack_kernel(count, channels, cells),
        (half, half, shape((2, 8, 128), jnp.int32), shape(x.shape, BF16), shape(x.shape, BF16),
         shape(first_weight.shape, BF16), shape(first_weight.shape, BF16)),
        tuple(pltpu.with_memory_space_constraint(v, pltpu.HBM) for v in (face_codes, x, g, first_weight, second_weight)),
        "pack", [pltpu.SMEM((1, 2), jnp.int32), pltpu.SemaphoreType.DMA((5,))], [HB] * 5)

    def cross_of(b):
        return (b + 1) % size if b % 2 == 1 else (b - 1) % size

    cross = lax.ppermute(cross, AXIS, [(b, cross_of(b)) for b in range(size)])
    pair = lax.ppermute(pair, AXIS, [(b, b ^ 1) for b in range(size)])
    ws, lo, hi, turn, pre_edge, grad_edge, xs, cs, pg_inner, part_one, part_two = call(
        make_interior_kernel(*sizes),
        (stack, stack, stack, shape((2, cells, cells), BF16), edges, edges, columns, columns,
         shape((count - 2, channels, cells), BF16), grads, shape((span, 3 * channels), F32)),
        (codes, x, g, first_weight, second_weight), "interior",
        [pltpu.VMEM(((count + 2) * channels, cells), BF16), pltpu.VMEM(((count + 3) * channels, cells), BF16)])
    keep, send, pg_edge = call(
        make_edge_kernel(*sizes), (grads, grads, shape((4, channels, cells), BF16)),
        (pair, cross, ws, lo, hi, turn, pre_edge, grad_edge, xs, cs, part_one, part_two), "edge",
        [pltpu.VMEM((4 * span, cells), BF16), pltpu.VMEM((4 * span, cells), BF16)])

    def swap(value, bit):
        return lax.ppermute(value, AXIS, [(b, b ^ bit) for b in range(size)])

    input_grad = call(
        make_input_kernel(*sizes), shape((count, channels, cells), F32), (pg_inner, pg_edge, g, ws, lo, hi),
        "input_grad", [pltpu.VMEM(((count + 2) * span, cells), BF16)])
    total = keep + swap(send, 1)
    bit = 2
    while bit < size:
        total = total + swap(total, bit)
        if bit == 2:
            total, input_grad = lax.optimization_barrier((total, input_grad))
        bit *= 2
    first, second = call(normalize_kernel, (grads, grads), (total, swap(total, 1)), "normalize")
    return (input_grad[None], first, second)


def solution(mesh):
    return jax.shard_map(
        body,
        mesh=mesh,
        in_specs=(
            P("groups", "blocks", None, None),
            P("groups", "blocks", None, None),
            P(),
            P(),
            P(("groups", "blocks"), None),
        ),
        out_specs=(P("groups", "blocks", None, None), P("groups", None), P("groups", None)),
        check_vma=False,
    )
```

```python
import jax
import jax.numpy as jnp
from jax import lax
from jax.experimental import pallas as pl
from jax.experimental.pallas import tpu as pltpu
from jax.sharding import PartitionSpec as P

R_CELLS = 32
AXIS = "blocks"
F32 = jnp.float32
BF16 = jnp.bfloat16
ORDER = (0, 1, 2, 3, 5, 6, 7, 8, 4)
VMEM_LIMIT = 24 * 1024 * 1024


def tap_masks(cells, vertical):
    lane = lax.broadcasted_iota(jnp.int32, (1, cells), 1)
    z = lane % vertical
    r = lane // vertical
    radial = cells // vertical
    masks = []
    for step_r in range(3):
        for step_z in range(3):
            ok = None
            if step_r == 0:
                ok = r >= 1
            if step_r == 2:
                ok = r < radial - 1
            if step_z == 0:
                ok = (z >= 1) if ok is None else ok & (z >= 1)
            if step_z == 2:
                ok = (z < vertical - 1) if ok is None else ok & (z < vertical - 1)
            masks.append(ok)
    return masks


def im2col(plane, store, masks, vertical):
    cells = plane.shape[1]
    wide = plane.astype(F32)
    for place, tap in enumerate(ORDER):
        offset = (tap // 3 - 1) * vertical + (tap % 3 - 1)
        if offset == 0:
            store(place, plane)
            continue
        moved = pltpu.roll(wide, (-offset) % cells, 1)
        moved = jnp.where(masks[tap], moved, 0.0)
        store(place, moved.astype(BF16))


def dot(a, b):
    return jnp.dot(a, b, preferred_element_type=F32)


def dot_nt(a, b):
    return lax.dot_general(a, b, (((1,), (1,)), ((), ())), preferred_element_type=F32)


def flip_planes(planes, code, vertical):
    lanes = 128
    parts = planes.shape[1] // lanes
    wide = planes.astype(F32)
    turn_r = code % 2 == 1
    bits = jnp.where(turn_r, lanes - vertical, 0) + jnp.where(code // 2 == 1, vertical - 1, 0)
    index = lax.broadcasted_iota(jnp.int32, (planes.shape[0], lanes), 1) ^ bits
    moved = [jnp.take_along_axis(wide[:, j * lanes:(j + 1) * lanes], index, axis=1) for j in range(parts)]
    return jnp.concatenate(
        [jnp.where(turn_r, moved[parts - 1 - j], moved[j]) for j in range(parts)], axis=1).astype(BF16)


def tap_flip_matrix(code, channels):
    size = 9 * channels
    row = lax.broadcasted_iota(jnp.int32, (size, size), 0)
    col = lax.broadcasted_iota(jnp.int32, (1, size), 1)
    place = col // channels
    tap = jnp.where(place == 8, 4, jnp.where(place >= 4, place + 1, place))
    r, z = tap // 3, tap % 3
    r = jnp.where(code % 2 == 1, 2 - r, r)
    z = jnp.where(code // 2 == 1, 2 - z, z)
    tap = 3 * r + z
    place = jnp.where(tap == 4, 8, jnp.where(tap > 4, tap - 1, tap))
    return jnp.where(row == place * channels + col % channels, 1.0, 0.0).astype(BF16)


def activation(pre, grad):
    sig = jax.nn.sigmoid(pre)
    hidden = (pre * sig).astype(BF16)
    return hidden, (grad * sig * (1.0 + pre * (1.0 - sig))).astype(BF16)


def filler(ref, channels, masks, vertical):
    def fill(position, plane):
        def store(tap, value):
            start = (9 * position + tap) * channels
            ref[start:start + channels, :] = value

        im2col(plane, store, masks, vertical)

    return fill


def make_pack_kernel(count):
    def kernel(codes_ref, x_ref, g_ref, w1_ref, w2_ref,
               cross_ref, pair_ref, codes_out, x_out, g_out, w1_out, w2_out, scalars, sems):
        moves = ((x_ref, x_out), (g_ref, g_out), (codes_ref, scalars), (w1_ref, w1_out), (w2_ref, w2_out))
        copies = [pltpu.make_async_copy(*move, sems.at[index]) for index, move in enumerate(moves)]
        for copy in copies:
            copy.start()
        is_odd = lax.axis_index(AXIS) % 2 == 1
        for index, field in enumerate((x_out, g_out)):
            copies[index].wait()
            low, high = field[0:2], field[count - 2:count]
            cross_ref[2 * index:2 * index + 2, :, :] = jnp.where(is_odd, high, low)
            pair_ref[2 * index:2 * index + 2, :, :] = jnp.where(is_odd, low, high)
        for copy in copies[2:]:
            copy.wait()
        for side in range(2):
            codes_out[side, :, :] = jnp.full((8, 128), scalars[0, side], jnp.int32)

    return kernel


def make_interior_kernel(count, channels, cells, vertical):
    span = 9 * channels
    most = 8 * channels
    wide = 3 * channels
    last = count - 1

    def kernel(codes_ref, x_ref, g_ref, w1_ref, w2_ref,
               ws_ref, lo_ref, hi_ref, t1_ref, t2_ref, pe_ref, ge_ref, xs_ref, cs_ref, pg_ref, g1_ref, g2_ref,
               h_ref, pr_ref):
        masks = tap_masks(cells, vertical)
        for step in range(3):
            rows = slice(step * channels, (step + 1) * channels)
            base = step * span
            half = 4 * channels
            ws_ref[rows, 0:half] = w1_ref[:, base:base + half]
            ws_ref[rows, half:most] = w1_ref[:, base + half + channels:base + span]
            ws_ref[rows, most:span] = w1_ref[:, base + half:base + half + channels]
        for weight_ref, base in ((w2_ref, wide), (w1_ref, 2 * wide)):
            turned = weight_ref[...].astype(F32).T
            for step in range(3):
                for place, tap in enumerate(ORDER):
                    at = (9 * (2 - step) + 8 - tap) * channels
                    ws_ref[base + step * channels:base + (step + 1) * channels,
                           place * channels:(place + 1) * channels] = turned[at:at + channels, :].astype(BF16)
        lo_ref[...] = dot(ws_ref[...], tap_flip_matrix(codes_ref[0, 0:1, 0:1], channels)).astype(BF16)
        hi_ref[...] = dot(ws_ref[...], tap_flip_matrix(codes_ref[1, 0:1, 0:1], channels)).astype(BF16)
        for ref, base in ((t1_ref, 0), (t2_ref, wide)):
            ref[...] = jnp.zeros_like(ref)
            for step in range(3):
                centre = ws_ref[base + step * channels:base + (step + 1) * channels, most:span]
                for a in range(count):
                    row = (a + 2 - step) * channels
                    ref[row:row + channels, a * channels:(a + 1) * channels] = centre

        fill_x = filler(xs_ref, channels, masks, vertical)
        fill_g = filler(cs_ref, channels, masks, vertical)
        for a in range(count):
            fill_x(a, x_ref[a])
            fill_g(a, g_ref[a])

        h_ref[...] = jnp.zeros_like(h_ref)
        pr_ref[...] = jnp.zeros_like(pr_ref)
        pre_all = dot(t1_ref[...], x_ref[...].reshape(count * channels, cells))
        grad_all = dot(t2_ref[...], g_ref[...].reshape(count * channels, cells))
        pre = {a: pre_all[(a + 1) * channels:(a + 2) * channels] for a in range(-1, count + 1)}
        grad = {a: grad_all[(a + 1) * channels:(a + 2) * channels] for a in range(-1, count + 1)}

        for a in range(count):
            columns = slice(a * span, a * span + most)
            y = dot(ws_ref[0:wide, 0:most], xs_ref[columns, :])
            v = dot(ws_ref[wide:2 * wide, 0:most], cs_ref[columns, :])
            for step in range(3):
                target = a + 1 - step
                rows = slice(step * channels, (step + 1) * channels)
                grad[target] = grad[target] + v[rows]
                if 0 <= target <= last:
                    pre[target] = pre[target] + y[rows]
            if a == 0:
                pre[-1] = pre[-1] + dot(lo_ref[2 * channels:wide, 0:most], xs_ref[columns, :])
            if a == last:
                pre[count] = pre[count] + dot(hi_ref[0:channels, 0:most], xs_ref[columns, :])
            done = a - 1
            if 1 <= done <= last - 1:
                hidden, pg = activation(pre.pop(done), grad.pop(done))
                h_ref[(done + 1) * channels:(done + 2) * channels, :] = hidden
                pg_ref[done - 1, :, :] = pg
                place = count + 1 - done
                pr_ref[place * channels:(place + 1) * channels, :] = pg
            if a == 1:
                for index, plane in ((0, -1), (1, 0)):
                    pe_ref[index, :, :] = pre.pop(plane)
                    ge_ref[index, :, :] = grad.pop(plane)
        for index, plane in ((2, last), (3, count)):
            pe_ref[index, :, :] = pre.pop(plane)
            ge_ref[index, :, :] = grad.pop(plane)

        grad_one, grad_two = None, None
        for a in range(0, count, 2):
            pairs = slice(a * span, (a + 2) * span)
            term = dot_nt(cs_ref[pairs, :], h_ref[a * channels:(a + 4) * channels, :])
            grad_two = term if grad_two is None else grad_two + term
            start = (count - 1 - a) * channels
            term = dot_nt(xs_ref[pairs, :], pr_ref[start:start + 4 * channels, :])
            grad_one = term if grad_one is None else grad_one + term
        g2_ref[...] = grad_two
        turned = grad_one.T
        for step in range(3):
            first, second = (step + 1) * channels, step * channels
            g1_ref[:, step * span:(step + 1) * span] = (
                turned[first:first + channels, 0:span] + turned[second:second + channels, span:])

    return kernel


def make_edge_kernel(count, channels, cells, vertical):
    span = 9 * channels
    most = 8 * channels
    wide = 3 * channels
    last = count - 1

    def kernel(cross_ref, pair_ref, ws_ref, lo_ref, hi_ref, t1_ref, t2_ref, codes_ref, pe_ref, ge_ref, xs_ref, cs_ref,
               g1_ref, g2_ref, keep_ref, send_ref, pg_ref, xh_ref, ch_ref):
        odd = lax.axis_index(AXIS) % 2
        is_odd = odd == 1
        masks = tap_masks(cells, vertical)
        fill_x = filler(xh_ref, channels, masks, vertical)
        fill_c = filler(ch_ref, channels, masks, vertical)
        pair = pair_ref[...].reshape(4 * channels, cells)
        cross = cross_ref[...].reshape(4 * channels, cells)
        centres = []
        for side in range(2):
            planes = jnp.where(is_odd, pair, cross) if side == 0 else jnp.where(is_odd, cross, pair)
            planes = flip_planes(planes, codes_ref[side, 0:1, 0:1], vertical)
            for index in range(2):
                fill_x(2 * side + index, planes[index * channels:(index + 1) * channels])
                fill_c(2 * side + index, planes[(index + 2) * channels:(index + 3) * channels])
            top = 2 * channels if side == 0 else 0
            for index, ref in enumerate((t1_ref, t2_ref)):
                centres.append(dot(ref[top:top + 2 * channels, 0:2 * channels],
                                   planes[2 * index * channels:2 * (index + 1) * channels]))

        def halo(ref, index, end=most):
            return ref[index * span:index * span + end, :]

        def rows(ref, part, first, end):
            return ref[part * wide + first * channels:part * wide + end * channels, 0:most]

        x_low, g_low, x_high, g_high = centres
        near = dot(jnp.concatenate([rows(lo_ref, 0, 1, 2), rows(ws_ref, 0, 0, 1)], axis=0), halo(xh_ref, 1)) + x_low
        pre_m = pe_ref[0] + near[:channels] + dot(rows(lo_ref, 0, 0, 1), halo(xh_ref, 0))
        pre_0 = pe_ref[1] + near[channels:]
        near = dot(rows(lo_ref, 1, 0, 2), halo(ch_ref, 1))
        grad_m = ge_ref[0] + near[channels:] + g_low[:channels] + dot(rows(lo_ref, 1, 0, 1), halo(ch_ref, 0))
        grad_0 = ge_ref[1] + near[:channels] + g_low[channels:]
        near = dot(jnp.concatenate([rows(ws_ref, 0, 2, 3), rows(hi_ref, 0, 1, 2)], axis=0), halo(xh_ref, 2)) + x_high
        pre_p = pe_ref[3] + near[channels:] + dot(rows(hi_ref, 0, 2, 3), halo(xh_ref, 3))
        pre_7 = pe_ref[2] + near[:channels]
        near = dot(rows(hi_ref, 1, 1, 3), halo(ch_ref, 2))
        grad_p = ge_ref[3] + near[:channels] + g_high[channels:] + dot(rows(hi_ref, 1, 2, 3), halo(ch_ref, 3))
        grad_7 = ge_ref[2] + near[channels:] + g_high[:channels]

        hid_m, pg_m = activation(pre_m, grad_m)
        hid_0, pg_0 = activation(pre_0, grad_0)
        hid_7, pg_7 = activation(pre_7, grad_7)
        hid_p, pg_p = activation(pre_p, grad_p)
        for index, pg in enumerate((pg_m, pg_0, pg_7, pg_p)):
            pg_ref[index, :, :] = pg

        zero = jnp.zeros((2 * channels, cells), BF16)
        grad_two = g2_ref[...]
        for a, stack in ((0, (hid_m, hid_0, zero)), (last - 1, (zero, hid_7, hid_p))):
            grad_two = grad_two + dot_nt(cs_ref[a * span:(a + 2) * span, :], jnp.concatenate(stack, axis=0))
        low_end = dot_nt(pg_0, halo(xh_ref, 1, span))
        low_own = dot_nt(pg_0, xs_ref[0:2 * span, :])
        high_own = dot_nt(pg_7, xs_ref[(last - 1) * span:(last + 1) * span, :])
        high_end = dot_nt(pg_7, halo(xh_ref, 2, span))

        def put(ref, one):
            if one:
                ref[:, 0:span] = g1_ref[:, 0:span] + low_end + high_own[:, 0:span]
                ref[:, span:2 * span] = g1_ref[:, span:2 * span] + low_own[:, 0:span] + high_own[:, span:]
                ref[:, 2 * span:] = g1_ref[:, 2 * span:] + low_own[:, span:] + high_end
            else:
                for step in range(3):
                    for place, tap in enumerate(ORDER):
                        at = (9 * step + 8 - tap) * channels
                        top = place * channels
                        ref[:, at:at + channels] = (
                            grad_two[top:top + channels, step * channels:(step + 1) * channels]
                            + grad_two[span + top:span + top + channels, (step + 1) * channels:(step + 2) * channels])

        @pl.when(odd == 0)
        def _():
            put(keep_ref, True)
            put(send_ref, False)

        @pl.when(odd == 1)
        def _():
            put(keep_ref, False)
            put(send_ref, True)

    return kernel


def make_input_kernel(count, channels, cells, vertical):
    span = 9 * channels
    wide = 3 * channels

    def kernel(pi_ref, pe_ref, g_ref, ws_ref, lo_ref, hi_ref, out_ref, ps_ref):
        fill = filler(ps_ref, channels, tap_masks(cells, vertical), vertical)
        total = {}
        for a in range(-1, count + 1):
            plane = pe_ref[a + 1] if a <= 0 else pe_ref[a - count + 3] if a >= count - 1 else pi_ref[a - 1]
            fill(a + 1, plane)
            columns = ps_ref[(a + 1) * span:(a + 2) * span, :]
            if a == -1:
                total[0] = dot(lo_ref[2 * wide:2 * wide + channels, :], columns)
            elif a == count:
                total[count - 1] = total[count - 1] + dot(hi_ref[3 * wide - channels:3 * wide, :], columns)
            else:
                y = dot(ws_ref[2 * wide:3 * wide, :], columns)
                for step in range(3):
                    target = a + 1 - step
                    if 0 <= target < count:
                        part = y[step * channels:(step + 1) * channels]
                        total[target] = part if target not in total else total[target] + part
            if a >= 1:
                out_ref[a - 1, :, :] = g_ref[a - 1].astype(F32) + total.pop(a - 1)

    return kernel


def normalize_kernel(mine_ref, other_ref, one_ref, two_ref):
    odd = lax.axis_index(AXIS) % 2
    span = mine_ref.shape[1] // 3
    part = span // 9

    def scaled(ref):
        v = ref[...]
        return v / jnp.sqrt(jnp.mean(v * v) + 1e-06)

    def put(ref, value):
        for step in range(3):
            base = step * span
            ref[:, base:base + 4 * part] = value[:, base:base + 4 * part]
            ref[:, base + 4 * part:base + 5 * part] = value[:, base + 8 * part:base + span]
            ref[:, base + 5 * part:base + span] = value[:, base + 4 * part:base + 8 * part]

    @pl.when(odd == 0)
    def _():
        put(one_ref, scaled(mine_ref))
        two_ref[...] = scaled(other_ref)

    @pl.when(odd == 1)
    def _():
        put(one_ref, scaled(other_ref))
        two_ref[...] = scaled(mine_ref)


VM = pl.BlockSpec(memory_space=pltpu.VMEM)
SM = pl.BlockSpec(memory_space=pltpu.SMEM)
HB = pl.BlockSpec(memory_space=pltpu.HBM)
PARAMS = pltpu.CompilerParams(vmem_limit_bytes=VMEM_LIMIT)


def body(snapshot, cotangent, first_weight, second_weight, face_codes):
    count, channels, cells = snapshot.shape[1:]
    vertical = cells // R_CELLS
    size = lax.axis_size(AXIS)
    x, g = snapshot[0], cotangent[0]
    def call(kernel, outs, operands, name, scratch=(), specs=None):
        return pl.pallas_call(
            kernel, out_shape=outs, in_specs=specs or [VM] * len(operands),
            out_specs=jax.tree.map(lambda _: VM, outs),
            scratch_shapes=list(scratch), compiler_params=PARAMS, name=name,
        )(*operands)

    span = 9 * channels
    shape = jax.ShapeDtypeStruct
    sizes = (count, channels, cells, vertical)
    stack = shape((span, span), BF16)
    band = shape(((count + 2) * channels, count * channels), BF16)
    edges = shape((4, channels, cells), F32)
    columns = shape((count * span, cells), BF16)
    grads = shape((channels, 27 * channels), F32)
    half = shape((4, channels, cells), BF16)
    weight = shape(first_weight.shape, BF16)
    pinned = [
        pltpu.with_memory_space_constraint(v, pltpu.HBM) for v in (face_codes, x, g, first_weight, second_weight)]
    cross, pair, codes, x, g, first_weight, second_weight = call(
        make_pack_kernel(count),
        (half, half, shape((2, 8, 128), jnp.int32), shape(x.shape, BF16), shape(x.shape, BF16), weight, weight),
        pinned, "pack", [pltpu.SMEM((1, 2), jnp.int32), pltpu.SemaphoreType.DMA((5,))], [HB] * 5)

    def cross_of(b):
        return (b + 1) % size if b % 2 == 1 else (b - 1) % size

    pair = lax.ppermute(pair, AXIS, [(b, b ^ 1) for b in range(size)])
    cross = lax.ppermute(cross, AXIS, [(b, cross_of(b)) for b in range(size)])
    ws, lo, hi, band_one, band_two, pre_edge, grad_edge, xs, cs, pg_inner, part_one, part_two = call(
        make_interior_kernel(*sizes),
        (stack, stack, stack, band, band, edges, edges, columns, columns,
         shape((count - 2, channels, cells), BF16), grads, shape((2 * span, 4 * channels), F32)),
        (codes, x, g, first_weight, second_weight), "interior",
        [pltpu.VMEM(((count + 2) * channels, cells), BF16), pltpu.VMEM(((count + 3) * channels, cells), BF16)])
    keep, send, pg_edge = call(
        make_edge_kernel(*sizes), (grads, grads, shape((4, channels, cells), BF16)),
        (cross, pair, ws, lo, hi, band_one, band_two, codes, pre_edge, grad_edge, xs, cs, part_one, part_two), "edge",
        [pltpu.VMEM((4 * span, cells), BF16), pltpu.VMEM((4 * span, cells), BF16)])

    def swap(value, bit):
        return lax.ppermute(value, AXIS, [(b, b ^ bit) for b in range(size)])

    input_grad = call(
        make_input_kernel(*sizes), shape((count, channels, cells), F32), (pg_inner, pg_edge, g, ws, lo, hi),
        "input_grad", [pltpu.VMEM(((count + 2) * span, cells), BF16)])
    total = keep + swap(send, 1)
    bit = 2
    while bit < size:
        total = total + swap(total, bit)
        if bit == 2:
            total, input_grad = lax.optimization_barrier((total, input_grad))
        bit *= 2
    first, second = call(normalize_kernel, (grads, grads), (total, swap(total, 1)), "normalize")
    return (input_grad[None], first, second)


def solution(mesh):
    return jax.shard_map(
        body,
        mesh=mesh,
        in_specs=(
            P("groups", "blocks", None, None),
            P("groups", "blocks", None, None),
            P(),
            P(),
            P(("groups", "blocks"), None),
        ),
        out_specs=(P("groups", "blocks", None, None), P("groups", None), P("groups", None)),
        check_vma=False,
    )
```

```python
import jax
import jax.numpy as jnp
from jax import lax
from jax.experimental import pallas as pl
from jax.experimental.pallas import tpu as pltpu
from jax.sharding import PartitionSpec as P

R_CELLS = 32
AXIS = "blocks"
F32 = jnp.float32
BF16 = jnp.bfloat16
ORDER = (0, 1, 2, 3, 5, 6, 7, 8, 4)
VMEM_LIMIT = 24 * 1024 * 1024


def tap_masks(cells, vertical):
    lane = lax.broadcasted_iota(jnp.int32, (1, cells), 1)
    z = lane % vertical
    r = lane // vertical
    radial = cells // vertical
    masks = []
    for step_r in range(3):
        for step_z in range(3):
            ok = None
            if step_r == 0:
                ok = r >= 1
            if step_r == 2:
                ok = r < radial - 1
            if step_z == 0:
                ok = (z >= 1) if ok is None else ok & (z >= 1)
            if step_z == 2:
                ok = (z < vertical - 1) if ok is None else ok & (z < vertical - 1)
            masks.append(ok)
    return masks


def im2col(plane, store, masks, vertical):
    cells = plane.shape[1]
    wide = plane.astype(F32)
    for place, tap in enumerate(ORDER):
        offset = (tap // 3 - 1) * vertical + (tap % 3 - 1)
        if offset == 0:
            store(place, plane)
            continue
        moved = pltpu.roll(wide, (-offset) % cells, 1)
        moved = jnp.where(masks[tap], moved, 0.0)
        store(place, moved.astype(BF16))


def dot(a, b):
    return jnp.dot(a, b, preferred_element_type=F32)


def dot_nt(a, b):
    return lax.dot_general(a, b, (((1,), (1,)), ((), ())), preferred_element_type=F32)


def flip_planes(planes, code, vertical):
    lanes = 128
    parts = planes.shape[1] // lanes
    wide = planes.astype(F32)
    turn_r = code % 2 == 1
    bits = jnp.where(turn_r, lanes - vertical, 0) + jnp.where(code // 2 == 1, vertical - 1, 0)
    index = lax.broadcasted_iota(jnp.int32, (planes.shape[0], lanes), 1) ^ bits
    moved = [jnp.take_along_axis(wide[:, j * lanes:(j + 1) * lanes], index, axis=1) for j in range(parts)]
    return jnp.concatenate(
        [jnp.where(turn_r, moved[parts - 1 - j], moved[j]) for j in range(parts)], axis=1).astype(BF16)


def flipped_places(code):
    flip_r, flip_z = code % 2, code // 2
    places = []
    for tap in ORDER:
        r, z = tap // 3, tap % 3
        moved = 3 * (r + (2 - 2 * r) * flip_r) + z + (2 - 2 * z) * flip_z
        places.append(8 if tap == 4 else moved - (moved > 4).astype(jnp.int32))
    return places


def activation(pre, grad):
    sig = jax.nn.sigmoid(pre)
    hidden = (pre * sig).astype(BF16)
    return hidden, (grad * sig * (1.0 + pre * (1.0 - sig))).astype(BF16)


def filler(ref, channels, masks, vertical):
    def fill(position, plane, places=None, also=None):
        def store(place, value):
            if places is None:
                start = (9 * position + place) * channels
            else:
                start = pl.multiple_of((9 * position + places[place]) * channels, channels)
            ref[pl.ds(start, channels), :] = value
            if also is not None:
                also[place * channels:(place + 1) * channels, :] = value

        im2col(plane, store, masks, vertical)

    return fill


def make_pack_kernel(count):
    def kernel(codes_ref, x_ref, g_ref, w1_ref, w2_ref, up_ref, codes_out, x_out, g_out, w1_out, w2_out, scalars, sems):
        moves = ((x_ref, x_out), (g_ref, g_out), (codes_ref, scalars), (w1_ref, w1_out), (w2_ref, w2_out))
        copies = [pltpu.make_async_copy(*move, sems.at[index]) for index, move in enumerate(moves)]
        for copy in copies:
            copy.start()
        for index, field in enumerate((x_out, g_out)):
            copies[index].wait()
            up_ref[2 * index:2 * index + 2, :, :] = field[count - 2:count]
        for copy in copies[2:]:
            copy.wait()
        for side in range(2):
            codes_out[side, :, :] = jnp.full((8, 128), scalars[0, side], jnp.int32)

    return kernel


def make_interior_kernel(count, channels, cells, vertical):
    span = 9 * channels
    most = 8 * channels
    wide = 3 * channels
    last = count - 1

    def kernel(x_ref, g_ref, w1_ref, w2_ref,
               ws_ref, t1_ref, t2_ref, pe_ref, ge_ref, xs_ref, cs_ref, pg_ref, g1_ref, g2_ref,
               h_ref, pr_ref):
        masks = tap_masks(cells, vertical)
        for step in range(3):
            rows = slice(step * channels, (step + 1) * channels)
            base = step * span
            half = 4 * channels
            ws_ref[rows, 0:half] = w1_ref[:, base:base + half]
            ws_ref[rows, half:most] = w1_ref[:, base + half + channels:base + span]
            ws_ref[rows, most:span] = w1_ref[:, base + half:base + half + channels]
        for weight_ref, base in ((w2_ref, wide), (w1_ref, 2 * wide)):
            turned = weight_ref[...].astype(F32).T
            for step in range(3):
                for place, tap in enumerate(ORDER):
                    at = (9 * (2 - step) + 8 - tap) * channels
                    ws_ref[base + step * channels:base + (step + 1) * channels,
                           place * channels:(place + 1) * channels] = turned[at:at + channels, :].astype(BF16)
        for ref, base in ((t1_ref, 0), (t2_ref, wide)):
            ref[...] = jnp.zeros_like(ref)
            for step in range(3):
                centre = ws_ref[base + step * channels:base + (step + 1) * channels, most:span]
                for a in range(count):
                    row = (a + 2 - step) * channels
                    ref[row:row + channels, a * channels:(a + 1) * channels] = centre

        fill_x = filler(xs_ref, channels, masks, vertical)
        fill_g = filler(cs_ref, channels, masks, vertical)
        for a in range(count):
            fill_x(a, x_ref[a])
            fill_g(a, g_ref[a])

        h_ref[...] = jnp.zeros_like(h_ref)
        pr_ref[...] = jnp.zeros_like(pr_ref)
        pre_all = dot(t1_ref[...], x_ref[...].reshape(count * channels, cells))
        grad_all = dot(t2_ref[...], g_ref[...].reshape(count * channels, cells))
        pre = {a: pre_all[(a + 1) * channels:(a + 2) * channels] for a in range(-1, last)}
        grad = {a: grad_all[(a + 1) * channels:(a + 2) * channels] for a in range(-1, last)}

        for a in range(count):
            columns = slice(a * span, a * span + most)
            first = max(0, a + 2 - last) * channels
            y = dot(ws_ref[first:wide, 0:most], xs_ref[columns, :])
            v = dot(ws_ref[wide + first:2 * wide, 0:most], cs_ref[columns, :])
            for step in range(3):
                target = a + 1 - step
                rows = slice(step * channels - first, (step + 1) * channels - first)
                if -1 <= target < last:
                    grad[target] = grad[target] + v[rows]
                if 0 <= target < last:
                    pre[target] = pre[target] + y[rows]
            done = a - 1
            if 1 <= done <= last - 1:
                hidden, pg = activation(pre.pop(done), grad.pop(done))
                h_ref[(done + 1) * channels:(done + 2) * channels, :] = hidden
                pg_ref[done - 1, :, :] = pg
                place = count + 1 - done
                pr_ref[place * channels:(place + 1) * channels, :] = pg
            if a == 1:
                for index, plane in ((0, -1), (1, 0)):
                    pe_ref[index, :, :] = pre.pop(plane)
                    ge_ref[index, :, :] = grad.pop(plane)
        grad_one, grad_two = None, None
        for a in range(0, count, 2):
            pairs = slice(a * span, (a + 2) * span)
            term = dot_nt(cs_ref[pairs, :], h_ref[a * channels:(a + 4) * channels, :])
            grad_two = term if grad_two is None else grad_two + term
            start = (count - 1 - a) * channels
            term = dot_nt(xs_ref[pairs, :], pr_ref[start:start + 4 * channels, :])
            grad_one = term if grad_one is None else grad_one + term
        g2_ref[...] = grad_two
        turned = grad_one.T
        for step in range(3):
            first, second = (step + 1) * channels, step * channels
            g1_ref[:, step * span:(step + 1) * span] = (
                turned[first:first + channels, 0:span] + turned[second:second + channels, span:])

    return kernel


def make_edge_kernel(count, channels, cells, vertical):
    span = 9 * channels
    most = 8 * channels
    wide = 3 * channels

    def kernel(up_ref, ws_ref, t1_ref, t2_ref, codes_ref, pe_ref, ge_ref, xs_ref, cs_ref, g1_ref, g2_ref,
               keep_ref, send_ref, pg_ref, xf_ref, xo_ref, cf_ref):
        odd = lax.axis_index(AXIS) % 2
        masks = tap_masks(cells, vertical)
        places = flipped_places(codes_ref[0, 0, 0])
        fill_x = filler(xf_ref, channels, masks, vertical)
        fill_c = filler(cf_ref, channels, masks, vertical)
        planes = flip_planes(up_ref[...].reshape(4 * channels, cells), codes_ref[0, 0:1, 0:1], vertical)
        fill_x(0, planes[0:channels], places)
        fill_x(1, planes[channels:2 * channels], places, xo_ref)
        for place in range(9):
            start = 2 * span + places[place] * channels
            xf_ref[pl.ds(pl.multiple_of(start, channels), channels), :] = xs_ref[place * channels:(place + 1) * channels, :]
        fill_c(0, planes[2 * channels:3 * channels], places)
        fill_c(1, planes[3 * channels:], places)

        def eight(ref, index):
            return ref[index * span:index * span + most, :]

        def rows(part, first, end):
            return ws_ref[part * wide + first * channels:part * wide + end * channels, 0:most]

        centre = slice(2 * channels, 4 * channels), slice(0, 2 * channels)
        x_mid = dot(t1_ref[centre], planes[:2 * channels])
        g_mid = dot(t2_ref[centre], planes[2 * channels:])
        pre_m = (pe_ref[0] + x_mid[:channels] + dot(rows(0, 0, 1), eight(xf_ref, 0))
                 + dot(rows(0, 1, 2), eight(xf_ref, 1)) + dot(rows(0, 2, 3), eight(xf_ref, 2)))
        pre_0 = pe_ref[1] + x_mid[channels:] + dot(rows(0, 0, 1), eight(xo_ref, 0))
        near = dot(rows(1, 0, 2), eight(cf_ref, 1))
        grad_m = ge_ref[0] + g_mid[:channels] + near[channels:] + dot(rows(1, 0, 1), eight(cf_ref, 0))
        grad_0 = ge_ref[1] + g_mid[channels:] + near[:channels]
        hid_m, pg_m = activation(pre_m, grad_m)
        hid_0, pg_0 = activation(pre_0, grad_0)
        pg_ref[0, :, :] = pg_m
        pg_ref[1, :, :] = pg_0

        zero = jnp.zeros((2 * channels, cells), BF16)
        grad_two = (g2_ref[...] + dot_nt(cf_ref[...], jnp.concatenate((zero, hid_m, hid_0), axis=0))
                    + dot_nt(cs_ref[0:2 * span, :], jnp.concatenate((hid_m, hid_0, zero), axis=0)))
        below = dot_nt(pg_m, xf_ref[...])
        own_end = dot_nt(pg_0, xo_ref[...])
        own = dot_nt(pg_0, xs_ref[0:2 * span, :])

        def put(ref, one):
            if one:
                ref[:, 0:span] = g1_ref[:, 0:span] + below[:, 0:span] + own_end
                ref[:, span:] = g1_ref[:, span:] + below[:, span:] + own
            else:
                total = grad_two[0:span] + pltpu.roll(grad_two[span:], 3 * channels, 1)
                for place, tap in enumerate(ORDER):
                    block = total[place * channels:(place + 1) * channels]
                    shift = ((8 - tap) * channels) % (4 * channels)
                    block = pltpu.roll(block, shift, 1) if shift else block
                    for step in range(3):
                        at = (9 * step + 8 - tap) * channels
                        lane = at % (4 * channels)
                        ref[:, at:at + channels] = block[:, lane:lane + channels]

        @pl.when(odd == 0)
        def _():
            put(keep_ref, True)
            put(send_ref, False)

        @pl.when(odd == 1)
        def _():
            put(keep_ref, False)
            put(send_ref, True)

    return kernel


def make_input_kernel(count, channels, cells, vertical):
    span = 9 * channels
    wide = 3 * channels

    def kernel(pi_ref, pe_ref, down_ref, codes_ref, g_ref, ws_ref, out_ref, ps_ref):
        fill = filler(ps_ref, channels, tap_masks(cells, vertical), vertical)
        above = flip_planes(down_ref[...].reshape(2 * channels, cells), codes_ref[1, 0:1, 0:1], vertical)
        weights = ws_ref[2 * wide:3 * wide, :]
        total = {}
        for a in range(-1, count + 1):
            if a <= 0:
                plane = pe_ref[a + 1]
            elif a >= count - 1:
                plane = above[(a - count + 1) * channels:(a - count + 2) * channels]
            else:
                plane = pi_ref[a - 1]
            side = {-1: 0, count: 1}.get(a)
            fill(a + 1, plane, None if side is None else flipped_places(codes_ref[side, 0, 0]))
            columns = ps_ref[(a + 1) * span:(a + 2) * span, :]
            if a == -1:
                total[0] = dot(weights[0:channels], columns)
            elif a == count:
                total[count - 1] = total[count - 1] + dot(weights[2 * channels:], columns)
            else:
                y = dot(weights, columns)
                for step in range(3):
                    target = a + 1 - step
                    if 0 <= target < count:
                        part = y[step * channels:(step + 1) * channels]
                        total[target] = part if target not in total else total[target] + part
            if a >= 1:
                out_ref[a - 1, :, :] = g_ref[a - 1].astype(F32) + total.pop(a - 1)

    return kernel


def normalize_kernel(mine_ref, other_ref, one_ref, two_ref):
    odd = lax.axis_index(AXIS) % 2
    span = mine_ref.shape[1] // 3
    part = span // 9

    def scaled(ref):
        v = ref[...]
        return v / jnp.sqrt(jnp.mean(v * v) + 1e-06)

    def put(ref, value):
        for step in range(3):
            base = step * span
            ref[:, base:base + 4 * part] = value[:, base:base + 4 * part]
            ref[:, base + 4 * part:base + 5 * part] = value[:, base + 8 * part:base + span]
            ref[:, base + 5 * part:base + span] = value[:, base + 4 * part:base + 8 * part]

    @pl.when(odd == 0)
    def _():
        put(one_ref, scaled(mine_ref))
        two_ref[...] = scaled(other_ref)

    @pl.when(odd == 1)
    def _():
        put(one_ref, scaled(other_ref))
        two_ref[...] = scaled(mine_ref)


VM = pl.BlockSpec(memory_space=pltpu.VMEM)
SM = pl.BlockSpec(memory_space=pltpu.SMEM)
HB = pl.BlockSpec(memory_space=pltpu.HBM)
PARAMS = pltpu.CompilerParams(vmem_limit_bytes=VMEM_LIMIT)


def body(snapshot, cotangent, first_weight, second_weight, face_codes):
    count, channels, cells = snapshot.shape[1:]
    vertical = cells // R_CELLS
    size = lax.axis_size(AXIS)
    x, g = snapshot[0], cotangent[0]
    def call(kernel, outs, operands, name, scratch=(), specs=None):
        return pl.pallas_call(
            kernel, out_shape=outs, in_specs=specs or [VM] * len(operands),
            out_specs=jax.tree.map(lambda _: VM, outs),
            scratch_shapes=list(scratch), compiler_params=PARAMS, name=name,
        )(*operands)

    span = 9 * channels
    shape = jax.ShapeDtypeStruct
    sizes = (count, channels, cells, vertical)
    stack = shape((span, span), BF16)
    band = shape(((count + 2) * channels, count * channels), BF16)
    edges = shape((2, channels, cells), F32)
    columns = shape((count * span, cells), BF16)
    grads = shape((channels, 27 * channels), F32)
    weight = shape(first_weight.shape, BF16)
    pinned = [
        pltpu.with_memory_space_constraint(v, pltpu.HBM) for v in (face_codes, x, g, first_weight, second_weight)]
    up, codes, x, g, first_weight, second_weight = call(
        make_pack_kernel(count),
        (shape((4, channels, cells), BF16), shape((2, 8, 128), jnp.int32), shape(x.shape, BF16), shape(x.shape, BF16),
         weight, weight),
        pinned, "pack", [pltpu.SMEM((1, 2), jnp.int32), pltpu.SemaphoreType.DMA((5,))], [HB] * 5)
    up = lax.ppermute(up, AXIS, [(b, (b + 1) % size) for b in range(size)])

    ws, band_one, band_two, pre_edge, grad_edge, xs, cs, pg_inner, part_one, part_two = call(
        make_interior_kernel(*sizes),
        (stack, band, band, edges, edges, columns, columns,
         shape((count - 2, channels, cells), BF16), grads, shape((2 * span, 4 * channels), F32)),
        (x, g, first_weight, second_weight), "interior",
        [pltpu.VMEM(((count + 2) * channels, cells), BF16), pltpu.VMEM(((count + 3) * channels, cells), BF16)])
    keep, send, pg_edge = call(
        make_edge_kernel(*sizes), (grads, grads, shape((2, channels, cells), BF16)),
        (up, ws, band_one, band_two, codes, pre_edge, grad_edge, xs, cs, part_one, part_two), "edge",
        [pltpu.VMEM((3 * span, cells), BF16), pltpu.VMEM((span, cells), BF16), pltpu.VMEM((2 * span, cells), BF16)])

    def swap(value, bit):
        return lax.ppermute(value, AXIS, [(b, b ^ bit) for b in range(size)])

    total, pg_sent = lax.optimization_barrier((keep + swap(send, 1), pg_edge))
    down = lax.ppermute(pg_sent, AXIS, [(b, (b - 1) % size) for b in range(size)])
    bit = 2
    while bit < size:
        total = total + swap(total, bit)
        if bit == 4:
            input_grad = call(
                make_input_kernel(*sizes), shape((count, channels, cells), F32),
                (pg_inner, pg_edge, down, codes, g, ws), "input_grad",
                [pltpu.VMEM(((count + 2) * span, cells), BF16)])
        if bit == 8:
            total, input_grad = lax.optimization_barrier((total, input_grad))
        bit *= 2
    first, second = call(normalize_kernel, (grads, grads), (total, swap(total, 1)), "normalize")
    return (input_grad[None], first, second)


def solution(mesh):
    return jax.shard_map(
        body,
        mesh=mesh,
        in_specs=(
            P("groups", "blocks", None, None),
            P("groups", "blocks", None, None),
            P(),
            P(),
            P(("groups", "blocks"), None),
        ),
        out_specs=(P("groups", "blocks", None, None), P("groups", None), P("groups", None)),
        check_vma=False,
    )
```

```python
import jax
import jax.numpy as jnp
from jax import lax
from jax.experimental import pallas as pl
from jax.experimental.pallas import tpu as pltpu
from jax.sharding import PartitionSpec as P

R_CELLS = 32
AXIS = "blocks"
F32 = jnp.float32
BF16 = jnp.bfloat16
ORDER = (0, 1, 2, 3, 5, 6, 7, 8, 4)
VMEM_LIMIT = 24 * 1024 * 1024


def tap_masks(cells, vertical):
    lane = lax.broadcasted_iota(jnp.int32, (1, cells), 1)
    z = lane % vertical
    r = lane // vertical
    radial = cells // vertical
    masks = []
    for step_r in range(3):
        for step_z in range(3):
            ok = None
            if step_r == 0:
                ok = r >= 1
            if step_r == 2:
                ok = r < radial - 1
            if step_z == 0:
                ok = (z >= 1) if ok is None else ok & (z >= 1)
            if step_z == 2:
                ok = (z < vertical - 1) if ok is None else ok & (z < vertical - 1)
            masks.append(ok)
    return masks


def im2col(plane, store, masks, vertical):
    cells = plane.shape[1]
    wide = plane.astype(F32)
    for place, tap in enumerate(ORDER):
        offset = (tap // 3 - 1) * vertical + (tap % 3 - 1)
        if offset == 0:
            store(place, plane)
            continue
        moved = pltpu.roll(wide, (-offset) % cells, 1)
        moved = jnp.where(masks[tap], moved, 0.0)
        store(place, moved.astype(BF16))


def dot(a, b):
    return jnp.dot(a, b, preferred_element_type=F32)


def dot_nt(a, b):
    return lax.dot_general(a, b, (((1,), (1,)), ((), ())), preferred_element_type=F32)


def flip_planes(planes, code, vertical):
    lanes = 128
    parts = planes.shape[1] // lanes
    wide = planes.astype(F32)
    turn_r = code % 2 == 1
    bits = jnp.where(turn_r, lanes - vertical, 0) + jnp.where(code // 2 == 1, vertical - 1, 0)
    index = lax.broadcasted_iota(jnp.int32, (planes.shape[0], lanes), 1) ^ bits
    moved = [jnp.take_along_axis(wide[:, j * lanes:(j + 1) * lanes], index, axis=1) for j in range(parts)]
    return jnp.concatenate(
        [jnp.where(turn_r, moved[parts - 1 - j], moved[j]) for j in range(parts)], axis=1).astype(BF16)


def flipped_places(code):
    flip_r, flip_z = code % 2, code // 2
    places = []
    for tap in ORDER:
        r, z = tap // 3, tap % 3
        moved = 3 * (r + (2 - 2 * r) * flip_r) + z + (2 - 2 * z) * flip_z
        places.append(8 if tap == 4 else moved - (moved > 4).astype(jnp.int32))
    return places


def activation(pre, grad):
    sig = jax.nn.sigmoid(pre)
    hidden = (pre * sig).astype(BF16)
    return hidden, (grad * sig * (1.0 + pre * (1.0 - sig))).astype(BF16)


def filler(ref, channels, masks, vertical):
    def fill(position, plane, places=None, also=None):
        def store(place, value):
            if places is None:
                start = (9 * position + place) * channels
            else:
                start = pl.multiple_of((9 * position + places[place]) * channels, channels)
            ref[pl.ds(start, channels), :] = value
            if also is not None:
                also[place * channels:(place + 1) * channels, :] = value

        im2col(plane, store, masks, vertical)

    return fill


def make_pack_kernel(count):
    def kernel(codes_ref, x_ref, g_ref, w1_ref, w2_ref, up_ref, codes_out, x_out, g_out, w1_out, w2_out, scalars, sems):
        moves = ((x_ref, x_out), (g_ref, g_out), (codes_ref, scalars), (w1_ref, w1_out), (w2_ref, w2_out))
        copies = [pltpu.make_async_copy(*move, sems.at[index]) for index, move in enumerate(moves)]
        for copy in copies:
            copy.start()
        for index, field in enumerate((x_out, g_out)):
            copies[index].wait()
            up_ref[2 * index:2 * index + 2, :, :] = field[count - 2:count]
        for copy in copies[2:]:
            copy.wait()
        for side in range(2):
            codes_out[side, :, :] = jnp.full((8, 128), scalars[0, side], jnp.int32)

    return kernel


def make_interior_kernel(count, channels, cells, vertical):
    span = 9 * channels
    most = 8 * channels
    wide = 3 * channels
    last = count - 1

    def kernel(x_ref, g_ref, w1_ref, w2_ref,
               ws_ref, t1_ref, t2_ref, pe_ref, ge_ref, xs_ref, cs_ref, ps_ref, g1_ref, g2_ref, h_ref):
        masks = tap_masks(cells, vertical)
        for step in range(3):
            rows = slice(step * channels, (step + 1) * channels)
            base = step * span
            half = 4 * channels
            ws_ref[rows, 0:half] = w1_ref[:, base:base + half]
            ws_ref[rows, half:most] = w1_ref[:, base + half + channels:base + span]
            ws_ref[rows, most:span] = w1_ref[:, base + half:base + half + channels]
        for weight_ref, base in ((w2_ref, wide), (w1_ref, 2 * wide)):
            turned = weight_ref[...].astype(F32).T
            for step in range(3):
                for place, tap in enumerate(ORDER):
                    at = (9 * (2 - step) + 8 - tap) * channels
                    ws_ref[base + step * channels:base + (step + 1) * channels,
                           place * channels:(place + 1) * channels] = turned[at:at + channels, :].astype(BF16)
        for ref, base in ((t1_ref, 0), (t2_ref, wide)):
            ref[...] = jnp.zeros_like(ref)
            for step in range(3):
                centre = ws_ref[base + step * channels:base + (step + 1) * channels, most:span]
                for a in range(count):
                    row = (a + 2 - step) * channels
                    ref[row:row + channels, a * channels:(a + 1) * channels] = centre

        fill_x = filler(xs_ref, channels, masks, vertical)
        fill_g = filler(cs_ref, channels, masks, vertical)
        fill_p = filler(ps_ref, channels, masks, vertical)
        for a in range(count):
            fill_x(a, x_ref[a])
            fill_g(a, g_ref[a])

        h_ref[...] = jnp.zeros_like(h_ref)
        pre_all = dot(t1_ref[...], x_ref[...].reshape(count * channels, cells))
        grad_all = dot(t2_ref[...], g_ref[...].reshape(count * channels, cells))
        pre = {a: pre_all[(a + 1) * channels:(a + 2) * channels] for a in range(-1, last)}
        grad = {a: grad_all[(a + 1) * channels:(a + 2) * channels] for a in range(-1, last)}

        for a in range(count):
            columns = slice(a * span, a * span + most)
            first = max(0, a + 2 - last) * channels
            y = dot(ws_ref[first:wide, 0:most], xs_ref[columns, :])
            v = dot(ws_ref[wide + first:2 * wide, 0:most], cs_ref[columns, :])
            for step in range(3):
                target = a + 1 - step
                rows = slice(step * channels - first, (step + 1) * channels - first)
                if -1 <= target < last:
                    grad[target] = grad[target] + v[rows]
                if 0 <= target < last:
                    pre[target] = pre[target] + y[rows]
            done = a - 1
            if 1 <= done <= last - 1:
                hidden, pg = activation(pre.pop(done), grad.pop(done))
                h_ref[(done + 1) * channels:(done + 2) * channels, :] = hidden
                fill_p(done - 1, pg)
            if a == 1:
                for index, plane in ((0, -1), (1, 0)):
                    pe_ref[index, :, :] = pre.pop(plane)
                    ge_ref[index, :, :] = grad.pop(plane)
        grad_one, grad_two = None, None
        for a in range(0, count, 2):
            term = dot_nt(cs_ref[a * span:(a + 2) * span, :], h_ref[a * channels:(a + 4) * channels, :])
            grad_two = term if grad_two is None else grad_two + term
        for a in range(1, last, 2):
            term = dot_nt(ps_ref[(a - 1) * span:(a + 1) * span, :], x_ref[a - 1:a + 3].reshape(4 * channels, cells))
            grad_one = term if grad_one is None else grad_one + term
        g1_ref[...] = grad_one
        g2_ref[...] = grad_two

    return kernel


def make_edge_kernel(count, channels, cells, vertical):
    span = 9 * channels
    most = 8 * channels
    wide = 3 * channels

    def kernel(up_ref, x_ref, ws_ref, t1_ref, t2_ref, codes_ref, pe_ref, ge_ref, xs_ref, cs_ref, g1_ref, g2_ref,
               keep_ref, send_ref, pg_ref, ps_ref, xf_ref, xo_ref, cf_ref):
        is_odd = lax.axis_index(AXIS) % 2 == 1
        masks = tap_masks(cells, vertical)
        places = flipped_places(codes_ref[0, 0, 0])
        fill_x = filler(xf_ref, channels, masks, vertical)
        fill_c = filler(cf_ref, channels, masks, vertical)
        fill_p = filler(ps_ref, channels, masks, vertical)
        planes = flip_planes(up_ref[...].reshape(4 * channels, cells), codes_ref[0, 0:1, 0:1], vertical)
        fill_x(0, planes[0:channels], places)
        fill_x(1, planes[channels:2 * channels], places, xo_ref)
        for place in range(9):
            start = 2 * span + places[place] * channels
            xf_ref[pl.ds(pl.multiple_of(start, channels), channels), :] = xs_ref[place * channels:(place + 1) * channels, :]
        fill_c(0, planes[2 * channels:3 * channels], places)
        fill_c(1, planes[3 * channels:], places)

        def eight(ref, index):
            return ref[index * span:index * span + most, :]

        def rows(part, first, end):
            return ws_ref[part * wide + first * channels:part * wide + end * channels, 0:most]

        centre = slice(2 * channels, 4 * channels), slice(0, 2 * channels)
        x_mid = dot(t1_ref[centre], planes[:2 * channels])
        g_mid = dot(t2_ref[centre], planes[2 * channels:])
        pre_m = (pe_ref[0] + x_mid[:channels] + dot(rows(0, 0, 1), eight(xf_ref, 0))
                 + dot(rows(0, 1, 2), eight(xf_ref, 1)) + dot(rows(0, 2, 3), eight(xf_ref, 2)))
        pre_0 = pe_ref[1] + x_mid[channels:] + dot(rows(0, 0, 1), eight(xo_ref, 0))
        near = dot(rows(1, 0, 2), eight(cf_ref, 1))
        grad_m = ge_ref[0] + g_mid[:channels] + near[channels:] + dot(rows(1, 0, 1), eight(cf_ref, 0))
        grad_0 = ge_ref[1] + g_mid[channels:] + near[:channels]
        hid_m, pg_m = activation(pre_m, grad_m)
        hid_0, pg_0 = activation(pre_0, grad_0)
        pg_ref[0, :, :] = pg_m
        pg_ref[1, :, :] = pg_0

        zero = jnp.zeros((2 * channels, cells), BF16)
        grad_two = (g2_ref[...] + dot_nt(cf_ref[...], jnp.concatenate((zero, hid_m, hid_0), axis=0))
                    + dot_nt(cs_ref[0:2 * span, :], jnp.concatenate((hid_m, hid_0, zero), axis=0)))
        fill_p(0, pg_m, places)
        fill_p(1, pg_0)
        near = jnp.concatenate((planes[:2 * channels], x_ref[0:2].reshape(2 * channels, cells)), axis=0)
        grad_one = g1_ref[...] + dot_nt(ps_ref[...], near)

        def put(ref, pairs):
            total = pairs[0:span] + pltpu.roll(pairs[span:], 3 * channels, 1)
            moved = {}
            for place, tap in enumerate(ORDER):
                block = total[place * channels:(place + 1) * channels]
                shift = ((8 - tap) * channels) % (4 * channels)
                moved[8 - tap] = pltpu.roll(block, shift, 1) if shift else block
            lane = lax.broadcasted_iota(jnp.int32, (channels, 4 * channels), 1) // channels
            for first in range(0, 27, 4):
                tile = moved[first % 9]
                for n in range(first + 1, min(first + 4, 27)):
                    tile = jnp.where(lane >= n - first, moved[n % 9], tile)
                width = min(4, 27 - first) * channels
                ref[:, first * channels:first * channels + width] = tile[:, :width]

        put(keep_ref, jnp.where(is_odd, grad_two, grad_one))
        put(send_ref, jnp.where(is_odd, grad_one, grad_two))

    return kernel


def make_input_kernel(count, channels, cells, vertical):
    span = 9 * channels
    wide = 3 * channels
    last = count - 1

    def kernel(inner_ref, edge_ref, g_ref, ws_ref, out_ref, rest_ref, done_ref, sems):
        weights = ws_ref[2 * wide:3 * wide, :]
        total = {}
        copies = []
        for a in range(-1, last):
            columns = edge_ref[(a + 1) * span:(a + 2) * span, :] if a <= 0 else inner_ref[(a - 1) * span:a * span, :]
            if a == -1:
                total[0] = dot(weights[0:channels], columns)
                continue
            y = dot(weights, columns)
            for step in range(3):
                target = a + 1 - step
                if 0 <= target < count:
                    part = y[step * channels:(step + 1) * channels]
                    total[target] = part if target not in total else total[target] + part
            if a >= 1:
                done_ref[a - 1, :, :] = g_ref[a - 1].astype(F32) + total.pop(a - 1)
                copies.append(pltpu.make_async_copy(done_ref.at[a - 1], out_ref.at[a - 1], sems.at[a - 1]))
                copies[-1].start()
        for index in range(2):
            a = last - 1 + index
            rest_ref[index, :, :] = g_ref[a].astype(F32) + total.pop(a)
        for copy in copies:
            copy.wait()

    return kernel


def make_upper_kernel(count, channels, cells, vertical):
    span = 9 * channels
    wide = 3 * channels
    last = count - 1

    def kernel(down_ref, codes_ref, ws_ref, rest_ref, _, out_ref, ps_ref, done_ref, sem):
        fill = filler(ps_ref, channels, tap_masks(cells, vertical), vertical)
        planes = flip_planes(down_ref[...].reshape(2 * channels, cells), codes_ref[1, 0:1, 0:1], vertical)
        fill(0, planes[:channels])
        fill(1, planes[channels:], flipped_places(codes_ref[1, 0, 0]))
        weights = ws_ref[2 * wide + channels:3 * wide, :]
        y = dot(weights, ps_ref[0:span, :])
        done_ref[0, :, :] = rest_ref[0] + y[channels:]
        done_ref[1, :, :] = rest_ref[1] + y[:channels] + dot(weights[channels:], ps_ref[span:, :])
        copy = pltpu.make_async_copy(done_ref, out_ref.at[last - 1:count], sem)
        copy.start()
        copy.wait()

    return kernel


def normalize_kernel(mine_ref, other_ref, one_ref, two_ref):
    odd = lax.axis_index(AXIS) % 2

    def scaled(ref):
        v = ref[...]
        return v / jnp.sqrt(jnp.mean(v * v) + 1e-06)

    @pl.when(odd == 0)
    def _():
        one_ref[...] = scaled(mine_ref)
        two_ref[...] = scaled(other_ref)

    @pl.when(odd == 1)
    def _():
        one_ref[...] = scaled(other_ref)
        two_ref[...] = scaled(mine_ref)


VM = pl.BlockSpec(memory_space=pltpu.VMEM)
SM = pl.BlockSpec(memory_space=pltpu.SMEM)
HB = pl.BlockSpec(memory_space=pltpu.HBM)
PARAMS = pltpu.CompilerParams(vmem_limit_bytes=VMEM_LIMIT)


def body(snapshot, cotangent, first_weight, second_weight, face_codes):
    count, channels, cells = snapshot.shape[1:]
    vertical = cells // R_CELLS
    size = lax.axis_size(AXIS)
    x, g = snapshot[0], cotangent[0]
    def call(kernel, outs, operands, name, scratch=(), specs=None, out_specs=None, aliases=None):
        return pl.pallas_call(
            kernel, out_shape=outs, in_specs=specs or [VM] * len(operands),
            out_specs=out_specs or jax.tree.map(lambda _: VM, outs), input_output_aliases=aliases or {},
            scratch_shapes=list(scratch), compiler_params=PARAMS, name=name,
        )(*operands)

    span = 9 * channels
    shape = jax.ShapeDtypeStruct
    sizes = (count, channels, cells, vertical)
    stack = shape((span, span), BF16)
    band = shape(((count + 2) * channels, count * channels), BF16)
    edges = shape((2, channels, cells), F32)
    columns = shape((count * span, cells), BF16)
    grads = shape((channels, 27 * channels), F32)
    weight = shape(first_weight.shape, BF16)
    pinned = [
        pltpu.with_memory_space_constraint(v, pltpu.HBM) for v in (face_codes, x, g, first_weight, second_weight)]
    up, codes, x, g, first_weight, second_weight = call(
        make_pack_kernel(count),
        (shape((4, channels, cells), BF16), shape((2, 8, 128), jnp.int32), shape(x.shape, BF16), shape(x.shape, BF16),
         weight, weight),
        pinned, "pack", [pltpu.SMEM((1, 2), jnp.int32), pltpu.SemaphoreType.DMA((5,))], [HB] * 5)
    up = lax.ppermute(up, AXIS, [(b, (b + 1) % size) for b in range(size)])

    sums = shape((2 * span, 4 * channels), F32)
    ws, band_one, band_two, pre_edge, grad_edge, xs, cs, ps, part_one, part_two = call(
        make_interior_kernel(*sizes),
        (stack, band, band, edges, edges, columns, columns, shape(((count - 2) * span, cells), BF16), sums, sums),
        (x, g, first_weight, second_weight), "interior", [pltpu.VMEM(((count + 2) * channels, cells), BF16)])
    keep, send, pg_edge, ps_edge = call(
        make_edge_kernel(*sizes),
        (grads, grads, shape((2, channels, cells), BF16), shape((2 * span, cells), BF16)),
        (up, x, ws, band_one, band_two, codes, pre_edge, grad_edge, xs, cs, part_one, part_two), "edge",
        [pltpu.VMEM((3 * span, cells), BF16), pltpu.VMEM((span, cells), BF16), pltpu.VMEM((2 * span, cells), BF16)])

    def swap(value, bit):
        return lax.ppermute(value, AXIS, [(b, b ^ bit) for b in range(size)])

    total, pg_sent = lax.optimization_barrier((keep + swap(send, 1), pg_edge))
    down = lax.ppermute(pg_sent, AXIS, [(b, (b - 1) % size) for b in range(size)])
    most_done, rest = call(
        make_input_kernel(*sizes), (shape((count, channels, cells), F32), edges),
        (ps, ps_edge, g, ws), "input_grad",
        [pltpu.VMEM((count - 2, channels, cells), F32),
         pltpu.SemaphoreType.DMA((count - 2,))], out_specs=(HB, VM))
    bits = [1 << power for power in range(1, size.bit_length() - 1)]
    rounds = list(zip(bits[-1:] + bits[:-1], bits))
    for index, choice in enumerate(rounds):
        total = total + lax.ppermute(total, AXIS, [(b, b ^ choice[b % 2]) for b in range(size)])
        if index == len(rounds) - 2:
            total, most_done, rest = lax.optimization_barrier((total, most_done, rest))
        if index == len(rounds) - 1:
            total, down = lax.optimization_barrier((total, down))
    other = swap(total, 1)
    input_grad = call(
        make_upper_kernel(*sizes), shape((count, channels, cells), F32), (down, codes, ws, rest, most_done), "upper_planes",
        [pltpu.VMEM((2 * span, cells), BF16), pltpu.VMEM((2, channels, cells), F32), pltpu.SemaphoreType.DMA],
        [VM, VM, VM, VM, HB], out_specs=HB, aliases={4: 0})
    first, second = call(normalize_kernel, (grads, grads), (total, other), "normalize")
    return (input_grad[None], first, second)


def solution(mesh):
    return jax.shard_map(
        body,
        mesh=mesh,
        in_specs=(
            P("groups", "blocks", None, None),
            P("groups", "blocks", None, None),
            P(),
            P(),
            P(("groups", "blocks"), None),
        ),
        out_specs=(P("groups", "blocks", None, None), P("groups", None), P("groups", None)),
        check_vma=False,
    )
```

```python
import jax
import jax.numpy as jnp
from jax import lax
from jax.experimental import pallas as pl
from jax.experimental.pallas import tpu as pltpu
from jax.sharding import PartitionSpec as P

R_CELLS = 32
AXIS = "blocks"
F32 = jnp.float32
BF16 = jnp.bfloat16
ORDER = (0, 1, 2, 3, 5, 6, 7, 8, 4)
VMEM_LIMIT = 24 * 1024 * 1024


def tap_masks(cells, vertical):
    lane = lax.broadcasted_iota(jnp.int32, (1, cells), 1)
    z = lane % vertical
    r = lane // vertical
    radial = cells // vertical
    masks = []
    for step_r in range(3):
        for step_z in range(3):
            ok = None
            if step_r == 0:
                ok = r >= 1
            if step_r == 2:
                ok = r < radial - 1
            if step_z == 0:
                ok = (z >= 1) if ok is None else ok & (z >= 1)
            if step_z == 2:
                ok = (z < vertical - 1) if ok is None else ok & (z < vertical - 1)
            masks.append(ok)
    return masks


def im2col(plane, store, masks, vertical):
    cells = plane.shape[1]
    wide = plane.astype(F32)
    for place, tap in enumerate(ORDER):
        offset = (tap // 3 - 1) * vertical + (tap % 3 - 1)
        if offset == 0:
            store(place, plane)
            continue
        moved = pltpu.roll(wide, (-offset) % cells, 1)
        moved = jnp.where(masks[tap], moved, 0.0)
        store(place, moved.astype(BF16))


def dot(a, b):
    return jnp.dot(a, b, preferred_element_type=F32)


def dot_nt(a, b):
    return lax.dot_general(a, b, (((1,), (1,)), ((), ())), preferred_element_type=F32)


def flip_planes(planes, code, vertical):
    lanes = 128
    parts = planes.shape[1] // lanes
    wide = planes.astype(F32)
    turn_r = code % 2 == 1
    bits = jnp.where(turn_r, lanes - vertical, 0) + jnp.where(code // 2 == 1, vertical - 1, 0)
    index = lax.broadcasted_iota(jnp.int32, (planes.shape[0], lanes), 1) ^ bits
    moved = [jnp.take_along_axis(wide[:, j * lanes:(j + 1) * lanes], index, axis=1) for j in range(parts)]
    return jnp.concatenate(
        [jnp.where(turn_r, moved[parts - 1 - j], moved[j]) for j in range(parts)], axis=1).astype(BF16)


def flipped_places(code):
    flip_r, flip_z = code % 2, code // 2
    places = []
    for tap in ORDER:
        r, z = tap // 3, tap % 3
        moved = 3 * (r + (2 - 2 * r) * flip_r) + z + (2 - 2 * z) * flip_z
        places.append(8 if tap == 4 else moved - (moved > 4).astype(jnp.int32))
    return places


def activation(pre, grad):
    sig = jax.nn.sigmoid(pre)
    hidden = (pre * sig).astype(BF16)
    return hidden, (grad * sig * (1.0 + pre * (1.0 - sig))).astype(BF16)


def filler(ref, channels, masks, vertical):
    def fill(position, plane, places=None, also=None):
        def store(place, value):
            if places is None:
                start = (9 * position + place) * channels
            else:
                start = pl.multiple_of((9 * position + places[place]) * channels, channels)
            ref[pl.ds(start, channels), :] = value
            if also is not None:
                also[place * channels:(place + 1) * channels, :] = value

        im2col(plane, store, masks, vertical)

    return fill


def make_pack_kernel(count):
    def kernel(codes_ref, x_ref, g_ref, w1_ref, w2_ref, up_ref, codes_out, x_out, g_out, w1_out, w2_out, scalars, sems):
        moves = ((x_ref, x_out), (g_ref, g_out), (codes_ref, scalars), (w1_ref, w1_out), (w2_ref, w2_out))
        copies = [pltpu.make_async_copy(*move, sems.at[index]) for index, move in enumerate(moves)]
        for copy in copies:
            copy.start()
        for index, field in enumerate((x_out, g_out)):
            copies[index].wait()
            up_ref[2 * index:2 * index + 2, :, :] = field[count - 2:count]
        for copy in copies[2:]:
            copy.wait()
        for side in range(2):
            codes_out[side, :, :] = jnp.full((8, 128), scalars[0, side], jnp.int32)

    return kernel


def make_interior_kernel(count, channels, cells, vertical):
    span = 9 * channels
    most = 8 * channels
    wide = 3 * channels
    last = count - 1

    def kernel(x_ref, g_ref, w1_ref, w2_ref,
               ws_ref, t1_ref, t2_ref, pe_ref, ge_ref, xs_ref, cs_ref, ps_ref, g1_ref, g2_ref, h_ref):
        masks = tap_masks(cells, vertical)
        for step in range(3):
            rows = slice(step * channels, (step + 1) * channels)
            base = step * span
            half = 4 * channels
            ws_ref[rows, 0:half] = w1_ref[:, base:base + half]
            ws_ref[rows, half:most] = w1_ref[:, base + half + channels:base + span]
            ws_ref[rows, most:span] = w1_ref[:, base + half:base + half + channels]
        for weight_ref, base in ((w2_ref, wide), (w1_ref, 2 * wide)):
            turned = weight_ref[...].astype(F32).T
            for step in range(3):
                for place, tap in enumerate(ORDER):
                    at = (9 * (2 - step) + 8 - tap) * channels
                    ws_ref[base + step * channels:base + (step + 1) * channels,
                           place * channels:(place + 1) * channels] = turned[at:at + channels, :].astype(BF16)
        for ref, base in ((t1_ref, 0), (t2_ref, wide)):
            ref[...] = jnp.zeros_like(ref)
            for step in range(3):
                centre = ws_ref[base + step * channels:base + (step + 1) * channels, most:span]
                for a in range(count):
                    row = (a + 2 - step) * channels
                    ref[row:row + channels, a * channels:(a + 1) * channels] = centre

        fill_x = filler(xs_ref, channels, masks, vertical)
        fill_g = filler(cs_ref, channels, masks, vertical)
        fill_p = filler(ps_ref, channels, masks, vertical)
        for a in range(count):
            fill_x(a, x_ref[a])
            fill_g(a, g_ref[a])

        h_ref[...] = jnp.zeros_like(h_ref)
        pre_all = dot(t1_ref[...], x_ref[...].reshape(count * channels, cells))
        grad_all = dot(t2_ref[...], g_ref[...].reshape(count * channels, cells))
        pre = {a: pre_all[(a + 1) * channels:(a + 2) * channels] for a in range(-1, last)}
        grad = {a: grad_all[(a + 1) * channels:(a + 2) * channels] for a in range(-1, last)}

        for a in range(count):
            columns = slice(a * span, a * span + most)
            first = max(0, a + 2 - last) * channels
            y = dot(ws_ref[first:wide, 0:most], xs_ref[columns, :])
            v = dot(ws_ref[wide + first:2 * wide, 0:most], cs_ref[columns, :])
            for step in range(3):
                target = a + 1 - step
                rows = slice(step * channels - first, (step + 1) * channels - first)
                if -1 <= target < last:
                    grad[target] = grad[target] + v[rows]
                if 0 <= target < last:
                    pre[target] = pre[target] + y[rows]
            done = a - 1
            if 1 <= done <= last - 1:
                hidden, pg = activation(pre.pop(done), grad.pop(done))
                h_ref[(done + 1) * channels:(done + 2) * channels, :] = hidden
                fill_p(done - 1, pg)
            if a == 1:
                for index, plane in ((0, -1), (1, 0)):
                    pe_ref[index, :, :] = pre.pop(plane)
                    ge_ref[index, :, :] = grad.pop(plane)
        grad_one, grad_two = None, None
        for a in range(0, count, 2):
            term = dot_nt(cs_ref[a * span:(a + 2) * span, :], h_ref[a * channels:(a + 4) * channels, :])
            grad_two = term if grad_two is None else grad_two + term
        for a in range(1, last, 2):
            term = dot_nt(ps_ref[(a - 1) * span:(a + 1) * span, :], x_ref[a - 1:a + 3].reshape(4 * channels, cells))
            grad_one = term if grad_one is None else grad_one + term
        g1_ref[...] = grad_one
        g2_ref[...] = grad_two

    return kernel


def put_blocks(ref, pairs, channels):
    span = 9 * channels
    total = pairs[0:span] + pltpu.roll(pairs[span:], 3 * channels, 1)
    moved = {}
    for place, tap in enumerate(ORDER):
        block = total[place * channels:(place + 1) * channels]
        shift = ((8 - tap) * channels) % (4 * channels)
        moved[8 - tap] = pltpu.roll(block, shift, 1) if shift else block
    lane = lax.broadcasted_iota(jnp.int32, (channels, 4 * channels), 1) // channels
    for first in range(0, 27, 4):
        tile = moved[first % 9]
        for n in range(first + 1, min(first + 4, 27)):
            tile = jnp.where(lane >= n - first, moved[n % 9], tile)
        width = min(4, 27 - first) * channels
        ref[:, first * channels:first * channels + width] = tile[:, :width]


def first_terms(sum_ref, ps_ref, low_ref, x_ref, channels):
    near = jnp.concatenate((low_ref[...], x_ref[0:2].reshape(low_ref.shape)), axis=0)
    return sum_ref[...] + dot_nt(ps_ref[...], near)


def second_terms(sum_ref, cf_ref, cs_ref, hidden, channels):
    zero = jnp.zeros_like(hidden)
    return (sum_ref[...] + dot_nt(cf_ref[...], jnp.concatenate((zero, hidden), axis=0))
            + dot_nt(cs_ref[0:18 * channels, :], jnp.concatenate((hidden, zero), axis=0)))


def make_keep_kernel(channels, cells, vertical):
    def kernel(x_ref, codes_ref, cs_ref, g1_ref, g2_ref, pg_ref, h_ref, low_ref, cf_ref, keep_ref, ps_ref):
        is_odd = lax.axis_index(AXIS) % 2 == 1
        fill_p = filler(ps_ref, channels, tap_masks(cells, vertical), vertical)
        fill_p(0, pg_ref[0], flipped_places(codes_ref[0, 0, 0]))
        fill_p(1, pg_ref[1])

        @pl.when(jnp.logical_not(is_odd))
        def _():
            put_blocks(keep_ref, first_terms(g1_ref, ps_ref, low_ref, x_ref, channels), channels)

        @pl.when(is_odd)
        def _():
            put_blocks(keep_ref, second_terms(g2_ref, cf_ref, cs_ref, h_ref[...], channels), channels)

    return kernel


def make_edge_kernel(count, channels, cells, vertical):
    span = 9 * channels
    most = 8 * channels
    wide = 3 * channels

    def kernel(up_ref, x_ref, ws_ref, t1_ref, t2_ref, codes_ref, pe_ref, ge_ref, xs_ref, cs_ref, g1_ref, g2_ref,
               send_ref, pg_ref, h_ref, low_ref, cf_ref, xf_ref, xo_ref, ps_ref):
        is_odd = lax.axis_index(AXIS) % 2 == 1
        masks = tap_masks(cells, vertical)
        places = flipped_places(codes_ref[0, 0, 0])
        fill_x = filler(xf_ref, channels, masks, vertical)
        fill_c = filler(cf_ref, channels, masks, vertical)
        planes = flip_planes(up_ref[...].reshape(4 * channels, cells), codes_ref[0, 0:1, 0:1], vertical)
        fill_x(0, planes[0:channels], places)
        fill_x(1, planes[channels:2 * channels], places, xo_ref)
        for place in range(9):
            start = 2 * span + places[place] * channels
            xf_ref[pl.ds(pl.multiple_of(start, channels), channels), :] = xs_ref[place * channels:(place + 1) * channels, :]
        fill_c(0, planes[2 * channels:3 * channels], places)
        fill_c(1, planes[3 * channels:], places)

        def eight(ref, index):
            return ref[index * span:index * span + most, :]

        def rows(part, first, end):
            return ws_ref[part * wide + first * channels:part * wide + end * channels, 0:most]

        centre = slice(2 * channels, 4 * channels), slice(0, 2 * channels)
        x_mid = dot(t1_ref[centre], planes[:2 * channels])
        g_mid = dot(t2_ref[centre], planes[2 * channels:])
        pre_m = (pe_ref[0] + x_mid[:channels] + dot(rows(0, 0, 1), eight(xf_ref, 0))
                 + dot(rows(0, 1, 2), eight(xf_ref, 1)) + dot(rows(0, 2, 3), eight(xf_ref, 2)))
        pre_0 = pe_ref[1] + x_mid[channels:] + dot(rows(0, 0, 1), eight(xo_ref, 0))
        near = dot(rows(1, 0, 2), eight(cf_ref, 1))
        grad_m = ge_ref[0] + g_mid[:channels] + near[channels:] + dot(rows(1, 0, 1), eight(cf_ref, 0))
        grad_0 = ge_ref[1] + g_mid[channels:] + near[:channels]
        hid_m, pg_m = activation(pre_m, grad_m)
        hid_0, pg_0 = activation(pre_0, grad_0)
        pg_ref[0, :, :] = pg_m
        pg_ref[1, :, :] = pg_0

        h_ref[0:channels, :] = hid_m
        h_ref[channels:, :] = hid_0
        low_ref[...] = planes[:2 * channels]

        @pl.when(jnp.logical_not(is_odd))
        def _():
            put_blocks(send_ref, second_terms(g2_ref, cf_ref, cs_ref, h_ref[...], channels), channels)

        @pl.when(is_odd)
        def _():
            fill_p = filler(ps_ref, channels, masks, vertical)
            fill_p(0, pg_m, places)
            fill_p(1, pg_0)
            put_blocks(send_ref, first_terms(g1_ref, ps_ref, low_ref, x_ref, channels), channels)

    return kernel


def make_input_kernel(count, channels, cells, vertical):
    span = 9 * channels
    wide = 3 * channels
    last = count - 1

    def kernel(inner_ref, edge_ref, g_ref, ws_ref, out_ref, rest_ref, done_ref, sems):
        weights = ws_ref[2 * wide:3 * wide, :]
        total = {}
        copies = []
        for a in range(-1, last):
            columns = edge_ref[(a + 1) * span:(a + 2) * span, :] if a <= 0 else inner_ref[(a - 1) * span:a * span, :]
            if a == -1:
                total[0] = dot(weights[0:channels], columns)
                continue
            y = dot(weights, columns)
            for step in range(3):
                target = a + 1 - step
                if 0 <= target < count:
                    part = y[step * channels:(step + 1) * channels]
                    total[target] = part if target not in total else total[target] + part
            if a >= 1:
                done_ref[a - 1, :, :] = g_ref[a - 1].astype(F32) + total.pop(a - 1)
                copies.append(pltpu.make_async_copy(done_ref.at[a - 1], out_ref.at[a - 1], sems.at[a - 1]))
                copies[-1].start()
        for index in range(2):
            a = last - 1 + index
            rest_ref[index, :, :] = g_ref[a].astype(F32) + total.pop(a)
        for copy in copies:
            copy.wait()

    return kernel


def write_update(scaled_ref, sum_ref, one_ref, two_ref, sems, swapped, finish):
    own = lax.axis_index(AXIS) % 2
    if not finish:
        v = sum_ref[...]
        scaled_ref[...] = v / jnp.sqrt(jnp.mean(v * v) + 1e-06)
    for index, target in enumerate((one_ref, two_ref)):

        @pl.when(own == (index ^ swapped))
        def _(index=index, target=target):
            copy = pltpu.make_async_copy(scaled_ref, target, sems.at[index])
            if finish:
                copy.wait()
            else:
                copy.start()


def make_upper_kernel(count, channels, cells, vertical):
    span = 9 * channels
    wide = 3 * channels
    last = count - 1

    def kernel(down_ref, codes_ref, ws_ref, rest_ref, mine_ref, _, out_ref, one_ref, two_ref,
               ps_ref, done_ref, scaled_ref, sem, sems):
        write_update(scaled_ref, mine_ref, one_ref, two_ref, sems, 0, False)
        fill = filler(ps_ref, channels, tap_masks(cells, vertical), vertical)
        planes = flip_planes(down_ref[...].reshape(2 * channels, cells), codes_ref[1, 0:1, 0:1], vertical)
        fill(0, planes[:channels])
        fill(1, planes[channels:], flipped_places(codes_ref[1, 0, 0]))
        weights = ws_ref[2 * wide + channels:3 * wide, :]
        y = dot(weights, ps_ref[0:span, :])
        done_ref[0, :, :] = rest_ref[0] + y[channels:]
        done_ref[1, :, :] = rest_ref[1] + y[:channels] + dot(weights[channels:], ps_ref[span:, :])
        copy = pltpu.make_async_copy(done_ref, out_ref.at[last - 1:count], sem)
        copy.start()
        write_update(scaled_ref, mine_ref, one_ref, two_ref, sems, 0, True)
        copy.wait()

    return kernel


def normalize_kernel(other_ref, _, __, one_ref, two_ref, scaled_ref, sems):
    write_update(scaled_ref, other_ref, one_ref, two_ref, sems, 1, False)
    write_update(scaled_ref, other_ref, one_ref, two_ref, sems, 1, True)


VM = pl.BlockSpec(memory_space=pltpu.VMEM)
SM = pl.BlockSpec(memory_space=pltpu.SMEM)
HB = pl.BlockSpec(memory_space=pltpu.HBM)
PARAMS = pltpu.CompilerParams(vmem_limit_bytes=VMEM_LIMIT)


def body(snapshot, cotangent, first_weight, second_weight, face_codes):
    count, channels, cells = snapshot.shape[1:]
    vertical = cells // R_CELLS
    size = lax.axis_size(AXIS)
    x, g = snapshot[0], cotangent[0]
    def call(kernel, outs, operands, name, scratch=(), specs=None, out_specs=None, aliases=None):
        return pl.pallas_call(
            kernel, out_shape=outs, in_specs=specs or [VM] * len(operands),
            out_specs=out_specs or jax.tree.map(lambda _: VM, outs), input_output_aliases=aliases or {},
            scratch_shapes=list(scratch), compiler_params=PARAMS, name=name,
        )(*operands)

    span = 9 * channels
    shape = jax.ShapeDtypeStruct
    sizes = (count, channels, cells, vertical)
    stack = shape((span, span), BF16)
    band = shape(((count + 2) * channels, count * channels), BF16)
    edges = shape((2, channels, cells), F32)
    columns = shape((count * span, cells), BF16)
    grads = shape((channels, 27 * channels), F32)
    weight = shape(first_weight.shape, BF16)
    pinned = [
        pltpu.with_memory_space_constraint(v, pltpu.HBM) for v in (face_codes, x, g, first_weight, second_weight)]
    up, codes, x, g, first_weight, second_weight = call(
        make_pack_kernel(count),
        (shape((4, channels, cells), BF16), shape((2, 8, 128), jnp.int32), shape(x.shape, BF16), shape(x.shape, BF16),
         weight, weight),
        pinned, "pack", [pltpu.SMEM((1, 2), jnp.int32), pltpu.SemaphoreType.DMA((5,))], [HB] * 5)
    up = lax.ppermute(up, AXIS, [(b, (b + 1) % size) for b in range(size)])

    sums = shape((2 * span, 4 * channels), F32)
    ws, band_one, band_two, pre_edge, grad_edge, xs, cs, ps, part_one, part_two = call(
        make_interior_kernel(*sizes),
        (stack, band, band, edges, edges, columns, columns, shape(((count - 2) * span, cells), BF16), sums, sums),
        (x, g, first_weight, second_weight), "interior", [pltpu.VMEM(((count + 2) * channels, cells), BF16)])
    two = shape((2 * channels, cells), BF16)
    send, pg_edge, h_edge, low, cf = call(
        make_edge_kernel(*sizes),
        (grads, shape((2, channels, cells), BF16), two, two, shape((2 * span, cells), BF16)),
        (up, x, ws, band_one, band_two, codes, pre_edge, grad_edge, xs, cs, part_one, part_two), "edge",
        [pltpu.VMEM((3 * span, cells), BF16), pltpu.VMEM((span, cells), BF16), pltpu.VMEM((2 * span, cells), BF16)])
    keep, ps_edge = call(
        make_keep_kernel(channels, cells, vertical), (grads, shape((2 * span, cells), BF16)),
        (x, codes, cs, part_one, part_two, pg_edge, h_edge, low, cf), "keep")

    def swap(value, bit):
        return lax.ppermute(value, AXIS, [(b, b ^ bit) for b in range(size)])

    total, pg_sent = lax.optimization_barrier((keep + swap(send, 1), pg_edge))
    down = lax.ppermute(pg_sent, AXIS, [(b, (b - 1) % size) for b in range(size)])
    most_done, rest = call(
        make_input_kernel(*sizes), (shape((count, channels, cells), F32), edges),
        (ps, ps_edge, g, ws), "input_grad",
        [pltpu.VMEM((count - 2, channels, cells), F32),
         pltpu.SemaphoreType.DMA((count - 2,))], out_specs=(HB, VM))
    bits = [1 << power for power in range(1, size.bit_length() - 1)]
    rounds = list(zip(bits[-1:] + bits[:-1], bits))
    for index, choice in enumerate(rounds):
        total = total + lax.ppermute(total, AXIS, [(b, b ^ choice[b % 2]) for b in range(size)])
        if index == len(rounds) - 2:
            total, most_done, rest = lax.optimization_barrier((total, most_done, rest))
        if index == len(rounds) - 1:
            total, down = lax.optimization_barrier((total, down))
    other = swap(total, 1)
    input_grad, first, second = call(
        make_upper_kernel(*sizes), (shape((count, channels, cells), F32), grads, grads),
        (down, codes, ws, rest, total, most_done), "upper_planes",
        [pltpu.VMEM((2 * span, cells), BF16), pltpu.VMEM((2, channels, cells), F32), pltpu.VMEM(grads.shape, F32),
         pltpu.SemaphoreType.DMA, pltpu.SemaphoreType.DMA((2,))],
        [VM, VM, VM, VM, VM, HB], out_specs=(HB, HB, HB), aliases={5: 0})
    first, second = call(
        normalize_kernel, (grads, grads), (other, first, second), "normalize",
        [pltpu.VMEM(grads.shape, F32), pltpu.SemaphoreType.DMA((2,))], [VM, HB, HB], out_specs=(HB, HB), aliases={1: 0, 2: 1})
    return (input_grad[None], first, second)


def solution(mesh):
    return jax.shard_map(
        body,
        mesh=mesh,
        in_specs=(
            P("groups", "blocks", None, None),
            P("groups", "blocks", None, None),
            P(),
            P(),
            P(("groups", "blocks"), None),
        ),
        out_specs=(P("groups", "blocks", None, None), P("groups", None), P("groups", None)),
        check_vma=False,
    )
```

```python
import jax
import jax.numpy as jnp
from jax import lax
from jax.experimental import pallas as pl
from jax.experimental.pallas import tpu as pltpu
from jax.sharding import PartitionSpec as P

R_CELLS = 32
AXIS = "blocks"
F32 = jnp.float32
BF16 = jnp.bfloat16
ORDER = (0, 1, 2, 3, 5, 6, 7, 8, 4)
VMEM_LIMIT = 24 * 1024 * 1024


def tap_masks(cells, vertical):
    lane = lax.broadcasted_iota(jnp.int32, (1, cells), 1)
    z = lane % vertical
    r = lane // vertical
    radial = cells // vertical
    masks = []
    for step_r in range(3):
        for step_z in range(3):
            ok = None
            if step_r == 0:
                ok = r >= 1
            if step_r == 2:
                ok = r < radial - 1
            if step_z == 0:
                ok = (z >= 1) if ok is None else ok & (z >= 1)
            if step_z == 2:
                ok = (z < vertical - 1) if ok is None else ok & (z < vertical - 1)
            masks.append(ok)
    return masks


def im2col(plane, store, masks, vertical):
    cells = plane.shape[1]
    wide = plane.astype(F32)
    for place, tap in enumerate(ORDER):
        offset = (tap // 3 - 1) * vertical + (tap % 3 - 1)
        if offset == 0:
            store(place, plane)
            continue
        moved = pltpu.roll(wide, (-offset) % cells, 1)
        moved = jnp.where(masks[tap], moved, 0.0)
        store(place, moved.astype(BF16))


def dot(a, b):
    return jnp.dot(a, b, preferred_element_type=F32)


def dot_nt(a, b):
    return lax.dot_general(a, b, (((1,), (1,)), ((), ())), preferred_element_type=F32)


def flip_planes(planes, code, vertical):
    lanes = 128
    parts = planes.shape[1] // lanes
    wide = planes.astype(F32)
    turn_r = code % 2 == 1
    bits = jnp.where(turn_r, lanes - vertical, 0) + jnp.where(code // 2 == 1, vertical - 1, 0)
    index = lax.broadcasted_iota(jnp.int32, (planes.shape[0], lanes), 1) ^ bits
    moved = [jnp.take_along_axis(wide[:, j * lanes:(j + 1) * lanes], index, axis=1) for j in range(parts)]
    return jnp.concatenate(
        [jnp.where(turn_r, moved[parts - 1 - j], moved[j]) for j in range(parts)], axis=1).astype(BF16)


def flipped_places(code):
    flip_r, flip_z = code % 2, code // 2
    places = []
    for tap in ORDER:
        r, z = tap // 3, tap % 3
        moved = 3 * (r + (2 - 2 * r) * flip_r) + z + (2 - 2 * z) * flip_z
        places.append(8 if tap == 4 else moved - (moved > 4).astype(jnp.int32))
    return places


def activation(pre, grad):
    sig = jax.nn.sigmoid(pre)
    hidden = (pre * sig).astype(BF16)
    return hidden, (grad * sig * (1.0 + pre * (1.0 - sig))).astype(BF16)


def filler(ref, channels, masks, vertical):
    def fill(position, plane, places=None, also=None):
        def store(place, value):
            if places is None:
                start = (9 * position + place) * channels
            else:
                start = pl.multiple_of((9 * position + places[place]) * channels, channels)
            ref[pl.ds(start, channels), :] = value
            if also is not None:
                also[place * channels:(place + 1) * channels, :] = value

        im2col(plane, store, masks, vertical)

    return fill


def make_pack_kernel(count):
    def kernel(codes_ref, x_ref, g_ref, w1_ref, w2_ref, up_ref, codes_out, x_out, g_out, w1_out, w2_out, scalars, sems):
        moves = ((x_ref, x_out), (g_ref, g_out), (codes_ref, scalars), (w1_ref, w1_out), (w2_ref, w2_out))
        copies = [pltpu.make_async_copy(*move, sems.at[index]) for index, move in enumerate(moves)]
        for copy in copies:
            copy.start()
        for index, field in enumerate((x_out, g_out)):
            copies[index].wait()
            up_ref[2 * index:2 * index + 2, :, :] = field[count - 2:count]
        for copy in copies[2:]:
            copy.wait()
        for side in range(2):
            codes_out[side, :, :] = jnp.full((8, 128), scalars[0, side], jnp.int32)

    return kernel


def stack_adjoint(weight_ref, out_ref, base, channels):
    turned = weight_ref[...].astype(F32).T
    for step in range(3):
        for place, tap in enumerate(ORDER):
            at = (9 * (2 - step) + 8 - tap) * channels
            out_ref[base + step * channels:base + (step + 1) * channels,
                    place * channels:(place + 1) * channels] = turned[at:at + channels, :].astype(BF16)


def make_interior_kernel(count, channels, cells, vertical):
    span = 9 * channels
    most = 8 * channels
    wide = 3 * channels
    last = count - 1

    def kernel(x_ref, g_ref, w1_ref, w2_ref,
               ws_ref, t1_ref, t2_ref, pe_ref, ge_ref, xs_ref, cs_ref, ps_ref, g1_ref, g2_ref, h_ref):
        masks = tap_masks(cells, vertical)
        for step in range(3):
            rows = slice(step * channels, (step + 1) * channels)
            base = step * span
            half = 4 * channels
            ws_ref[rows, 0:half] = w1_ref[:, base:base + half]
            ws_ref[rows, half:most] = w1_ref[:, base + half + channels:base + span]
            ws_ref[rows, most:span] = w1_ref[:, base + half:base + half + channels]
        stack_adjoint(w2_ref, ws_ref, wide, channels)
        for ref, base in ((t1_ref, 0), (t2_ref, wide)):
            ref[...] = jnp.zeros_like(ref)
            for step in range(3):
                centre = ws_ref[base + step * channels:base + (step + 1) * channels, most:span]
                for a in range(count):
                    row = (a + 2 - step) * channels
                    ref[row:row + channels, a * channels:(a + 1) * channels] = centre

        fill_x = filler(xs_ref, channels, masks, vertical)
        fill_g = filler(cs_ref, channels, masks, vertical)
        fill_p = filler(ps_ref, channels, masks, vertical)
        for a in range(count):
            fill_x(a, x_ref[a])
            fill_g(a, g_ref[a])

        h_ref[...] = jnp.zeros_like(h_ref)
        pre_all = dot(t1_ref[...], x_ref[...].reshape(count * channels, cells))
        grad_all = dot(t2_ref[...], g_ref[...].reshape(count * channels, cells))
        pre = {a: pre_all[(a + 1) * channels:(a + 2) * channels] for a in range(-1, last)}
        grad = {a: grad_all[(a + 1) * channels:(a + 2) * channels] for a in range(-1, last)}

        for a in range(count):
            columns = slice(a * span, a * span + most)
            first = max(0, a + 2 - last) * channels
            y = dot(ws_ref[first:wide, 0:most], xs_ref[columns, :])
            v = dot(ws_ref[wide + first:2 * wide, 0:most], cs_ref[columns, :])
            for step in range(3):
                target = a + 1 - step
                rows = slice(step * channels - first, (step + 1) * channels - first)
                if -1 <= target < last:
                    grad[target] = grad[target] + v[rows]
                if 0 <= target < last:
                    pre[target] = pre[target] + y[rows]
            done = a - 1
            if 1 <= done <= last - 1:
                hidden, pg = activation(pre.pop(done), grad.pop(done))
                h_ref[(done + 1) * channels:(done + 2) * channels, :] = hidden
                fill_p(done - 1, pg)
            if a == 1:
                for index, plane in ((0, -1), (1, 0)):
                    pe_ref[index, :, :] = pre.pop(plane)
                    ge_ref[index, :, :] = grad.pop(plane)
        grad_one, grad_two = None, None
        for a in range(0, count, 2):
            term = dot_nt(cs_ref[a * span:(a + 2) * span, :], h_ref[a * channels:(a + 4) * channels, :])
            grad_two = term if grad_two is None else grad_two + term
        for a in range(1, last, 2):
            term = dot_nt(ps_ref[(a - 1) * span:(a + 1) * span, :], x_ref[a - 1:a + 3].reshape(4 * channels, cells))
            grad_one = term if grad_one is None else grad_one + term
        g1_ref[...] = grad_one
        g2_ref[...] = grad_two

    return kernel


def put_blocks(ref, pairs, channels):
    span = 9 * channels
    total = pairs[0:span] + pltpu.roll(pairs[span:], 3 * channels, 1)
    moved = {}
    for place, tap in enumerate(ORDER):
        block = total[place * channels:(place + 1) * channels]
        shift = ((8 - tap) * channels) % (4 * channels)
        moved[8 - tap] = pltpu.roll(block, shift, 1) if shift else block
    lane = lax.broadcasted_iota(jnp.int32, (channels, 4 * channels), 1) // channels
    for first in range(0, 27, 4):
        tile = moved[first % 9]
        for n in range(first + 1, min(first + 4, 27)):
            tile = jnp.where(lane >= n - first, moved[n % 9], tile)
        width = min(4, 27 - first) * channels
        ref[:, first * channels:first * channels + width] = tile[:, :width]


def first_terms(sum_ref, ps_ref, low_ref, x_ref, channels):
    near = jnp.concatenate((low_ref[...], x_ref[0:2].reshape(low_ref.shape)), axis=0)
    return sum_ref[...] + dot_nt(ps_ref[...], near)


def second_terms(sum_ref, cf_ref, cs_ref, hidden, channels):
    zero = jnp.zeros_like(hidden)
    return (sum_ref[...] + dot_nt(cf_ref[...], jnp.concatenate((zero, hidden), axis=0))
            + dot_nt(cs_ref[0:18 * channels, :], jnp.concatenate((hidden, zero), axis=0)))


def make_keep_kernel(channels, cells, vertical):
    def kernel(x_ref, codes_ref, cs_ref, g1_ref, g2_ref, pg_ref, h_ref, low_ref, cf_ref, keep_ref, ps_ref):
        is_odd = lax.axis_index(AXIS) % 2 == 1
        fill_p = filler(ps_ref, channels, tap_masks(cells, vertical), vertical)
        fill_p(0, pg_ref[0], flipped_places(codes_ref[0, 0, 0]))
        fill_p(1, pg_ref[1])

        @pl.when(jnp.logical_not(is_odd))
        def _():
            put_blocks(keep_ref, first_terms(g1_ref, ps_ref, low_ref, x_ref, channels), channels)

        @pl.when(is_odd)
        def _():
            put_blocks(keep_ref, second_terms(g2_ref, cf_ref, cs_ref, h_ref[...], channels), channels)

    return kernel


def make_edge_kernel(count, channels, cells, vertical):
    span = 9 * channels
    most = 8 * channels
    wide = 3 * channels

    def kernel(up_ref, x_ref, ws_ref, t1_ref, t2_ref, codes_ref, pe_ref, ge_ref, xs_ref, cs_ref, g1_ref, g2_ref,
               send_ref, pg_ref, h_ref, low_ref, cf_ref, xf_ref, xo_ref, ps_ref):
        is_odd = lax.axis_index(AXIS) % 2 == 1
        masks = tap_masks(cells, vertical)
        places = flipped_places(codes_ref[0, 0, 0])
        fill_x = filler(xf_ref, channels, masks, vertical)
        fill_c = filler(cf_ref, channels, masks, vertical)
        planes = flip_planes(up_ref[...].reshape(4 * channels, cells), codes_ref[0, 0:1, 0:1], vertical)
        fill_x(0, planes[0:channels], places)
        fill_x(1, planes[channels:2 * channels], places, xo_ref)
        for place in range(9):
            start = 2 * span + places[place] * channels
            xf_ref[pl.ds(pl.multiple_of(start, channels), channels), :] = xs_ref[place * channels:(place + 1) * channels, :]
        fill_c(0, planes[2 * channels:3 * channels], places)
        fill_c(1, planes[3 * channels:], places)

        def eight(ref, index):
            return ref[index * span:index * span + most, :]

        def rows(part, first, end):
            return ws_ref[part * wide + first * channels:part * wide + end * channels, 0:most]

        centre = slice(2 * channels, 4 * channels), slice(0, 2 * channels)
        x_mid = dot(t1_ref[centre], planes[:2 * channels])
        g_mid = dot(t2_ref[centre], planes[2 * channels:])
        pre_m = (pe_ref[0] + x_mid[:channels] + dot(rows(0, 0, 1), eight(xf_ref, 0))
                 + dot(rows(0, 1, 2), eight(xf_ref, 1)) + dot(rows(0, 2, 3), eight(xf_ref, 2)))
        pre_0 = pe_ref[1] + x_mid[channels:] + dot(rows(0, 0, 1), eight(xo_ref, 0))
        near = dot(rows(1, 0, 2), eight(cf_ref, 1))
        grad_m = ge_ref[0] + g_mid[:channels] + near[channels:] + dot(rows(1, 0, 1), eight(cf_ref, 0))
        grad_0 = ge_ref[1] + g_mid[channels:] + near[:channels]
        hid_m, pg_m = activation(pre_m, grad_m)
        hid_0, pg_0 = activation(pre_0, grad_0)
        pg_ref[0, :, :] = pg_m
        pg_ref[1, :, :] = pg_0

        h_ref[0:channels, :] = hid_m
        h_ref[channels:, :] = hid_0
        low_ref[...] = planes[:2 * channels]

        @pl.when(jnp.logical_not(is_odd))
        def _():
            put_blocks(send_ref, second_terms(g2_ref, cf_ref, cs_ref, h_ref[...], channels), channels)

        @pl.when(is_odd)
        def _():
            fill_p = filler(ps_ref, channels, masks, vertical)
            fill_p(0, pg_m, places)
            fill_p(1, pg_0)
            put_blocks(send_ref, first_terms(g1_ref, ps_ref, low_ref, x_ref, channels), channels)

    return kernel


def make_input_kernel(count, channels, cells, vertical):
    span = 9 * channels
    wide = 3 * channels
    last = count - 1

    def kernel(inner_ref, edge_ref, g_ref, w1_ref, out_ref, rest_ref, ws_ref, done_ref, sems):
        stack_adjoint(w1_ref, ws_ref, 0, channels)
        weights = ws_ref[...]
        total = {}
        copies = []
        for a in range(-1, last):
            columns = edge_ref[(a + 1) * span:(a + 2) * span, :] if a <= 0 else inner_ref[(a - 1) * span:a * span, :]
            if a == -1:
                total[0] = dot(weights[0:channels], columns)
                continue
            y = dot(weights, columns)
            for step in range(3):
                target = a + 1 - step
                if 0 <= target < count:
                    part = y[step * channels:(step + 1) * channels]
                    total[target] = part if target not in total else total[target] + part
            if a >= 1:
                done_ref[a - 1, :, :] = g_ref[a - 1].astype(F32) + total.pop(a - 1)
                copies.append(pltpu.make_async_copy(done_ref.at[a - 1], out_ref.at[a - 1], sems.at[a - 1]))
                copies[-1].start()
        for index in range(2):
            a = last - 1 + index
            rest_ref[index, :, :] = g_ref[a].astype(F32) + total.pop(a)
        for copy in copies:
            copy.wait()

    return kernel


def write_update(scaled_ref, sum_ref, one_ref, two_ref, sems, swapped, finish):
    own = lax.axis_index(AXIS) % 2
    if not finish:
        v = sum_ref[...]
        scaled_ref[...] = v / jnp.sqrt(jnp.mean(v * v) + 1e-06)
    for index, target in enumerate((one_ref, two_ref)):

        @pl.when(own == (index ^ swapped))
        def _(index=index, target=target):
            copy = pltpu.make_async_copy(scaled_ref, target, sems.at[index])
            if finish:
                copy.wait()
            else:
                copy.start()


def make_upper_kernel(count, channels, cells, vertical):
    span = 9 * channels
    wide = 3 * channels
    last = count - 1

    def kernel(down_ref, codes_ref, ws_ref, rest_ref, mine_ref, _, out_ref, one_ref, two_ref,
               ps_ref, done_ref, scaled_ref, sem, sems):
        write_update(scaled_ref, mine_ref, one_ref, two_ref, sems, 0, False)
        fill = filler(ps_ref, channels, tap_masks(cells, vertical), vertical)
        planes = flip_planes(down_ref[...].reshape(2 * channels, cells), codes_ref[1, 0:1, 0:1], vertical)
        fill(0, planes[:channels])
        fill(1, planes[channels:], flipped_places(codes_ref[1, 0, 0]))
        weights = ws_ref[channels:3 * channels, :]
        y = dot(weights, ps_ref[0:span, :])
        done_ref[0, :, :] = rest_ref[0] + y[channels:]
        done_ref[1, :, :] = rest_ref[1] + y[:channels] + dot(weights[channels:], ps_ref[span:, :])
        copy = pltpu.make_async_copy(done_ref, out_ref.at[last - 1:count], sem)
        copy.start()
        write_update(scaled_ref, mine_ref, one_ref, two_ref, sems, 0, True)
        copy.wait()

    return kernel


def normalize_kernel(other_ref, _, __, one_ref, two_ref, scaled_ref, sems):
    write_update(scaled_ref, other_ref, one_ref, two_ref, sems, 1, False)
    write_update(scaled_ref, other_ref, one_ref, two_ref, sems, 1, True)


VM = pl.BlockSpec(memory_space=pltpu.VMEM)
SM = pl.BlockSpec(memory_space=pltpu.SMEM)
HB = pl.BlockSpec(memory_space=pltpu.HBM)
PARAMS = pltpu.CompilerParams(vmem_limit_bytes=VMEM_LIMIT)


def body(snapshot, cotangent, first_weight, second_weight, face_codes):
    count, channels, cells = snapshot.shape[1:]
    vertical = cells // R_CELLS
    size = lax.axis_size(AXIS)
    x, g = snapshot[0], cotangent[0]
    def call(kernel, outs, operands, name, scratch=(), specs=None, out_specs=None, aliases=None):
        return pl.pallas_call(
            kernel, out_shape=outs, in_specs=specs or [VM] * len(operands),
            out_specs=out_specs or jax.tree.map(lambda _: VM, outs), input_output_aliases=aliases or {},
            scratch_shapes=list(scratch), compiler_params=PARAMS, name=name,
        )(*operands)

    span = 9 * channels
    shape = jax.ShapeDtypeStruct
    sizes = (count, channels, cells, vertical)
    stack = shape((6 * channels, span), BF16)
    band = shape(((count + 2) * channels, count * channels), BF16)
    edges = shape((2, channels, cells), F32)
    columns = shape((count * span, cells), BF16)
    grads = shape((channels, 27 * channels), F32)
    weight = shape(first_weight.shape, BF16)
    pinned = [
        pltpu.with_memory_space_constraint(v, pltpu.HBM) for v in (face_codes, x, g, first_weight, second_weight)]
    up, codes, x, g, first_weight, second_weight = call(
        make_pack_kernel(count),
        (shape((4, channels, cells), BF16), shape((2, 8, 128), jnp.int32), shape(x.shape, BF16), shape(x.shape, BF16),
         weight, weight),
        pinned, "pack", [pltpu.SMEM((1, 2), jnp.int32), pltpu.SemaphoreType.DMA((5,))], [HB] * 5)
    up = lax.ppermute(up, AXIS, [(b, (b + 1) % size) for b in range(size)])

    sums = shape((2 * span, 4 * channels), F32)
    ws, band_one, band_two, pre_edge, grad_edge, xs, cs, ps, part_one, part_two = call(
        make_interior_kernel(*sizes),
        (stack, band, band, edges, edges, columns, columns, shape(((count - 2) * span, cells), BF16), sums, sums),
        (x, g, first_weight, second_weight), "interior", [pltpu.VMEM(((count + 2) * channels, cells), BF16)])
    two = shape((2 * channels, cells), BF16)
    send, pg_edge, h_edge, low, cf = call(
        make_edge_kernel(*sizes),
        (grads, shape((2, channels, cells), BF16), two, two, shape((2 * span, cells), BF16)),
        (up, x, ws, band_one, band_two, codes, pre_edge, grad_edge, xs, cs, part_one, part_two), "edge",
        [pltpu.VMEM((3 * span, cells), BF16), pltpu.VMEM((span, cells), BF16), pltpu.VMEM((2 * span, cells), BF16)])
    keep, ps_edge = call(
        make_keep_kernel(channels, cells, vertical), (grads, shape((2 * span, cells), BF16)),
        (x, codes, cs, part_one, part_two, pg_edge, h_edge, low, cf), "keep")

    def swap(value, bit):
        return lax.ppermute(value, AXIS, [(b, b ^ bit) for b in range(size)])

    total, pg_sent = lax.optimization_barrier((keep + swap(send, 1), pg_edge))
    down = lax.ppermute(pg_sent, AXIS, [(b, (b - 1) % size) for b in range(size)])
    most_done, rest, back = call(
        make_input_kernel(*sizes), (shape((count, channels, cells), F32), edges, shape((3 * channels, span), BF16)),
        (ps, ps_edge, g, first_weight), "input_grad",
        [pltpu.VMEM((count - 2, channels, cells), F32),
         pltpu.SemaphoreType.DMA((count - 2,))], out_specs=(HB, VM, VM))
    bits = [1 << power for power in range(1, size.bit_length() - 1)]
    rounds = list(zip(bits[-1:] + bits[:-1], bits))
    for index, choice in enumerate(rounds):
        total = total + lax.ppermute(total, AXIS, [(b, b ^ choice[b % 2]) for b in range(size)])
        if index == len(rounds) - 2:
            total, most_done, rest, back = lax.optimization_barrier((total, most_done, rest, back))
        if index == len(rounds) - 1:
            total, down = lax.optimization_barrier((total, down))
    other = swap(total, 1)
    input_grad, first, second = call(
        make_upper_kernel(*sizes), (shape((count, channels, cells), F32), grads, grads),
        (down, codes, back, rest, total, most_done), "upper_planes",
        [pltpu.VMEM((2 * span, cells), BF16), pltpu.VMEM((2, channels, cells), F32), pltpu.VMEM(grads.shape, F32),
         pltpu.SemaphoreType.DMA, pltpu.SemaphoreType.DMA((2,))],
        [VM, VM, VM, VM, VM, HB], out_specs=(HB, HB, HB), aliases={5: 0})
    first, second = call(
        normalize_kernel, (grads, grads), (other, first, second), "normalize",
        [pltpu.VMEM(grads.shape, F32), pltpu.SemaphoreType.DMA((2,))], [VM, HB, HB], out_specs=(HB, HB), aliases={1: 0, 2: 1})
    return (input_grad[None], first, second)


def solution(mesh):
    return jax.shard_map(
        body,
        mesh=mesh,
        in_specs=(
            P("groups", "blocks", None, None),
            P("groups", "blocks", None, None),
            P(),
            P(),
            P(("groups", "blocks"), None),
        ),
        out_specs=(P("groups", "blocks", None, None), P("groups", None), P("groups", None)),
        check_vma=False,
    )
```

```python
import jax
import jax.numpy as jnp
from jax import lax
from jax.experimental import pallas as pl
from jax.experimental.pallas import tpu as pltpu
from jax.sharding import PartitionSpec as P

R_CELLS = 32
AXIS = "blocks"
F32 = jnp.float32
BF16 = jnp.bfloat16
ORDER = (0, 1, 2, 3, 5, 6, 7, 8, 4)
VMEM_LIMIT = 24 * 1024 * 1024


def tap_masks(cells, vertical):
    lane = lax.broadcasted_iota(jnp.int32, (1, cells), 1)
    z = lane % vertical
    r = lane // vertical
    radial = cells // vertical
    masks = []
    for step_r in range(3):
        for step_z in range(3):
            ok = None
            if step_r == 0:
                ok = r >= 1
            if step_r == 2:
                ok = r < radial - 1
            if step_z == 0:
                ok = (z >= 1) if ok is None else ok & (z >= 1)
            if step_z == 2:
                ok = (z < vertical - 1) if ok is None else ok & (z < vertical - 1)
            masks.append(ok)
    return masks


def im2col(plane, store, masks, vertical):
    cells = plane.shape[1]
    wide = plane.astype(F32)
    for place, tap in enumerate(ORDER):
        offset = (tap // 3 - 1) * vertical + (tap % 3 - 1)
        if offset == 0:
            store(place, plane)
            continue
        moved = pltpu.roll(wide, (-offset) % cells, 1)
        moved = jnp.where(masks[tap], moved, 0.0)
        store(place, moved.astype(BF16))


def dot(a, b):
    return jnp.dot(a, b, preferred_element_type=F32)


def dot_nt(a, b):
    return lax.dot_general(a, b, (((1,), (1,)), ((), ())), preferred_element_type=F32)


def flip_planes(planes, code, vertical):
    lanes = 128
    parts = planes.shape[1] // lanes
    wide = planes.astype(F32)
    turn_r = code % 2 == 1
    bits = jnp.where(turn_r, lanes - vertical, 0) + jnp.where(code // 2 == 1, vertical - 1, 0)
    index = lax.broadcasted_iota(jnp.int32, (planes.shape[0], lanes), 1) ^ bits
    moved = [jnp.take_along_axis(wide[:, j * lanes:(j + 1) * lanes], index, axis=1) for j in range(parts)]
    return jnp.concatenate(
        [jnp.where(turn_r, moved[parts - 1 - j], moved[j]) for j in range(parts)], axis=1).astype(BF16)


def flipped_places(code):
    flip_r, flip_z = code % 2, code // 2
    places = []
    for tap in ORDER:
        r, z = tap // 3, tap % 3
        moved = 3 * (r + (2 - 2 * r) * flip_r) + z + (2 - 2 * z) * flip_z
        places.append(8 if tap == 4 else moved - (moved > 4).astype(jnp.int32))
    return places


def activation(pre, grad):
    sig = jax.nn.sigmoid(pre)
    hidden = (pre * sig).astype(BF16)
    return hidden, (grad * sig * (1.0 + pre * (1.0 - sig))).astype(BF16)


def filler(ref, channels, masks, vertical):
    def fill(position, plane, places=None, also=None):
        def store(place, value):
            if places is None:
                start = (9 * position + place) * channels
            else:
                start = pl.multiple_of((9 * position + places[place]) * channels, channels)
            ref[pl.ds(start, channels), :] = value
            if also is not None:
                also[place * channels:(place + 1) * channels, :] = value

        im2col(plane, store, masks, vertical)

    return fill


def make_pack_kernel(count):
    def kernel(x_ref, g_ref, up_ref, x_out, g_out, sems):
        moves = ((x_ref, x_out), (g_ref, g_out))
        copies = [pltpu.make_async_copy(*move, sems.at[index]) for index, move in enumerate(moves)]
        for copy in copies:
            copy.start()
        for index, field in enumerate((x_out, g_out)):
            copies[index].wait()
            up_ref[2 * index:2 * index + 2, :, :] = field[count - 2:count]

    return kernel


def make_interior_kernel(count, channels, cells, vertical):
    span = 9 * channels
    most = 8 * channels
    wide = 3 * channels
    last = count - 1

    def kernel(x_ref, g_ref, codes_hbm, w1_hbm, w2_hbm,
               codes_ref, ws_ref, t1_ref, t2_ref, pe_ref, ge_ref, xs_ref, cs_ref, ps_ref, g1_ref, g2_ref, h_ref,
               scalars, w1_ref, w2_ref, sems):
        moves = ((codes_hbm, scalars), (w1_hbm, w1_ref), (w2_hbm, w2_ref))
        copies = [pltpu.make_async_copy(*move, sems.at[index]) for index, move in enumerate(moves)]
        for copy in copies:
            copy.start()
        masks = tap_masks(cells, vertical)
        fill_x = filler(xs_ref, channels, masks, vertical)
        fill_g = filler(cs_ref, channels, masks, vertical)
        fill_p = filler(ps_ref, channels, masks, vertical)
        for a in range(count):
            fill_x(a, x_ref[a])
            fill_g(a, g_ref[a])

        for copy in copies:
            copy.wait()
        for side in range(2):
            codes_ref[side, :, :] = jnp.full((8, 128), scalars[0, side], jnp.int32)
        for step in range(3):
            rows = slice(step * channels, (step + 1) * channels)
            base = step * span
            half = 4 * channels
            ws_ref[rows, 0:half] = w1_ref[:, base:base + half]
            ws_ref[rows, half:most] = w1_ref[:, base + half + channels:base + span]
            ws_ref[rows, most:span] = w1_ref[:, base + half:base + half + channels]
        for weight_ref, base in ((w2_ref, wide), (w1_ref, 2 * wide)):
            turned = weight_ref[...].astype(F32).T
            for step in range(3):
                for place, tap in enumerate(ORDER):
                    at = (9 * (2 - step) + 8 - tap) * channels
                    ws_ref[base + step * channels:base + (step + 1) * channels,
                           place * channels:(place + 1) * channels] = turned[at:at + channels, :].astype(BF16)
        for ref, base in ((t1_ref, 0), (t2_ref, wide)):
            ref[...] = jnp.zeros_like(ref)
            for step in range(3):
                centre = ws_ref[base + step * channels:base + (step + 1) * channels, most:span]
                for a in range(count):
                    row = (a + 2 - step) * channels
                    ref[row:row + channels, a * channels:(a + 1) * channels] = centre

        h_ref[...] = jnp.zeros_like(h_ref)
        pre_all = dot(t1_ref[...], x_ref[...].reshape(count * channels, cells))
        grad_all = dot(t2_ref[...], g_ref[...].reshape(count * channels, cells))
        pre = {a: pre_all[(a + 1) * channels:(a + 2) * channels] for a in range(-1, last)}
        grad = {a: grad_all[(a + 1) * channels:(a + 2) * channels] for a in range(-1, last)}

        for a in range(count):
            columns = slice(a * span, a * span + most)
            first = max(0, a + 2 - last) * channels
            y = dot(ws_ref[first:wide, 0:most], xs_ref[columns, :])
            v = dot(ws_ref[wide + first:2 * wide, 0:most], cs_ref[columns, :])
            for step in range(3):
                target = a + 1 - step
                rows = slice(step * channels - first, (step + 1) * channels - first)
                if -1 <= target < last:
                    grad[target] = grad[target] + v[rows]
                if 0 <= target < last:
                    pre[target] = pre[target] + y[rows]
            done = a - 1
            if 1 <= done <= last - 1:
                hidden, pg = activation(pre.pop(done), grad.pop(done))
                h_ref[(done + 1) * channels:(done + 2) * channels, :] = hidden
                fill_p(done - 1, pg)
            if a == 1:
                for index, plane in ((0, -1), (1, 0)):
                    pe_ref[index, :, :] = pre.pop(plane)
                    ge_ref[index, :, :] = grad.pop(plane)
        grad_one, grad_two = None, None
        for a in range(0, count, 2):
            term = dot_nt(cs_ref[a * span:(a + 2) * span, :], h_ref[a * channels:(a + 4) * channels, :])
            grad_two = term if grad_two is None else grad_two + term
        for a in range(1, last, 2):
            term = dot_nt(ps_ref[(a - 1) * span:(a + 1) * span, :], x_ref[a - 1:a + 3].reshape(4 * channels, cells))
            grad_one = term if grad_one is None else grad_one + term
        g1_ref[...] = grad_one
        g2_ref[...] = grad_two

    return kernel


def put_blocks(ref, pairs, channels):
    span = 9 * channels
    total = pairs[0:span] + pltpu.roll(pairs[span:], 3 * channels, 1)
    moved = {}
    for place, tap in enumerate(ORDER):
        block = total[place * channels:(place + 1) * channels]
        shift = ((8 - tap) * channels) % (4 * channels)
        moved[8 - tap] = pltpu.roll(block, shift, 1) if shift else block
    lane = lax.broadcasted_iota(jnp.int32, (channels, 4 * channels), 1) // channels
    for first in range(0, 27, 4):
        tile = moved[first % 9]
        for n in range(first + 1, min(first + 4, 27)):
            tile = jnp.where(lane >= n - first, moved[n % 9], tile)
        width = min(4, 27 - first) * channels
        ref[:, first * channels:first * channels + width] = tile[:, :width]


def first_terms(sum_ref, ps_ref, low_ref, x_ref, channels):
    near = jnp.concatenate((low_ref[...], x_ref[0:2].reshape(low_ref.shape)), axis=0)
    return sum_ref[...] + dot_nt(ps_ref[...], near)


def second_terms(sum_ref, cf_ref, cs_ref, hidden, channels):
    zero = jnp.zeros_like(hidden)
    return (sum_ref[...] + dot_nt(cf_ref[...], jnp.concatenate((zero, hidden), axis=0))
            + dot_nt(cs_ref[0:18 * channels, :], jnp.concatenate((hidden, zero), axis=0)))


def make_keep_kernel(channels, cells, vertical):
    def kernel(x_ref, codes_ref, cs_ref, g1_ref, g2_ref, pg_ref, h_ref, low_ref, cf_ref, keep_ref, ps_ref):
        is_odd = lax.axis_index(AXIS) % 2 == 1
        fill_p = filler(ps_ref, channels, tap_masks(cells, vertical), vertical)
        fill_p(0, pg_ref[0], flipped_places(codes_ref[0, 0, 0]))
        fill_p(1, pg_ref[1])

        @pl.when(jnp.logical_not(is_odd))
        def _():
            put_blocks(keep_ref, first_terms(g1_ref, ps_ref, low_ref, x_ref, channels), channels)

        @pl.when(is_odd)
        def _():
            put_blocks(keep_ref, second_terms(g2_ref, cf_ref, cs_ref, h_ref[...], channels), channels)

    return kernel


def make_edge_kernel(count, channels, cells, vertical):
    span = 9 * channels
    most = 8 * channels
    wide = 3 * channels

    def kernel(up_ref, x_ref, ws_ref, t1_ref, t2_ref, codes_ref, pe_ref, ge_ref, xs_ref, cs_ref, g1_ref, g2_ref,
               send_ref, pg_ref, h_ref, low_ref, cf_ref, xf_ref, xo_ref, ps_ref):
        is_odd = lax.axis_index(AXIS) % 2 == 1
        masks = tap_masks(cells, vertical)
        places = flipped_places(codes_ref[0, 0, 0])
        fill_x = filler(xf_ref, channels, masks, vertical)
        fill_c = filler(cf_ref, channels, masks, vertical)
        planes = flip_planes(up_ref[...].reshape(4 * channels, cells), codes_ref[0, 0:1, 0:1], vertical)
        fill_x(0, planes[0:channels], places)
        fill_x(1, planes[channels:2 * channels], places, xo_ref)
        for place in range(9):
            start = 2 * span + places[place] * channels
            xf_ref[pl.ds(pl.multiple_of(start, channels), channels), :] = xs_ref[place * channels:(place + 1) * channels, :]
        fill_c(0, planes[2 * channels:3 * channels], places)
        fill_c(1, planes[3 * channels:], places)

        def eight(ref, index):
            return ref[index * span:index * span + most, :]

        def rows(part, first, end):
            return ws_ref[part * wide + first * channels:part * wide + end * channels, 0:most]

        centre = slice(2 * channels, 4 * channels), slice(0, 2 * channels)
        x_mid = dot(t1_ref[centre], planes[:2 * channels])
        g_mid = dot(t2_ref[centre], planes[2 * channels:])
        pre_m = (pe_ref[0] + x_mid[:channels] + dot(rows(0, 0, 1), eight(xf_ref, 0))
                 + dot(rows(0, 1, 2), eight(xf_ref, 1)) + dot(rows(0, 2, 3), eight(xf_ref, 2)))
        pre_0 = pe_ref[1] + x_mid[channels:] + dot(rows(0, 0, 1), eight(xo_ref, 0))
        near = dot(rows(1, 0, 2), eight(cf_ref, 1))
        grad_m = ge_ref[0] + g_mid[:channels] + near[channels:] + dot(rows(1, 0, 1), eight(cf_ref, 0))
        grad_0 = ge_ref[1] + g_mid[channels:] + near[:channels]
        hid_m, pg_m = activation(pre_m, grad_m)
        hid_0, pg_0 = activation(pre_0, grad_0)
        pg_ref[0, :, :] = pg_m
        pg_ref[1, :, :] = pg_0

        h_ref[0:channels, :] = hid_m
        h_ref[channels:, :] = hid_0
        low_ref[...] = planes[:2 * channels]

        @pl.when(jnp.logical_not(is_odd))
        def _():
            put_blocks(send_ref, second_terms(g2_ref, cf_ref, cs_ref, h_ref[...], channels), channels)

        @pl.when(is_odd)
        def _():
            fill_p = filler(ps_ref, channels, masks, vertical)
            fill_p(0, pg_m, places)
            fill_p(1, pg_0)
            put_blocks(send_ref, first_terms(g1_ref, ps_ref, low_ref, x_ref, channels), channels)

    return kernel


def make_input_kernel(count, channels, cells, vertical):
    span = 9 * channels
    wide = 3 * channels
    last = count - 1

    def kernel(inner_ref, edge_ref, g_ref, ws_ref, out_ref, rest_ref, done_ref, sems):
        weights = ws_ref[2 * wide:3 * wide, :]
        total = {}
        copies = []
        for a in range(-1, last):
            columns = edge_ref[(a + 1) * span:(a + 2) * span, :] if a <= 0 else inner_ref[(a - 1) * span:a * span, :]
            if a == -1:
                total[0] = dot(weights[0:channels], columns)
                continue
            y = dot(weights, columns)
            for step in range(3):
                target = a + 1 - step
                if 0 <= target < count:
                    part = y[step * channels:(step + 1) * channels]
                    total[target] = part if target not in total else total[target] + part
            if a >= 1:
                done_ref[a - 1, :, :] = g_ref[a - 1].astype(F32) + total.pop(a - 1)
                copies.append(pltpu.make_async_copy(done_ref.at[a - 1], out_ref.at[a - 1], sems.at[a - 1]))
                copies[-1].start()
        for index in range(2):
            a = last - 1 + index
            rest_ref[index, :, :] = g_ref[a].astype(F32) + total.pop(a)
        for copy in copies:
            copy.wait()

    return kernel


def write_update(scaled_ref, sum_ref, one_ref, two_ref, sems, swapped, finish):
    own = lax.axis_index(AXIS) % 2
    if not finish:
        v = sum_ref[...]
        scaled_ref[...] = v / jnp.sqrt(jnp.mean(v * v) + 1e-06)
    for index, target in enumerate((one_ref, two_ref)):

        @pl.when(own == (index ^ swapped))
        def _(index=index, target=target):
            copy = pltpu.make_async_copy(scaled_ref, target, sems.at[index])
            if finish:
                copy.wait()
            else:
                copy.start()


def make_upper_kernel(count, channels, cells, vertical):
    span = 9 * channels
    wide = 3 * channels
    last = count - 1

    def kernel(down_ref, codes_ref, ws_ref, rest_ref, mine_ref, _, out_ref, one_ref, two_ref,
               ps_ref, done_ref, scaled_ref, sem, sems):
        write_update(scaled_ref, mine_ref, one_ref, two_ref, sems, 0, False)
        fill = filler(ps_ref, channels, tap_masks(cells, vertical), vertical)
        planes = flip_planes(down_ref[...].reshape(2 * channels, cells), codes_ref[1, 0:1, 0:1], vertical)
        fill(0, planes[:channels])
        fill(1, planes[channels:], flipped_places(codes_ref[1, 0, 0]))
        weights = ws_ref[2 * wide + channels:3 * wide, :]
        y = dot(weights, ps_ref[0:span, :])
        done_ref[0, :, :] = rest_ref[0] + y[channels:]
        done_ref[1, :, :] = rest_ref[1] + y[:channels] + dot(weights[channels:], ps_ref[span:, :])
        copy = pltpu.make_async_copy(done_ref, out_ref.at[last - 1:count], sem)
        copy.start()
        write_update(scaled_ref, mine_ref, one_ref, two_ref, sems, 0, True)
        copy.wait()

    return kernel


def normalize_kernel(other_ref, _, __, one_ref, two_ref, scaled_ref, sems):
    write_update(scaled_ref, other_ref, one_ref, two_ref, sems, 1, False)
    write_update(scaled_ref, other_ref, one_ref, two_ref, sems, 1, True)


VM = pl.BlockSpec(memory_space=pltpu.VMEM)
SM = pl.BlockSpec(memory_space=pltpu.SMEM)
HB = pl.BlockSpec(memory_space=pltpu.HBM)
PARAMS = pltpu.CompilerParams(vmem_limit_bytes=VMEM_LIMIT)


def body(snapshot, cotangent, first_weight, second_weight, face_codes):
    count, channels, cells = snapshot.shape[1:]
    vertical = cells // R_CELLS
    size = lax.axis_size(AXIS)
    x, g = snapshot[0], cotangent[0]
    def call(kernel, outs, operands, name, scratch=(), specs=None, out_specs=None, aliases=None):
        return pl.pallas_call(
            kernel, out_shape=outs, in_specs=specs or [VM] * len(operands),
            out_specs=out_specs or jax.tree.map(lambda _: VM, outs), input_output_aliases=aliases or {},
            scratch_shapes=list(scratch), compiler_params=PARAMS, name=name,
        )(*operands)

    span = 9 * channels
    shape = jax.ShapeDtypeStruct
    sizes = (count, channels, cells, vertical)
    stack = shape((span, span), BF16)
    band = shape(((count + 2) * channels, count * channels), BF16)
    edges = shape((2, channels, cells), F32)
    columns = shape((count * span, cells), BF16)
    grads = shape((channels, 27 * channels), F32)
    weight = shape(first_weight.shape, BF16)
    pinned = [
        pltpu.with_memory_space_constraint(v, pltpu.HBM) for v in (face_codes, x, g, first_weight, second_weight)]
    face_codes, x, g, first_weight, second_weight = pinned
    up, x, g = call(
        make_pack_kernel(count),
        (shape((4, channels, cells), BF16), shape(x.shape, BF16), shape(x.shape, BF16)),
        (x, g), "pack", [pltpu.SemaphoreType.DMA((2,))], [HB] * 2)
    up = lax.ppermute(up, AXIS, [(b, (b + 1) % size) for b in range(size)])

    sums = shape((2 * span, 4 * channels), F32)
    codes, ws, band_one, band_two, pre_edge, grad_edge, xs, cs, ps, part_one, part_two = call(
        make_interior_kernel(*sizes),
        (shape((2, 8, 128), jnp.int32), stack, band, band, edges, edges, columns, columns, shape(((count - 2) * span, cells), BF16), sums, sums),
        (x, g, face_codes, first_weight, second_weight), "interior",
        [pltpu.VMEM(((count + 2) * channels, cells), BF16), pltpu.SMEM((1, 2), jnp.int32),
         pltpu.VMEM(weight.shape, BF16), pltpu.VMEM(weight.shape, BF16), pltpu.SemaphoreType.DMA((3,))],
        [VM, VM, HB, HB, HB])
    two = shape((2 * channels, cells), BF16)
    send, pg_edge, h_edge, low, cf = call(
        make_edge_kernel(*sizes),
        (grads, shape((2, channels, cells), BF16), two, two, shape((2 * span, cells), BF16)),
        (up, x, ws, band_one, band_two, codes, pre_edge, grad_edge, xs, cs, part_one, part_two), "edge",
        [pltpu.VMEM((3 * span, cells), BF16), pltpu.VMEM((span, cells), BF16), pltpu.VMEM((2 * span, cells), BF16)])
    keep, ps_edge = call(
        make_keep_kernel(channels, cells, vertical), (grads, shape((2 * span, cells), BF16)),
        (x, codes, cs, part_one, part_two, pg_edge, h_edge, low, cf), "keep")

    def swap(value, bit):
        return lax.ppermute(value, AXIS, [(b, b ^ bit) for b in range(size)])

    total, pg_sent = lax.optimization_barrier((keep + swap(send, 1), pg_edge))
    down = lax.ppermute(pg_sent, AXIS, [(b, (b - 1) % size) for b in range(size)])
    most_done, rest = call(
        make_input_kernel(*sizes), (shape((count, channels, cells), F32), edges),
        (ps, ps_edge, g, ws), "input_grad",
        [pltpu.VMEM((count - 2, channels, cells), F32),
         pltpu.SemaphoreType.DMA((count - 2,))], out_specs=(HB, VM))
    bits = [1 << power for power in range(1, size.bit_length() - 1)]
    rounds = list(zip(bits[-1:] + bits[:-1], bits))
    for index, choice in enumerate(rounds):
        total = total + lax.ppermute(total, AXIS, [(b, b ^ choice[b % 2]) for b in range(size)])
        if index == len(rounds) - 2:
            total, most_done, rest = lax.optimization_barrier((total, most_done, rest))
        if index == len(rounds) - 1:
            total, down = lax.optimization_barrier((total, down))
    other = swap(total, 1)
    input_grad, first, second = call(
        make_upper_kernel(*sizes), (shape((count, channels, cells), F32), grads, grads),
        (down, codes, ws, rest, total, most_done), "upper_planes",
        [pltpu.VMEM((2 * span, cells), BF16), pltpu.VMEM((2, channels, cells), F32), pltpu.VMEM(grads.shape, F32),
         pltpu.SemaphoreType.DMA, pltpu.SemaphoreType.DMA((2,))],
        [VM, VM, VM, VM, VM, HB], out_specs=(HB, HB, HB), aliases={5: 0})
    first, second = call(
        normalize_kernel, (grads, grads), (other, first, second), "normalize",
        [pltpu.VMEM(grads.shape, F32), pltpu.SemaphoreType.DMA((2,))], [VM, HB, HB], out_specs=(HB, HB), aliases={1: 0, 2: 1})
    return (input_grad[None], first, second)


def solution(mesh):
    return jax.shard_map(
        body,
        mesh=mesh,
        in_specs=(
            P("groups", "blocks", None, None),
            P("groups", "blocks", None, None),
            P(),
            P(),
            P(("groups", "blocks"), None),
        ),
        out_specs=(P("groups", "blocks", None, None), P("groups", None), P("groups", None)),
        check_vma=False,
    )
```

```python
import jax
import jax.numpy as jnp
from jax import lax
from jax.experimental import pallas as pl
from jax.experimental.pallas import tpu as pltpu
from jax.sharding import PartitionSpec as P

R_CELLS = 32
AXIS = "blocks"
F32 = jnp.float32
BF16 = jnp.bfloat16
ORDER = (0, 1, 2, 3, 5, 6, 7, 8, 4)
VMEM_LIMIT = 24 * 1024 * 1024


def tap_masks(cells, vertical):
    lane = lax.broadcasted_iota(jnp.int32, (1, cells), 1)
    z = lane % vertical
    r = lane // vertical
    radial = cells // vertical
    masks = []
    for step_r in range(3):
        for step_z in range(3):
            ok = None
            if step_r == 0:
                ok = r >= 1
            if step_r == 2:
                ok = r < radial - 1
            if step_z == 0:
                ok = (z >= 1) if ok is None else ok & (z >= 1)
            if step_z == 2:
                ok = (z < vertical - 1) if ok is None else ok & (z < vertical - 1)
            masks.append(ok)
    return masks


def im2col(plane, store, masks, vertical):
    cells = plane.shape[1]
    wide = plane.astype(F32)
    for place, tap in enumerate(ORDER):
        offset = (tap // 3 - 1) * vertical + (tap % 3 - 1)
        if offset == 0:
            store(place, plane)
            continue
        moved = pltpu.roll(wide, (-offset) % cells, 1)
        moved = jnp.where(masks[tap], moved, 0.0)
        store(place, moved.astype(BF16))


def dot(a, b):
    return jnp.dot(a, b, preferred_element_type=F32)


def dot_nt(a, b):
    return lax.dot_general(a, b, (((1,), (1,)), ((), ())), preferred_element_type=F32)


def flip_planes(planes, code, vertical):
    lanes = 128
    parts = planes.shape[1] // lanes
    wide = planes.astype(F32)
    turn_r = code % 2 == 1
    bits = jnp.where(turn_r, lanes - vertical, 0) + jnp.where(code // 2 == 1, vertical - 1, 0)
    index = lax.broadcasted_iota(jnp.int32, (planes.shape[0], lanes), 1) ^ bits
    moved = [jnp.take_along_axis(wide[:, j * lanes:(j + 1) * lanes], index, axis=1) for j in range(parts)]
    return jnp.concatenate(
        [jnp.where(turn_r, moved[parts - 1 - j], moved[j]) for j in range(parts)], axis=1).astype(BF16)


def flipped_places(code):
    flip_r, flip_z = code % 2, code // 2
    places = []
    for tap in ORDER:
        r, z = tap // 3, tap % 3
        moved = 3 * (r + (2 - 2 * r) * flip_r) + z + (2 - 2 * z) * flip_z
        places.append(8 if tap == 4 else moved - (moved > 4).astype(jnp.int32))
    return places


def activation(pre, grad):
    sig = jax.nn.sigmoid(pre)
    hidden = (pre * sig).astype(BF16)
    return hidden, (grad * sig * (1.0 + pre * (1.0 - sig))).astype(BF16)


def filler(ref, channels, masks, vertical):
    def fill(position, plane, places=None, also=None):
        def store(place, value):
            if places is None:
                start = (9 * position + place) * channels
            else:
                start = pl.multiple_of((9 * position + places[place]) * channels, channels)
            ref[pl.ds(start, channels), :] = value
            if also is not None:
                also[place * channels:(place + 1) * channels, :] = value

        im2col(plane, store, masks, vertical)

    return fill


def make_pack_kernel(count):
    def kernel(codes_ref, x_ref, g_ref, w1_ref, w2_ref, up_ref, codes_out, x_out, g_out, w1_out, w2_out, scalars, sems):
        moves = ((x_ref, x_out), (g_ref, g_out), (codes_ref, scalars), (w1_ref, w1_out), (w2_ref, w2_out))
        copies = [pltpu.make_async_copy(*move, sems.at[index]) for index, move in enumerate(moves)]
        for copy in copies:
            copy.start()
        for index, field in enumerate((x_out, g_out)):
            copies[index].wait()
            up_ref[2 * index:2 * index + 2, :, :] = field[count - 2:count]
        for copy in copies[2:]:
            copy.wait()
        for side in range(2):
            codes_out[side, :, :] = jnp.full((8, 128), scalars[0, side], jnp.int32)

    return kernel


def make_interior_kernel(count, channels, cells, vertical):
    span = 9 * channels
    most = 8 * channels
    wide = 3 * channels
    last = count - 1

    def kernel(x_ref, g_ref, w1_ref, w2_ref,
               ws_ref, t1_ref, t2_ref, pe_ref, ge_ref, xs_ref, cs_ref, ps_ref, g1_ref, g2_ref, h_ref):
        masks = tap_masks(cells, vertical)
        for step in range(3):
            rows = slice(step * channels, (step + 1) * channels)
            base = step * span
            half = 4 * channels
            ws_ref[rows, 0:half] = w1_ref[:, base:base + half]
            ws_ref[rows, half:most] = w1_ref[:, base + half + channels:base + span]
            ws_ref[rows, most:span] = w1_ref[:, base + half:base + half + channels]
        for weight_ref, base in ((w2_ref, wide), (w1_ref, 2 * wide)):
            turned = weight_ref[...].astype(F32).T
            for step in range(3):
                for place, tap in enumerate(ORDER):
                    at = (9 * (2 - step) + 8 - tap) * channels
                    ws_ref[base + step * channels:base + (step + 1) * channels,
                           place * channels:(place + 1) * channels] = turned[at:at + channels, :].astype(BF16)
        for ref, base in ((t1_ref, 0), (t2_ref, wide)):
            ref[...] = jnp.zeros_like(ref)
            for step in range(3):
                centre = ws_ref[base + step * channels:base + (step + 1) * channels, most:span]
                for a in range(count):
                    row = (a + 2 - step) * channels
                    ref[row:row + channels, a * channels:(a + 1) * channels] = centre

        fill_x = filler(xs_ref, channels, masks, vertical)
        fill_g = filler(cs_ref, channels, masks, vertical)
        fill_p = filler(ps_ref, channels, masks, vertical)
        for a in range(count):
            fill_x(a, x_ref[a])
            fill_g(a, g_ref[a])

        h_ref[...] = jnp.zeros_like(h_ref)
        pre_all = dot(t1_ref[...], x_ref[...].reshape(count * channels, cells))
        grad_all = dot(t2_ref[...], g_ref[...].reshape(count * channels, cells))
        pre = {a: pre_all[(a + 1) * channels:(a + 2) * channels] for a in range(-1, last)}
        grad = {a: grad_all[(a + 1) * channels:(a + 2) * channels] for a in range(-1, last)}

        for a in range(count):
            columns = slice(a * span, a * span + most)
            first = max(0, a + 2 - last) * channels
            y = dot(ws_ref[first:wide, 0:most], xs_ref[columns, :])
            v = dot(ws_ref[wide + first:2 * wide, 0:most], cs_ref[columns, :])
            for step in range(3):
                target = a + 1 - step
                rows = slice(step * channels - first, (step + 1) * channels - first)
                if -1 <= target < last:
                    grad[target] = grad[target] + v[rows]
                if 0 <= target < last:
                    pre[target] = pre[target] + y[rows]
            done = a - 1
            if 1 <= done <= last - 1:
                hidden, pg = activation(pre.pop(done), grad.pop(done))
                h_ref[(done + 1) * channels:(done + 2) * channels, :] = hidden
                fill_p(done - 1, pg)
            if a == 1:
                for index, plane in ((0, -1), (1, 0)):
                    pe_ref[index, :, :] = pre.pop(plane)
                    ge_ref[index, :, :] = grad.pop(plane)
        grad_one, grad_two = None, None
        for a in range(0, count, 2):
            term = dot_nt(cs_ref[a * span:(a + 2) * span, :], h_ref[a * channels:(a + 4) * channels, :])
            grad_two = term if grad_two is None else grad_two + term
        for a in range(1, last, 2):
            term = dot_nt(ps_ref[(a - 1) * span:(a + 1) * span, :], x_ref[a - 1:a + 3].reshape(4 * channels, cells))
            grad_one = term if grad_one is None else grad_one + term
        g1_ref[...] = grad_one
        g2_ref[...] = grad_two

    return kernel


def put_blocks(ref, pairs, channels):
    span = 9 * channels
    total = pairs[0:span] + pltpu.roll(pairs[span:], 3 * channels, 1)
    moved = {}
    for place, tap in enumerate(ORDER):
        block = total[place * channels:(place + 1) * channels]
        shift = ((8 - tap) * channels) % (4 * channels)
        moved[8 - tap] = pltpu.roll(block, shift, 1) if shift else block
    lane = lax.broadcasted_iota(jnp.int32, (channels, 4 * channels), 1) // channels
    for first in range(0, 27, 4):
        tile = moved[first % 9]
        for n in range(first + 1, min(first + 4, 27)):
            tile = jnp.where(lane >= n - first, moved[n % 9], tile)
        width = min(4, 27 - first) * channels
        ref[:, first * channels:first * channels + width] = tile[:, :width]


def first_terms(sum_ref, ps_ref, low_ref, x_ref, channels):
    near = jnp.concatenate((low_ref[...], x_ref[0:2].reshape(low_ref.shape)), axis=0)
    return sum_ref[...] + dot_nt(ps_ref[...], near)


def second_terms(sum_ref, cf_ref, cs_ref, hidden, channels):
    zero = jnp.zeros_like(hidden)
    return (sum_ref[...] + dot_nt(cf_ref[...], jnp.concatenate((zero, hidden), axis=0))
            + dot_nt(cs_ref[0:18 * channels, :], jnp.concatenate((hidden, zero), axis=0)))


def make_keep_kernel(channels, cells, vertical):
    def kernel(x_ref, codes_ref, cs_ref, g1_ref, g2_ref, pg_ref, h_ref, low_ref, cf_ref, keep_ref, ps_ref):
        is_odd = lax.axis_index(AXIS) % 2 == 1
        fill_p = filler(ps_ref, channels, tap_masks(cells, vertical), vertical)
        fill_p(0, pg_ref[0], flipped_places(codes_ref[0, 0, 0]))
        fill_p(1, pg_ref[1])

        @pl.when(jnp.logical_not(is_odd))
        def _():
            put_blocks(keep_ref, first_terms(g1_ref, ps_ref, low_ref, x_ref, channels), channels)

        @pl.when(is_odd)
        def _():
            put_blocks(keep_ref, second_terms(g2_ref, cf_ref, cs_ref, h_ref[...], channels), channels)

    return kernel


def make_edge_kernel(count, channels, cells, vertical):
    span = 9 * channels
    most = 8 * channels
    wide = 3 * channels

    def kernel(up_ref, x_ref, ws_ref, t1_ref, t2_ref, codes_ref, pe_ref, ge_ref, xs_ref, cs_ref, g1_ref, g2_ref,
               send_ref, pg_ref, h_ref, low_ref, cf_ref, xf_ref, xo_ref, ps_ref):
        is_odd = lax.axis_index(AXIS) % 2 == 1
        masks = tap_masks(cells, vertical)
        places = flipped_places(codes_ref[0, 0, 0])
        fill_x = filler(xf_ref, channels, masks, vertical)
        fill_c = filler(cf_ref, channels, masks, vertical)
        planes = flip_planes(up_ref[...].reshape(4 * channels, cells), codes_ref[0, 0:1, 0:1], vertical)
        fill_x(0, planes[0:channels], places)
        fill_x(1, planes[channels:2 * channels], places, xo_ref)
        for place in range(9):
            start = 2 * span + places[place] * channels
            xf_ref[pl.ds(pl.multiple_of(start, channels), channels), :] = xs_ref[place * channels:(place + 1) * channels, :]
        fill_c(0, planes[2 * channels:3 * channels], places)
        fill_c(1, planes[3 * channels:], places)

        def eight(ref, index):
            return ref[index * span:index * span + most, :]

        def rows(part, first, end):
            return ws_ref[part * wide + first * channels:part * wide + end * channels, 0:most]

        centre = slice(2 * channels, 4 * channels), slice(0, 2 * channels)
        x_mid = dot(t1_ref[centre], planes[:2 * channels])
        g_mid = dot(t2_ref[centre], planes[2 * channels:])
        pre_m = (pe_ref[0] + x_mid[:channels] + dot(rows(0, 0, 1), eight(xf_ref, 0))
                 + dot(rows(0, 1, 2), eight(xf_ref, 1)) + dot(rows(0, 2, 3), eight(xf_ref, 2)))
        pre_0 = pe_ref[1] + x_mid[channels:] + dot(rows(0, 0, 1), eight(xo_ref, 0))
        near = dot(rows(1, 0, 2), eight(cf_ref, 1))
        grad_m = ge_ref[0] + g_mid[:channels] + near[channels:] + dot(rows(1, 0, 1), eight(cf_ref, 0))
        grad_0 = ge_ref[1] + g_mid[channels:] + near[:channels]
        hid_m, pg_m = activation(pre_m, grad_m)
        hid_0, pg_0 = activation(pre_0, grad_0)
        pg_ref[0, :, :] = pg_m
        pg_ref[1, :, :] = pg_0

        h_ref[0:channels, :] = hid_m
        h_ref[channels:, :] = hid_0
        low_ref[...] = planes[:2 * channels]

        @pl.when(jnp.logical_not(is_odd))
        def _():
            put_blocks(send_ref, second_terms(g2_ref, cf_ref, cs_ref, h_ref[...], channels), channels)

        @pl.when(is_odd)
        def _():
            fill_p = filler(ps_ref, channels, masks, vertical)
            fill_p(0, pg_m, places)
            fill_p(1, pg_0)
            put_blocks(send_ref, first_terms(g1_ref, ps_ref, low_ref, x_ref, channels), channels)

    return kernel


def make_input_kernel(count, channels, cells, vertical):
    span = 9 * channels
    wide = 3 * channels
    last = count - 1

    def kernel(inner_ref, edge_ref, g_ref, ws_ref, out_ref, rest_ref, done_ref, sems):
        weights = ws_ref[2 * wide:3 * wide, :]
        total = {}
        copies = []
        for a in range(-1, last):
            columns = edge_ref[(a + 1) * span:(a + 2) * span, :] if a <= 0 else inner_ref[(a - 1) * span:a * span, :]
            if a == -1:
                total[0] = dot(weights[0:channels], columns)
                continue
            y = dot(weights, columns)
            for step in range(3):
                target = a + 1 - step
                if 0 <= target < count:
                    part = y[step * channels:(step + 1) * channels]
                    total[target] = part if target not in total else total[target] + part
            if a >= 1:
                done_ref[a - 1, :, :] = g_ref[a - 1].astype(F32) + total.pop(a - 1)
                copies.append(pltpu.make_async_copy(done_ref.at[a - 1], out_ref.at[a - 1], sems.at[a - 1]))
                copies[-1].start()
        for index in range(2):
            a = last - 1 + index
            rest_ref[index, :, :] = g_ref[a].astype(F32) + total.pop(a)
        for copy in copies:
            copy.wait()

    return kernel


def write_update(scaled_ref, sum_ref, one_ref, two_ref, sems, swapped, finish):
    own = lax.axis_index(AXIS) % 2
    if not finish:
        v = sum_ref[...]
        scaled_ref[...] = v / jnp.sqrt(jnp.mean(v * v) + 1e-06)
    for index, target in enumerate((one_ref, two_ref)):

        @pl.when(own == (index ^ swapped))
        def _(index=index, target=target):
            copy = pltpu.make_async_copy(scaled_ref, target, sems.at[index])
            if finish:
                copy.wait()
            else:
                copy.start()


def make_upper_kernel(count, channels, cells, vertical):
    span = 9 * channels
    wide = 3 * channels
    last = count - 1

    def kernel(down_ref, codes_ref, ws_ref, rest_ref, mine_ref, _, out_ref, one_ref, two_ref,
               ps_ref, done_ref, scaled_ref, sem, sems):
        write_update(scaled_ref, mine_ref, one_ref, two_ref, sems, 0, False)
        fill = filler(ps_ref, channels, tap_masks(cells, vertical), vertical)
        planes = flip_planes(down_ref[...].reshape(2 * channels, cells), codes_ref[1, 0:1, 0:1], vertical)
        fill(0, planes[:channels])
        fill(1, planes[channels:], flipped_places(codes_ref[1, 0, 0]))
        weights = ws_ref[2 * wide + channels:3 * wide, :]
        y = dot(weights, ps_ref[0:span, :])
        done_ref[0, :, :] = rest_ref[0] + y[channels:]
        done_ref[1, :, :] = rest_ref[1] + y[:channels] + dot(weights[channels:], ps_ref[span:, :])
        copy = pltpu.make_async_copy(done_ref, out_ref.at[last - 1:count], sem)
        copy.start()
        write_update(scaled_ref, mine_ref, one_ref, two_ref, sems, 0, True)
        copy.wait()

    return kernel


def normalize_kernel(other_ref, _, __, one_ref, two_ref, scaled_ref, sems):
    write_update(scaled_ref, other_ref, one_ref, two_ref, sems, 1, False)
    write_update(scaled_ref, other_ref, one_ref, two_ref, sems, 1, True)


VM = pl.BlockSpec(memory_space=pltpu.VMEM)
SM = pl.BlockSpec(memory_space=pltpu.SMEM)
HB = pl.BlockSpec(memory_space=pltpu.HBM)
PARAMS = pltpu.CompilerParams(vmem_limit_bytes=VMEM_LIMIT)


def body(snapshot, cotangent, first_weight, second_weight, face_codes):
    count, channels, cells = snapshot.shape[1:]
    vertical = cells // R_CELLS
    size = lax.axis_size(AXIS)
    x, g = snapshot[0], cotangent[0]
    def call(kernel, outs, operands, name, scratch=(), specs=None, out_specs=None, aliases=None):
        return pl.pallas_call(
            kernel, out_shape=outs, in_specs=specs or [VM] * len(operands),
            out_specs=out_specs or jax.tree.map(lambda _: VM, outs), input_output_aliases=aliases or {},
            scratch_shapes=list(scratch), compiler_params=PARAMS, name=name,
        )(*operands)

    span = 9 * channels
    shape = jax.ShapeDtypeStruct
    sizes = (count, channels, cells, vertical)
    stack = shape((span, span), BF16)
    band = shape(((count + 2) * channels, count * channels), BF16)
    edges = shape((2, channels, cells), F32)
    columns = shape((count * span, cells), BF16)
    grads = shape((channels, 27 * channels), F32)
    weight = shape(first_weight.shape, BF16)
    pinned = [
        pltpu.with_memory_space_constraint(v, pltpu.HBM) for v in (face_codes, x, g, first_weight, second_weight)]
    up, codes, x, g, first_weight, second_weight = call(
        make_pack_kernel(count),
        (shape((4, channels, cells), BF16), shape((2, 8, 128), jnp.int32), shape(x.shape, BF16), shape(x.shape, BF16),
         weight, weight),
        pinned, "pack", [pltpu.SMEM((1, 2), jnp.int32), pltpu.SemaphoreType.DMA((5,))], [HB] * 5)
    up = lax.ppermute(up, AXIS, [(b, (b + 1) % size) for b in range(size)])

    sums = shape((2 * span, 4 * channels), F32)
    ws, band_one, band_two, pre_edge, grad_edge, xs, cs, ps, part_one, part_two = call(
        make_interior_kernel(*sizes),
        (stack, band, band, edges, edges, columns, columns, shape(((count - 2) * span, cells), BF16), sums, sums),
        (x, g, first_weight, second_weight), "interior", [pltpu.VMEM(((count + 2) * channels, cells), BF16)])
    two = shape((2 * channels, cells), BF16)
    send, pg_edge, h_edge, low, cf = call(
        make_edge_kernel(*sizes),
        (grads, shape((2, channels, cells), BF16), two, two, shape((2 * span, cells), BF16)),
        (up, x, ws, band_one, band_two, codes, pre_edge, grad_edge, xs, cs, part_one, part_two), "edge",
        [pltpu.VMEM((3 * span, cells), BF16), pltpu.VMEM((span, cells), BF16), pltpu.VMEM((2 * span, cells), BF16)])
    keep, ps_edge = call(
        make_keep_kernel(channels, cells, vertical), (grads, shape((2 * span, cells), BF16)),
        (x, codes, cs, part_one, part_two, pg_edge, h_edge, low, cf), "keep")

    def swap(value, bit):
        return lax.ppermute(value, AXIS, [(b, b ^ bit) for b in range(size)])

    total, pg_sent = lax.optimization_barrier((keep + swap(send, 1), pg_edge))
    down = lax.ppermute(pg_sent, AXIS, [(b, (b - 1) % size) for b in range(size)])
    most_done, rest = call(
        make_input_kernel(*sizes), (shape((count, channels, cells), F32), edges),
        (ps, ps_edge, g, ws), "input_grad",
        [pltpu.VMEM((count - 2, channels, cells), F32),
         pltpu.SemaphoreType.DMA((count - 2,))], out_specs=(HB, VM))
    bits = [1 << power for power in range(1, size.bit_length() - 1)]
    rounds = list(zip(bits, bits[1:2] + bits[:1] + bits[2:]))
    for index, choice in enumerate(rounds):
        total = total + lax.ppermute(total, AXIS, [(b, b ^ choice[b % 2]) for b in range(size)])
        if index == len(rounds) - 2:
            total, most_done, rest = lax.optimization_barrier((total, most_done, rest))
        if index == len(rounds) - 1:
            total, down = lax.optimization_barrier((total, down))
    other = swap(total, 1)
    input_grad, first, second = call(
        make_upper_kernel(*sizes), (shape((count, channels, cells), F32), grads, grads),
        (down, codes, ws, rest, total, most_done), "upper_planes",
        [pltpu.VMEM((2 * span, cells), BF16), pltpu.VMEM((2, channels, cells), F32), pltpu.VMEM(grads.shape, F32),
         pltpu.SemaphoreType.DMA, pltpu.SemaphoreType.DMA((2,))],
        [VM, VM, VM, VM, VM, HB], out_specs=(HB, HB, HB), aliases={5: 0})
    first, second = call(
        normalize_kernel, (grads, grads), (other, first, second), "normalize",
        [pltpu.VMEM(grads.shape, F32), pltpu.SemaphoreType.DMA((2,))], [VM, HB, HB], out_specs=(HB, HB), aliases={1: 0, 2: 1})
    return (input_grad[None], first, second)


def solution(mesh):
    return jax.shard_map(
        body,
        mesh=mesh,
        in_specs=(
            P("groups", "blocks", None, None),
            P("groups", "blocks", None, None),
            P(),
            P(),
            P(("groups", "blocks"), None),
        ),
        out_specs=(P("groups", "blocks", None, None), P("groups", None), P("groups", None)),
        check_vma=False,
    )
```

```python
import jax
import jax.numpy as jnp
from jax import lax
from jax.experimental import pallas as pl
from jax.experimental.pallas import tpu as pltpu
from jax.sharding import PartitionSpec as P

R_CELLS = 32
AXIS = "blocks"
F32 = jnp.float32
BF16 = jnp.bfloat16
ORDER = (0, 1, 2, 3, 5, 6, 7, 8, 4)
VMEM_LIMIT = 24 * 1024 * 1024


def tap_masks(cells, vertical):
    lane = lax.broadcasted_iota(jnp.int32, (1, cells), 1)
    z = lane % vertical
    r = lane // vertical
    radial = cells // vertical
    masks = []
    for step_r in range(3):
        for step_z in range(3):
            ok = None
            if step_r == 0:
                ok = r >= 1
            if step_r == 2:
                ok = r < radial - 1
            if step_z == 0:
                ok = (z >= 1) if ok is None else ok & (z >= 1)
            if step_z == 2:
                ok = (z < vertical - 1) if ok is None else ok & (z < vertical - 1)
            masks.append(ok)
    return masks


def im2col(plane, store, masks, vertical):
    cells = plane.shape[1]
    wide = plane.astype(F32)
    for place, tap in enumerate(ORDER):
        offset = (tap // 3 - 1) * vertical + (tap % 3 - 1)
        if offset == 0:
            store(place, plane)
            continue
        moved = pltpu.roll(wide, (-offset) % cells, 1)
        moved = jnp.where(masks[tap], moved, 0.0)
        store(place, moved.astype(BF16))


def dot(a, b):
    return jnp.dot(a, b, preferred_element_type=F32)


def dot_nt(a, b):
    return lax.dot_general(a, b, (((1,), (1,)), ((), ())), preferred_element_type=F32)


def flip_planes(planes, code, vertical):
    lanes = 128
    parts = planes.shape[1] // lanes
    wide = planes.astype(F32)
    turn_r = code % 2 == 1
    bits = jnp.where(turn_r, lanes - vertical, 0) + jnp.where(code // 2 == 1, vertical - 1, 0)
    index = lax.broadcasted_iota(jnp.int32, (planes.shape[0], lanes), 1) ^ bits
    moved = [jnp.take_along_axis(wide[:, j * lanes:(j + 1) * lanes], index, axis=1) for j in range(parts)]
    return jnp.concatenate(
        [jnp.where(turn_r, moved[parts - 1 - j], moved[j]) for j in range(parts)], axis=1).astype(BF16)


def flipped_places(code):
    flip_r, flip_z = code % 2, code // 2
    places = []
    for tap in ORDER:
        r, z = tap // 3, tap % 3
        moved = 3 * (r + (2 - 2 * r) * flip_r) + z + (2 - 2 * z) * flip_z
        places.append(8 if tap == 4 else moved - (moved > 4).astype(jnp.int32))
    return places


def activation(pre, grad):
    sig = jax.nn.sigmoid(pre)
    hidden = (pre * sig).astype(BF16)
    return hidden, (grad * sig * (1.0 + pre * (1.0 - sig))).astype(BF16)


def filler(ref, channels, masks, vertical):
    def fill(position, plane, places=None, also=None):
        def store(place, value):
            if places is None:
                start = (9 * position + place) * channels
            else:
                start = pl.multiple_of((9 * position + places[place]) * channels, channels)
            ref[pl.ds(start, channels), :] = value
            if also is not None:
                also[place * channels:(place + 1) * channels, :] = value

        im2col(plane, store, masks, vertical)

    return fill


def make_pack_kernel(count):
    def kernel(codes_ref, x_ref, g_ref, w1_ref, w2_ref, up_ref, codes_out, x_out, g_out, w1_out, w2_out, scalars, sems):
        moves = ((x_ref, x_out), (g_ref, g_out), (codes_ref, scalars), (w1_ref, w1_out), (w2_ref, w2_out))
        copies = [pltpu.make_async_copy(*move, sems.at[index]) for index, move in enumerate(moves)]
        for copy in copies:
            copy.start()
        for index, field in enumerate((x_out, g_out)):
            copies[index].wait()
            up_ref[2 * index:2 * index + 2, :, :] = field[count - 2:count]
        for copy in copies[2:]:
            copy.wait()
        for side in range(2):
            codes_out[side, :, :] = jnp.full((8, 128), scalars[0, side], jnp.int32)

    return kernel


def make_interior_kernel(count, channels, cells, vertical):
    span = 9 * channels
    most = 8 * channels
    wide = 3 * channels
    last = count - 1

    def kernel(x_ref, g_ref, w1_ref, w2_ref,
               ws_ref, t1_ref, t2_ref, pe_ref, ge_ref, xs_ref, cs_ref, ps_ref, g1_ref, g2_ref, h_ref):
        masks = tap_masks(cells, vertical)
        for step in range(3):
            rows = slice(step * channels, (step + 1) * channels)
            base = step * span
            half = 4 * channels
            ws_ref[rows, 0:half] = w1_ref[:, base:base + half]
            ws_ref[rows, half:most] = w1_ref[:, base + half + channels:base + span]
            ws_ref[rows, most:span] = w1_ref[:, base + half:base + half + channels]
        for weight_ref, base in ((w2_ref, wide), (w1_ref, 2 * wide)):
            turned = weight_ref[...].astype(F32).T
            for step in range(3):
                for place, tap in enumerate(ORDER):
                    at = (9 * (2 - step) + 8 - tap) * channels
                    ws_ref[base + step * channels:base + (step + 1) * channels,
                           place * channels:(place + 1) * channels] = turned[at:at + channels, :].astype(BF16)
        for ref, base in ((t1_ref, 0), (t2_ref, wide)):
            ref[...] = jnp.zeros_like(ref)
            for step in range(3):
                centre = ws_ref[base + step * channels:base + (step + 1) * channels, most:span]
                for a in range(count):
                    row = (a + 2 - step) * channels
                    ref[row:row + channels, a * channels:(a + 1) * channels] = centre

        fill_x = filler(xs_ref, channels, masks, vertical)
        fill_g = filler(cs_ref, channels, masks, vertical)
        fill_p = filler(ps_ref, channels, masks, vertical)
        for a in range(count):
            fill_x(a, x_ref[a])
            fill_g(a, g_ref[a])

        h_ref[...] = jnp.zeros_like(h_ref)
        pre_all = dot(t1_ref[...], x_ref[...].reshape(count * channels, cells))
        grad_all = dot(t2_ref[...], g_ref[...].reshape(count * channels, cells))
        pre = {a: pre_all[(a + 1) * channels:(a + 2) * channels] for a in range(-1, last)}
        grad = {a: grad_all[(a + 1) * channels:(a + 2) * channels] for a in range(-1, last)}

        for a in range(count):
            columns = slice(a * span, a * span + most)
            first = max(0, a + 2 - last) * channels
            y = dot(ws_ref[first:wide, 0:most], xs_ref[columns, :])
            v = dot(ws_ref[wide + first:2 * wide, 0:most], cs_ref[columns, :])
            for step in range(3):
                target = a + 1 - step
                rows = slice(step * channels - first, (step + 1) * channels - first)
                if -1 <= target < last:
                    grad[target] = grad[target] + v[rows]
                if 0 <= target < last:
                    pre[target] = pre[target] + y[rows]
            done = a - 1
            if 1 <= done <= last - 1:
                hidden, pg = activation(pre.pop(done), grad.pop(done))
                h_ref[(done + 1) * channels:(done + 2) * channels, :] = hidden
                fill_p(done - 1, pg)
            if a == 1:
                for index, plane in ((0, -1), (1, 0)):
                    pe_ref[index, :, :] = pre.pop(plane)
                    ge_ref[index, :, :] = grad.pop(plane)
        grad_one, grad_two = None, None
        for a in range(0, count, 2):
            term = dot_nt(cs_ref[a * span:(a + 2) * span, :], h_ref[a * channels:(a + 4) * channels, :])
            grad_two = term if grad_two is None else grad_two + term
        for a in range(1, last, 2):
            term = dot_nt(ps_ref[(a - 1) * span:(a + 1) * span, :], x_ref[a - 1:a + 3].reshape(4 * channels, cells))
            grad_one = term if grad_one is None else grad_one + term
        g1_ref[...] = grad_one
        g2_ref[...] = grad_two

    return kernel


def put_blocks(ref, pairs, channels):
    span = 9 * channels
    total = pairs[0:span] + pltpu.roll(pairs[span:], 3 * channels, 1)
    moved = {}
    for place, tap in enumerate(ORDER):
        block = total[place * channels:(place + 1) * channels]
        shift = ((8 - tap) * channels) % (4 * channels)
        moved[8 - tap] = pltpu.roll(block, shift, 1) if shift else block
    lane = lax.broadcasted_iota(jnp.int32, (channels, 4 * channels), 1) // channels
    for first in range(0, 27, 4):
        tile = moved[first % 9]
        for n in range(first + 1, min(first + 4, 27)):
            tile = jnp.where(lane >= n - first, moved[n % 9], tile)
        width = min(4, 27 - first) * channels
        ref[:, first * channels:first * channels + width] = tile[:, :width]


def first_terms(sum_ref, ps_ref, low_ref, x_ref, channels):
    near = jnp.concatenate((low_ref[...], x_ref[0:2].reshape(low_ref.shape)), axis=0)
    return sum_ref[...] + dot_nt(ps_ref[...], near)


def second_terms(sum_ref, cf_ref, cs_ref, hidden, channels):
    zero = jnp.zeros_like(hidden)
    return (sum_ref[...] + dot_nt(cf_ref[...], jnp.concatenate((zero, hidden), axis=0))
            + dot_nt(cs_ref[0:18 * channels, :], jnp.concatenate((hidden, zero), axis=0)))


def make_keep_kernel(channels, cells, vertical):
    def kernel(x_ref, codes_ref, cs_ref, g1_ref, g2_ref, pg_ref, h_ref, low_ref, cf_ref, keep_ref, ps_ref):
        is_odd = lax.axis_index(AXIS) % 2 == 1
        fill_p = filler(ps_ref, channels, tap_masks(cells, vertical), vertical)
        fill_p(0, pg_ref[0], flipped_places(codes_ref[0, 0, 0]))
        fill_p(1, pg_ref[1])

        @pl.when(jnp.logical_not(is_odd))
        def _():
            put_blocks(keep_ref, first_terms(g1_ref, ps_ref, low_ref, x_ref, channels), channels)

        @pl.when(is_odd)
        def _():
            put_blocks(keep_ref, second_terms(g2_ref, cf_ref, cs_ref, h_ref[...], channels), channels)

    return kernel


def make_edge_kernel(count, channels, cells, vertical):
    span = 9 * channels
    most = 8 * channels
    wide = 3 * channels

    def kernel(up_ref, x_ref, ws_ref, t1_ref, t2_ref, codes_ref, pe_ref, ge_ref, xs_ref, cs_ref, g1_ref, g2_ref,
               send_ref, pg_ref, h_ref, low_ref, cf_ref, xf_ref, xo_ref, ps_ref):
        is_odd = lax.axis_index(AXIS) % 2 == 1
        masks = tap_masks(cells, vertical)
        places = flipped_places(codes_ref[0, 0, 0])
        fill_x = filler(xf_ref, channels, masks, vertical)
        fill_c = filler(cf_ref, channels, masks, vertical)
        planes = flip_planes(up_ref[...].reshape(4 * channels, cells), codes_ref[0, 0:1, 0:1], vertical)
        fill_x(0, planes[0:channels], places)
        fill_x(1, planes[channels:2 * channels], places, xo_ref)
        for place in range(9):
            start = 2 * span + places[place] * channels
            xf_ref[pl.ds(pl.multiple_of(start, channels), channels), :] = xs_ref[place * channels:(place + 1) * channels, :]
        fill_c(0, planes[2 * channels:3 * channels], places)
        fill_c(1, planes[3 * channels:], places)

        def eight(ref, index):
            return ref[index * span:index * span + most, :]

        def rows(part, first, end):
            return ws_ref[part * wide + first * channels:part * wide + end * channels, 0:most]

        centre = slice(2 * channels, 4 * channels), slice(0, 2 * channels)
        x_mid = dot(t1_ref[centre], planes[:2 * channels])
        g_mid = dot(t2_ref[centre], planes[2 * channels:])
        pre_m = (pe_ref[0] + x_mid[:channels] + dot(rows(0, 0, 1), eight(xf_ref, 0))
                 + dot(rows(0, 1, 2), eight(xf_ref, 1)) + dot(rows(0, 2, 3), eight(xf_ref, 2)))
        pre_0 = pe_ref[1] + x_mid[channels:] + dot(rows(0, 0, 1), eight(xo_ref, 0))
        near = dot(rows(1, 0, 2), eight(cf_ref, 1))
        grad_m = ge_ref[0] + g_mid[:channels] + near[channels:] + dot(rows(1, 0, 1), eight(cf_ref, 0))
        grad_0 = ge_ref[1] + g_mid[channels:] + near[:channels]
        hid_m, pg_m = activation(pre_m, grad_m)
        hid_0, pg_0 = activation(pre_0, grad_0)
        pg_ref[0, :, :] = pg_m
        pg_ref[1, :, :] = pg_0

        h_ref[0:channels, :] = hid_m
        h_ref[channels:, :] = hid_0
        low_ref[...] = planes[:2 * channels]

        @pl.when(jnp.logical_not(is_odd))
        def _():
            put_blocks(send_ref, second_terms(g2_ref, cf_ref, cs_ref, h_ref[...], channels), channels)

        @pl.when(is_odd)
        def _():
            fill_p = filler(ps_ref, channels, masks, vertical)
            fill_p(0, pg_m, places)
            fill_p(1, pg_0)
            put_blocks(send_ref, first_terms(g1_ref, ps_ref, low_ref, x_ref, channels), channels)

    return kernel


def make_input_kernel(count, channels, cells, vertical):
    span = 9 * channels
    wide = 3 * channels
    last = count - 1

    def kernel(inner_ref, edge_ref, g_ref, ws_ref, out_ref, rest_ref, done_ref, sems):
        weights = ws_ref[2 * wide:3 * wide, :]
        total = {}
        copies = []
        for a in range(-1, last):
            columns = edge_ref[(a + 1) * span:(a + 2) * span, :] if a <= 0 else inner_ref[(a - 1) * span:a * span, :]
            if a == -1:
                total[0] = dot(weights[0:channels], columns)
                continue
            y = dot(weights, columns)
            for step in range(3):
                target = a + 1 - step
                if 0 <= target < count:
                    part = y[step * channels:(step + 1) * channels]
                    total[target] = part if target not in total else total[target] + part
            if a >= 1:
                done_ref[a - 1, :, :] = g_ref[a - 1].astype(F32) + total.pop(a - 1)
                copies.append(pltpu.make_async_copy(done_ref.at[a - 1], out_ref.at[a - 1], sems.at[a - 1]))
                copies[-1].start()
        for index in range(2):
            a = last - 1 + index
            rest_ref[index, :, :] = g_ref[a].astype(F32) + total.pop(a)
        for copy in copies:
            copy.wait()

    return kernel


def write_update(scaled_ref, sum_ref, one_ref, two_ref, sems, swapped, finish):
    own = lax.axis_index(AXIS) % 2
    if not finish:
        v = sum_ref[...]
        scaled_ref[...] = v / jnp.sqrt(jnp.mean(v * v) + 1e-06)
    for index, target in enumerate((one_ref, two_ref)):

        @pl.when(own == (index ^ swapped))
        def _(index=index, target=target):
            copy = pltpu.make_async_copy(scaled_ref, target, sems.at[index])
            if finish:
                copy.wait()
            else:
                copy.start()


def make_upper_kernel(count, channels, cells, vertical):
    span = 9 * channels
    wide = 3 * channels
    last = count - 1

    def kernel(down_ref, codes_ref, ws_ref, rest_ref, mine_ref, _, out_ref, one_ref, two_ref,
               ps_ref, done_ref, scaled_ref, sem, sems):
        write_update(scaled_ref, mine_ref, one_ref, two_ref, sems, 0, False)
        fill = filler(ps_ref, channels, tap_masks(cells, vertical), vertical)
        planes = flip_planes(down_ref[...].reshape(2 * channels, cells), codes_ref[1, 0:1, 0:1], vertical)
        fill(0, planes[:channels])
        fill(1, planes[channels:], flipped_places(codes_ref[1, 0, 0]))
        weights = ws_ref[2 * wide + channels:3 * wide, :]
        y = dot(weights, ps_ref[0:span, :])
        done_ref[0, :, :] = rest_ref[0] + y[channels:]
        done_ref[1, :, :] = rest_ref[1] + y[:channels] + dot(weights[channels:], ps_ref[span:, :])
        copy = pltpu.make_async_copy(done_ref, out_ref.at[last - 1:count], sem)
        copy.start()
        write_update(scaled_ref, mine_ref, one_ref, two_ref, sems, 0, True)
        copy.wait()

    return kernel


def normalize_kernel(other_ref, _, __, one_ref, two_ref, scaled_ref, sems):
    write_update(scaled_ref, other_ref, one_ref, two_ref, sems, 1, False)
    write_update(scaled_ref, other_ref, one_ref, two_ref, sems, 1, True)


VM = pl.BlockSpec(memory_space=pltpu.VMEM)
SM = pl.BlockSpec(memory_space=pltpu.SMEM)
HB = pl.BlockSpec(memory_space=pltpu.HBM)
PARAMS = pltpu.CompilerParams(vmem_limit_bytes=VMEM_LIMIT)


def body(snapshot, cotangent, first_weight, second_weight, face_codes):
    count, channels, cells = snapshot.shape[1:]
    vertical = cells // R_CELLS
    size = lax.axis_size(AXIS)
    x, g = snapshot[0], cotangent[0]
    def call(kernel, outs, operands, name, scratch=(), specs=None, out_specs=None, aliases=None):
        return pl.pallas_call(
            kernel, out_shape=outs, in_specs=specs or [VM] * len(operands),
            out_specs=out_specs or jax.tree.map(lambda _: VM, outs), input_output_aliases=aliases or {},
            scratch_shapes=list(scratch), compiler_params=PARAMS, name=name,
        )(*operands)

    span = 9 * channels
    shape = jax.ShapeDtypeStruct
    sizes = (count, channels, cells, vertical)
    stack = shape((span, span), BF16)
    band = shape(((count + 2) * channels, count * channels), BF16)
    edges = shape((2, channels, cells), F32)
    columns = shape((count * span, cells), BF16)
    grads = shape((channels, 27 * channels), F32)
    weight = shape(first_weight.shape, BF16)
    pinned = [
        pltpu.with_memory_space_constraint(v, pltpu.HBM) for v in (face_codes, x, g, first_weight, second_weight)]
    up, codes, x, g, first_weight, second_weight = call(
        make_pack_kernel(count),
        (shape((4, channels, cells), BF16), shape((2, 8, 128), jnp.int32), shape(x.shape, BF16), shape(x.shape, BF16),
         weight, weight),
        pinned, "pack", [pltpu.SMEM((1, 2), jnp.int32), pltpu.SemaphoreType.DMA((5,))], [HB] * 5)
    up = lax.ppermute(up, AXIS, [(b, (b + 1) % size) for b in range(size)])

    sums = shape((2 * span, 4 * channels), F32)
    ws, band_one, band_two, pre_edge, grad_edge, xs, cs, ps, part_one, part_two = call(
        make_interior_kernel(*sizes),
        (stack, band, band, edges, edges, columns, columns, shape(((count - 2) * span, cells), BF16), sums, sums),
        (x, g, first_weight, second_weight), "interior", [pltpu.VMEM(((count + 2) * channels, cells), BF16)])
    two = shape((2 * channels, cells), BF16)
    send, pg_edge, h_edge, low, cf = call(
        make_edge_kernel(*sizes),
        (grads, shape((2, channels, cells), BF16), two, two, shape((2 * span, cells), BF16)),
        (up, x, ws, band_one, band_two, codes, pre_edge, grad_edge, xs, cs, part_one, part_two), "edge",
        [pltpu.VMEM((3 * span, cells), BF16), pltpu.VMEM((span, cells), BF16), pltpu.VMEM((2 * span, cells), BF16)])
    keep, ps_edge = call(
        make_keep_kernel(channels, cells, vertical), (grads, shape((2 * span, cells), BF16)),
        (x, codes, cs, part_one, part_two, pg_edge, h_edge, low, cf), "keep")

    def swap(value, bit):
        return lax.ppermute(value, AXIS, [(b, b ^ bit) for b in range(size)])

    total, pg_sent = lax.optimization_barrier((keep + swap(send, 1), pg_edge))
    down = lax.ppermute(pg_sent, AXIS, [(b, (b - 1) % size) for b in range(size)])
    most_done, rest = call(
        make_input_kernel(*sizes), (shape((count, channels, cells), F32), edges),
        (ps, ps_edge, g, ws), "input_grad",
        [pltpu.VMEM((count - 2, channels, cells), F32),
         pltpu.SemaphoreType.DMA((count - 2,))], out_specs=(HB, VM))
    bits = [1 << power for power in range(1, size.bit_length() - 1)]
    rounds = list(zip(bits[:1] + bits[-1:] + bits[1:-1], bits[-1:] + bits[:1] + bits[1:-1]))
    for index, choice in enumerate(rounds):
        total = total + lax.ppermute(total, AXIS, [(b, b ^ choice[b % 2]) for b in range(size)])
        if index == len(rounds) - 2:
            total, most_done, rest = lax.optimization_barrier((total, most_done, rest))
        if index == len(rounds) - 1:
            total, down = lax.optimization_barrier((total, down))
    other = swap(total, 1)
    input_grad, first, second = call(
        make_upper_kernel(*sizes), (shape((count, channels, cells), F32), grads, grads),
        (down, codes, ws, rest, total, most_done), "upper_planes",
        [pltpu.VMEM((2 * span, cells), BF16), pltpu.VMEM((2, channels, cells), F32), pltpu.VMEM(grads.shape, F32),
         pltpu.SemaphoreType.DMA, pltpu.SemaphoreType.DMA((2,))],
        [VM, VM, VM, VM, VM, HB], out_specs=(HB, HB, HB), aliases={5: 0})
    first, second = call(
        normalize_kernel, (grads, grads), (other, first, second), "normalize",
        [pltpu.VMEM(grads.shape, F32), pltpu.SemaphoreType.DMA((2,))], [VM, HB, HB], out_specs=(HB, HB), aliases={1: 0, 2: 1})
    return (input_grad[None], first, second)


def solution(mesh):
    return jax.shard_map(
        body,
        mesh=mesh,
        in_specs=(
            P("groups", "blocks", None, None),
            P("groups", "blocks", None, None),
            P(),
            P(),
            P(("groups", "blocks"), None),
        ),
        out_specs=(P("groups", "blocks", None, None), P("groups", None), P("groups", None)),
        check_vma=False,
    )
```
